512 devices in a mesh: layer: 128 (over y, z, core), inl: 4 (over x).
Axes of the slice: x: 4, y: 4, z: 16, core: 2. Of those that a mesh axis runs over, the one named last changes fastest.
Arguments:
- blocks: bfloat16 [512, 128, 128, 128], P('layer', 'inl'), may hold values from -6 to 6
- coords: int32 [512, 3], P('layer'), may hold values from 0 to 15
- filled: int32 [128], P('layer'), may hold values from 1 to 4, as said below
- factor_b: bfloat16 [16, 128, 256], P(None, 'inl'), may hold values from -0.022094727 to 0.044189453
- factor_c: bfloat16 [16, 128, 256], P(None, 'inl'), may hold values from -0.022094727 to 0.044189453
Outputs:
- factor_a: float32 [16, 128, 256], P(None, 'inl')
The draws below stay inside these ranges and needn't reach their ends.
Inputs may be any that keep to these rules, and one draw needn't show every extreme that they name: `filled`: some layer has all 4 slots live in every draw.
All inputs are finite; a program needn't handle non-finite values.
Results may differ from the reference program's by a relative error of at most 0.0031.
Values may be sent and summed in bfloat16 or wider, within the bound.
A program may use at most 64 MiB of HBM per device.

```python
import jax
import jax.numpy as jnp
from jax import lax

BS = 128
RANK = 256
NB_SIDE = 16
SLOTS = 4
LAYERS = 128
NBLK = 512


def draw_filled(key, part):
    key_counts, key_busiest = jax.random.split(key)
    counts = jax.random.randint(key_counts, (LAYERS,), 1, SLOTS + 1)
    busiest = jax.random.randint(key_busiest, (), 0, LAYERS)
    return counts.at[busiest].set(SLOTS).astype(jnp.int32)


def with_ends(result, stream_key, least, high):
    extent = result.shape
    index_at = [jax.random.randint(jax.random.fold_in(stream_key, axis), (), 0, extent[axis]) for axis in range(len(extent))]
    result = result.at[tuple(index_at)].set(least)
    longest = extent.index(max(extent))
    index_at[longest] = (index_at[longest] + 1) % extent[longest]
    return result.at[tuple(index_at)].set(high)


def block_scale(rng, dims, cuts, least, high):
    factor_of = 1.0
    for dim, parts in cuts:
        heights = jax.random.uniform(jax.random.fold_in(jax.random.fold_in(rng, 6), dim), (parts,), jnp.float32, least / len(cuts), high / len(cuts))
        factor_of = factor_of * jnp.repeat(jnp.exp(heights), dims[dim] // parts).reshape((-1,) + (1,) * (len(dims) - 1 - dim))
    return factor_of


def bell_draw(stream_key, dims, deviation, bound, shards=(), kind=jnp.bfloat16):
    drawn = deviation * jax.random.normal(stream_key, dims, jnp.float32)
    if shards:
        drawn = drawn * block_scale(stream_key, dims, shards, -0.22, 0.18)
    return jnp.clip(drawn, -bound, bound).astype(kind)


def setup_inputs(seed: int = 0) -> dict:
    key_of = jax.random.split(jax.random.key(seed), 6)
    return {
        "blocks": bell_draw(key_of[0], (NBLK, BS, BS, BS), 1.0, 6.0, ((0, 128), (1, 4))),
        "coords": with_ends(jax.random.randint(key_of[1], (NBLK, 3), 0, NB_SIDE), jax.random.fold_in(key_of[1], 1), 0, NB_SIDE - 1).astype(jnp.int32),
        "filled": draw_filled(jax.random.fold_in(key_of[5], 71), 0),
        "factor_b": jnp.clip(-0.022094727 + 0.06628418 * jax.random.uniform(key_of[3], (NB_SIDE, BS, RANK), jnp.float32) ** block_scale(key_of[3], (NB_SIDE, BS, RANK), ((1, 4),), -0.2, 0.2), -0.022094727, 0.044189453).astype(jnp.bfloat16),
        "factor_c": jnp.clip(-0.022094727 + 0.06628418 * jax.random.uniform(key_of[4], (NB_SIDE, BS, RANK), jnp.float32) ** block_scale(key_of[4], (NB_SIDE, BS, RANK), ((1, 4),), -0.2, 0.2), -0.022094727, 0.044189453).astype(jnp.bfloat16),
    }


def apply_inverse(lower, right_rows):
    forward = jax.scipy.linalg.solve_triangular(lower, right_rows.T, lower=True)
    return jax.scipy.linalg.solve_triangular(lower.T, forward, lower=False).T

def reference(blocks, coords, filled, factor_b, factor_c):
    slot_ids = jnp.arange(NBLK, dtype=jnp.int32)
    live_mask = (slot_ids % SLOTS < filled[slot_ids // SLOTS]).astype(jnp.float32)

    def one_block(buffer, items):
        block_data, coord_row, weight_live = items
        b_rows = factor_b[coord_row[1]]
        c_rows = factor_c[coord_row[2]]
        khatri = (b_rows[:, None, :] * c_rows[None, :, :]).reshape(BS * BS, RANK)
        slot_term = jnp.dot(block_data.reshape(BS, BS * BS).astype(jnp.float32), khatri.astype(jnp.float32), preferred_element_type=jnp.float32) * weight_live
        current = lax.dynamic_index_in_dim(buffer, coord_row[0], 0, keepdims=True)
        return (lax.dynamic_update_index_in_dim(buffer, current + slot_term[None], coord_row[0], 0), None)
    initial = jnp.zeros((NB_SIDE, BS, RANK), jnp.float32)
    buffer, unused = lax.scan(one_block, initial, (blocks, coords, live_mask))
    flat_b = factor_b.reshape(NB_SIDE * BS, RANK)
    flat_c = factor_c.reshape(NB_SIDE * BS, RANK)
    gram_b = jnp.dot(flat_b.T.astype(jnp.float32), flat_b.astype(jnp.float32), preferred_element_type=jnp.float32)
    gram_c = jnp.dot(flat_c.T.astype(jnp.float32), flat_c.astype(jnp.float32), preferred_element_type=jnp.float32)
    lower = jnp.linalg.cholesky(gram_b * gram_c)
    return apply_inverse(lower, buffer.reshape(NB_SIDE * BS, RANK)).reshape(NB_SIDE, BS, RANK)
```

```python
import functools

import jax
import jax.numpy as jnp
from jax import lax
from jax.experimental import pallas as pl
from jax.experimental.pallas import tpu as pltpu
from jax.sharding import PartitionSpec as P

INV_STEPS = 24
MESH = pl.DeviceIdType.MESH


def gram_inverse(gram):
    width = gram.shape[0]
    ident = jnp.eye(width, dtype=jnp.float32)
    start = ident / jnp.sqrt(jnp.sum(gram * gram))

    def refine(step_index, current):
        product = jnp.dot(gram, current, precision=lax.Precision.HIGHEST)
        return jnp.dot(current, 2.0 * ident - product, precision=lax.Precision.HIGHEST)

    return lax.fori_loop(0, INV_STEPS, refine, start)


def self_gram(factor_rows):
    return lax.dot_general(
        factor_rows, factor_rows, (((0,), (0,)), ((), ())), preferred_element_type=jnp.float32
    )


def contract_slot(block_slab, b_rows, c_rows):
    side_cells = b_rows.shape[0]
    rank_width = b_rows.shape[1]
    khatri = (b_rows[:, None, :] * c_rows[None, :, :]).reshape(side_cells * side_cells, rank_width)
    flat_slab = block_slab.reshape(block_slab.shape[0], side_cells * side_cells)
    return jnp.dot(flat_slab, khatri, preferred_element_type=jnp.float32)


def layer_allreduce_kernel(nbits, x_ref, o_ref, acc, gath, *rest):
    recv_bufs = rest[:nbits]
    send_sem, recv_sem = rest[nbits], rest[nbits + 1]
    me = lax.axis_index("layer")
    col = lax.axis_index("inl")

    def partner_of(k):
        bit = (me // (1 << k)) % 2
        return me + (1 - 2 * bit) * (1 << k), bit

    barrier = pltpu.get_barrier_semaphore()
    for k in range(nbits):
        partner, _ = partner_of(k)
        pl.semaphore_signal(barrier, inc=1, device_id=(partner, col), device_id_type=MESH)
    pl.semaphore_wait(barrier, nbits)

    acc[...] = x_ref[...]
    lo = 0
    size = acc.shape[0]
    spans = []
    for k in range(nbits):
        half = size // 2
        partner, bit = partner_of(k)
        keep_lo = lo + bit * half
        send_lo = lo + (1 - bit) * half
        copy = pltpu.make_async_remote_copy(
            src_ref=acc.at[pl.ds(send_lo, half)],
            dst_ref=recv_bufs[k],
            send_sem=send_sem.at[k],
            recv_sem=recv_sem.at[k],
            device_id=(partner, col),
            device_id_type=MESH,
        )
        copy.start()
        copy.wait()
        acc[pl.ds(keep_lo, half)] = acc[pl.ds(keep_lo, half)] + recv_bufs[k][...]
        spans.append((keep_lo, half))
        lo = keep_lo
        size = half

    gath[pl.ds(lo, size)] = acc[pl.ds(lo, size)]
    for k in reversed(range(nbits)):
        partner, _ = partner_of(k)
        keep_lo, half = spans[k]
        copy = pltpu.make_async_remote_copy(
            src_ref=gath.at[pl.ds(keep_lo, half)],
            dst_ref=gath.at[pl.ds(keep_lo, half)],
            send_sem=send_sem.at[nbits + k],
            recv_sem=recv_sem.at[nbits + k],
            device_id=(partner, col),
            device_id_type=MESH,
        )
        copy.start()
        copy.wait()

    o_ref[...] = gath[...]


def layer_allreduce(rows, layer_count):
    nbits = layer_count.bit_length() - 1
    total = rows.size
    pieces = rows.reshape(layer_count, total // (layer_count * 128), 128)
    recv_shapes = [
        pltpu.VMEM((layer_count >> (k + 1),) + pieces.shape[1:], jnp.float32) for k in range(nbits)
    ]
    summed = pl.pallas_call(
        functools.partial(layer_allreduce_kernel, nbits),
        out_shape=jax.ShapeDtypeStruct(pieces.shape, jnp.float32),
        in_specs=[pl.BlockSpec(memory_space=pltpu.VMEM)],
        out_specs=pl.BlockSpec(memory_space=pltpu.VMEM),
        scratch_shapes=[pltpu.VMEM(pieces.shape, jnp.float32)] * 2
        + recv_shapes
        + [pltpu.SemaphoreType.DMA((2 * nbits,)), pltpu.SemaphoreType.DMA((2 * nbits,))],
        compiler_params=pltpu.CompilerParams(collective_id=0, has_side_effects=True),
    )(pieces)
    return summed.reshape(rows.shape)


def on_device(layer_count, blocks, coords, filled, factor_b, factor_c):
    slot_count = blocks.shape[0]
    own_cells = blocks.shape[1]
    side_blocks = factor_b.shape[0]
    rank_width = factor_b.shape[2]
    whole_b, whole_c = (
        lax.all_gather(factor_b, "inl", axis=1, tiled=True),
        lax.all_gather(factor_c, "inl", axis=1, tiled=True),
    )
    local_b = factor_b.reshape(-1, rank_width)
    local_c = factor_c.reshape(-1, rank_width)
    gram_parts = lax.psum((self_gram(local_b), self_gram(local_c)), "inl")
    partials = []
    for slot_index in range(slot_count):
        b_rows = lax.dynamic_index_in_dim(whole_b, coords[slot_index, 1], 0, keepdims=False)
        c_rows = lax.dynamic_index_in_dim(whole_c, coords[slot_index, 2], 0, keepdims=False)
        partials.append(contract_slot(blocks[slot_index], b_rows, c_rows))
    stacked_parts = jnp.stack(partials)
    live_mask = (jnp.arange(slot_count, dtype=jnp.int32) < filled[0]).astype(jnp.float32)
    selector = (coords[:, 0][:, None] == jnp.arange(side_blocks, dtype=jnp.int32)[None, :]).astype(
        jnp.float32
    )
    selector = selector * live_mask[:, None]
    buffer = jnp.einsum("sn,sxr->nxr", selector, stacked_parts, precision=lax.Precision.HIGHEST)
    row_totals = buffer.reshape(side_blocks * own_cells, rank_width)
    inverse = gram_inverse(gram_parts[0] * gram_parts[1])
    summed_all = layer_allreduce(row_totals, layer_count)
    solved = jnp.dot(summed_all, inverse, precision=lax.Precision.HIGHEST)
    return solved.reshape(side_blocks, own_cells, rank_width)


def solution(mesh):
    in_specs = (
        P("layer", "inl", None, None),
        P("layer", None),
        P("layer"),
        P(None, "inl", None),
        P(None, "inl", None),
    )
    out_specs = P(None, "inl", None)
    return jax.shard_map(
        functools.partial(on_device, mesh.shape["layer"]),
        mesh=mesh,
        in_specs=in_specs,
        out_specs=out_specs,
        check_vma=False,
    )
```

```python
import functools

import jax
import jax.numpy as jnp
from jax import lax
from jax.experimental import pallas as pl
from jax.experimental.pallas import tpu as pltpu
from jax.sharding import PartitionSpec as P

INV_STEPS = 24
MESH = pl.DeviceIdType.MESH


def gram_inverse(gram):
    width = gram.shape[0]
    ident = jnp.eye(width, dtype=jnp.float32)
    start = ident / jnp.sqrt(jnp.sum(gram * gram))

    def refine(step_index, current):
        product = jnp.dot(gram, current, precision=lax.Precision.HIGHEST)
        return jnp.dot(current, 2.0 * ident - product, precision=lax.Precision.HIGHEST)

    return lax.fori_loop(0, INV_STEPS, refine, start)


def self_gram(factor_rows):
    return lax.dot_general(
        factor_rows, factor_rows, (((0,), (0,)), ((), ())), preferred_element_type=jnp.float32
    )


def contract_slot(block_slab, b_rows, c_rows):
    side_cells = b_rows.shape[0]
    rank_width = b_rows.shape[1]
    khatri = (b_rows[:, None, :] * c_rows[None, :, :]).reshape(side_cells * side_cells, rank_width)
    flat_slab = block_slab.reshape(block_slab.shape[0], side_cells * side_cells)
    return jnp.dot(flat_slab, khatri, preferred_element_type=jnp.float32)


def layer_allreduce_kernel(nbits, x_ref, o_ref, acc, gath, *rest):
    recv_bufs = rest[:nbits]
    send_sem, recv_sem = rest[nbits], rest[nbits + 1]
    me = lax.axis_index("layer")
    col = lax.axis_index("inl")

    def partner_of(k):
        bit = (me // (1 << k)) % 2
        return me + (1 - 2 * bit) * (1 << k), bit

    barrier = pltpu.get_barrier_semaphore()
    for k in range(nbits):
        partner, _ = partner_of(k)
        pl.semaphore_signal(barrier, inc=1, device_id=(partner, col), device_id_type=MESH)
    pl.semaphore_wait(barrier, nbits)

    acc[...] = x_ref[...]
    lo = 0
    size = acc.shape[0]
    spans = []
    for k in range(nbits):
        half = size // 2
        partner, bit = partner_of(k)
        keep_lo = lo + bit * half
        send_lo = lo + (1 - bit) * half
        copy = pltpu.make_async_remote_copy(
            src_ref=acc.at[pl.ds(send_lo, half)],
            dst_ref=recv_bufs[k],
            send_sem=send_sem.at[k],
            recv_sem=recv_sem.at[k],
            device_id=(partner, col),
            device_id_type=MESH,
        )
        copy.start()
        copy.wait()
        acc[pl.ds(keep_lo, half)] = acc[pl.ds(keep_lo, half)] + recv_bufs[k][...]
        spans.append((keep_lo, half))
        lo = keep_lo
        size = half

    gath[pl.ds(lo, size)] = acc[pl.ds(lo, size)]
    for k in reversed(range(nbits)):
        partner, _ = partner_of(k)
        keep_lo, half = spans[k]
        copy = pltpu.make_async_remote_copy(
            src_ref=gath.at[pl.ds(keep_lo, half)],
            dst_ref=gath.at[pl.ds(keep_lo, half)],
            send_sem=send_sem.at[nbits + k],
            recv_sem=recv_sem.at[nbits + k],
            device_id=(partner, col),
            device_id_type=MESH,
        )
        copy.start()
        copy.wait()

    o_ref[...] = gath[...]


def layer_allreduce(rows, layer_count):
    nbits = layer_count.bit_length() - 1
    total = rows.size
    pieces = rows.reshape(layer_count, total // (layer_count * 128), 128)
    recv_shapes = [
        pltpu.VMEM((layer_count >> (k + 1),) + pieces.shape[1:], jnp.float32) for k in range(nbits)
    ]
    summed = pl.pallas_call(
        functools.partial(layer_allreduce_kernel, nbits),
        out_shape=jax.ShapeDtypeStruct(pieces.shape, jnp.float32),
        in_specs=[pl.BlockSpec(memory_space=pltpu.VMEM)],
        out_specs=pl.BlockSpec(memory_space=pltpu.VMEM),
        scratch_shapes=[pltpu.VMEM(pieces.shape, jnp.float32)] * 2
        + recv_shapes
        + [pltpu.SemaphoreType.DMA((2 * nbits,)), pltpu.SemaphoreType.DMA((2 * nbits,))],
        compiler_params=pltpu.CompilerParams(collective_id=0, has_side_effects=True),
    )(pieces)
    return summed.reshape(rows.shape)


def inl_gather_kernel(ways, x_ref, o_ref, send_sem, recv_sem):
    row = lax.axis_index("layer")
    col = lax.axis_index("inl")
    barrier = pltpu.get_barrier_semaphore()
    for step in range(1, ways):
        pl.semaphore_signal(
            barrier, inc=1, device_id=(row, (col + step) % ways), device_id_type=MESH
        )
    pl.semaphore_wait(barrier, ways - 1)
    copies = []
    for step in range(1, ways):
        copy = pltpu.make_async_remote_copy(
            src_ref=x_ref,
            dst_ref=o_ref.at[col],
            send_sem=send_sem.at[step],
            recv_sem=recv_sem.at[col],
            device_id=(row, (col + step) % ways),
            device_id_type=MESH,
        )
        copy.start()
        copies.append(copy)
    o_ref[col] = x_ref[...]
    for copy in copies:
        copy.wait_send()
    for step in range(1, ways):
        source = (col + step) % ways
        pltpu.make_async_remote_copy(
            src_ref=x_ref,
            dst_ref=o_ref.at[source],
            send_sem=send_sem.at[0],
            recv_sem=recv_sem.at[source],
            device_id=(row, source),
            device_id_type=MESH,
        ).wait_recv()


def inl_gather(shards, ways):
    return pl.pallas_call(
        functools.partial(inl_gather_kernel, ways),
        out_shape=jax.ShapeDtypeStruct((ways,) + shards.shape, shards.dtype),
        in_specs=[pl.BlockSpec(memory_space=pltpu.VMEM)],
        out_specs=pl.BlockSpec(memory_space=pltpu.VMEM),
        scratch_shapes=[pltpu.SemaphoreType.DMA((ways,)), pltpu.SemaphoreType.DMA((ways,))],
        compiler_params=pltpu.CompilerParams(collective_id=1, has_side_effects=True),
    )(shards)


def on_device(layer_count, inl_count, blocks, coords, filled, factor_b, factor_c):
    slot_count = blocks.shape[0]
    own_cells = blocks.shape[1]
    side_blocks = factor_b.shape[0]
    rank_width = factor_b.shape[2]
    ways = inl_count
    gathered = inl_gather(jnp.stack([factor_b, factor_c]), ways)
    whole = jnp.transpose(gathered, (1, 2, 0, 3, 4)).reshape(
        2, side_blocks, ways * factor_b.shape[1], rank_width
    )
    whole_b, whole_c = whole[0], whole[1]
    gram_parts = (
        self_gram(whole_b.reshape(-1, rank_width)),
        self_gram(whole_c.reshape(-1, rank_width)),
    )
    partials = []
    for slot_index in range(slot_count):
        b_rows = lax.dynamic_index_in_dim(whole_b, coords[slot_index, 1], 0, keepdims=False)
        c_rows = lax.dynamic_index_in_dim(whole_c, coords[slot_index, 2], 0, keepdims=False)
        partials.append(contract_slot(blocks[slot_index], b_rows, c_rows))
    stacked_parts = jnp.stack(partials)
    live_mask = (jnp.arange(slot_count, dtype=jnp.int32) < filled[0]).astype(jnp.float32)
    selector = (coords[:, 0][:, None] == jnp.arange(side_blocks, dtype=jnp.int32)[None, :]).astype(
        jnp.float32
    )
    selector = selector * live_mask[:, None]
    buffer = jnp.einsum("sn,sxr->nxr", selector, stacked_parts, precision=lax.Precision.HIGHEST)
    row_totals = buffer.reshape(side_blocks * own_cells, rank_width)
    inverse = gram_inverse(gram_parts[0] * gram_parts[1])
    summed_all = layer_allreduce(row_totals, layer_count)
    solved = jnp.dot(summed_all, inverse, precision=lax.Precision.HIGHEST)
    return solved.reshape(side_blocks, own_cells, rank_width)


def solution(mesh):
    in_specs = (
        P("layer", "inl", None, None),
        P("layer", None),
        P("layer"),
        P(None, "inl", None),
        P(None, "inl", None),
    )
    out_specs = P(None, "inl", None)
    return jax.shard_map(
        functools.partial(on_device, mesh.shape["layer"], mesh.shape["inl"]),
        mesh=mesh,
        in_specs=in_specs,
        out_specs=out_specs,
        check_vma=False,
    )
```

```python
import functools

import jax
import jax.numpy as jnp
from jax import lax
from jax.experimental import pallas as pl
from jax.experimental.pallas import tpu as pltpu
from jax.sharding import PartitionSpec as P

INV_STEPS = 24
MESH = pl.DeviceIdType.MESH


def gram_inverse(gram):
    width = gram.shape[0]
    ident = jnp.eye(width, dtype=jnp.float32)
    start = ident / jnp.sqrt(jnp.sum(gram * gram))

    def refine(step_index, current):
        product = jnp.dot(gram, current, precision=lax.Precision.HIGHEST)
        return jnp.dot(current, 2.0 * ident - product, precision=lax.Precision.HIGHEST)

    return lax.fori_loop(0, INV_STEPS, refine, start)


def self_gram(factor_rows):
    return lax.dot_general(
        factor_rows, factor_rows, (((0,), (0,)), ((), ())), preferred_element_type=jnp.float32
    )


def contract_slot(block_slab, b_rows, c_rows):
    side_cells = b_rows.shape[0]
    rank_width = b_rows.shape[1]
    khatri = (b_rows[:, None, :] * c_rows[None, :, :]).reshape(side_cells * side_cells, rank_width)
    flat_slab = block_slab.reshape(block_slab.shape[0], side_cells * side_cells)
    return jnp.dot(flat_slab, khatri, preferred_element_type=jnp.float32)


def layer_allreduce_kernel(nbits, x_ref, o_ref, acc, gath, *rest):
    recv_bufs = rest[:nbits]
    send_sem, recv_sem = rest[nbits], rest[nbits + 1]
    me = lax.axis_index("layer")
    col = lax.axis_index("inl")

    def partner_of(k):
        bit = (me // (1 << k)) % 2
        return me + (1 - 2 * bit) * (1 << k), bit

    barrier = pltpu.get_barrier_semaphore()
    for k in range(nbits):
        partner, _ = partner_of(k)
        pl.semaphore_signal(barrier, inc=1, device_id=(partner, col), device_id_type=MESH)
    pl.semaphore_wait(barrier, nbits)

    acc[...] = x_ref[...]
    lo = 0
    size = acc.shape[0]
    spans = []
    for k in range(nbits):
        half = size // 2
        partner, bit = partner_of(k)
        keep_lo = lo + bit * half
        send_lo = lo + (1 - bit) * half
        copy = pltpu.make_async_remote_copy(
            src_ref=acc.at[pl.ds(send_lo, half)],
            dst_ref=recv_bufs[k],
            send_sem=send_sem.at[k],
            recv_sem=recv_sem.at[k],
            device_id=(partner, col),
            device_id_type=MESH,
        )
        copy.start()
        copy.wait()
        acc[pl.ds(keep_lo, half)] = acc[pl.ds(keep_lo, half)] + recv_bufs[k][...]
        spans.append((keep_lo, half))
        lo = keep_lo
        size = half

    gath[pl.ds(lo, size)] = acc[pl.ds(lo, size)]
    for k in reversed(range(nbits)):
        partner, _ = partner_of(k)
        keep_lo, half = spans[k]
        copy = pltpu.make_async_remote_copy(
            src_ref=gath.at[pl.ds(keep_lo, half)],
            dst_ref=gath.at[pl.ds(keep_lo, half)],
            send_sem=send_sem.at[nbits + k],
            recv_sem=recv_sem.at[nbits + k],
            device_id=(partner, col),
            device_id_type=MESH,
        )
        copy.start()
        copy.wait()

    o_ref[...] = gath[...]


def layer_allreduce(rows, layer_count):
    nbits = layer_count.bit_length() - 1
    total = rows.size
    pieces = rows.reshape(layer_count, total // (layer_count * 128), 128)
    recv_shapes = [
        pltpu.VMEM((layer_count >> (k + 1),) + pieces.shape[1:], jnp.float32) for k in range(nbits)
    ]
    summed = pl.pallas_call(
        functools.partial(layer_allreduce_kernel, nbits),
        out_shape=jax.ShapeDtypeStruct(pieces.shape, jnp.float32),
        in_specs=[pl.BlockSpec(memory_space=pltpu.VMEM)],
        out_specs=pl.BlockSpec(memory_space=pltpu.VMEM),
        scratch_shapes=[pltpu.VMEM(pieces.shape, jnp.float32)] * 2
        + recv_shapes
        + [pltpu.SemaphoreType.DMA((2 * nbits,)), pltpu.SemaphoreType.DMA((2 * nbits,))],
        compiler_params=pltpu.CompilerParams(collective_id=0, has_side_effects=True),
    )(pieces)
    return summed.reshape(rows.shape)


def inl_gather_kernel(ways, x_ref, o_ref, send_sem, recv_sem):
    row = lax.axis_index("layer")
    col = lax.axis_index("inl")
    barrier = pltpu.get_barrier_semaphore()
    for step in range(1, ways):
        pl.semaphore_signal(
            barrier, inc=1, device_id=(row, (col + step) % ways), device_id_type=MESH
        )
    pl.semaphore_wait(barrier, ways - 1)
    copies = []
    for step in range(1, ways):
        copy = pltpu.make_async_remote_copy(
            src_ref=x_ref,
            dst_ref=o_ref.at[col],
            send_sem=send_sem.at[step],
            recv_sem=recv_sem.at[col],
            device_id=(row, (col + step) % ways),
            device_id_type=MESH,
        )
        copy.start()
        copies.append(copy)
    o_ref[col] = x_ref[...]
    for copy in copies:
        copy.wait_send()
    for step in range(1, ways):
        source = (col + step) % ways
        pltpu.make_async_remote_copy(
            src_ref=x_ref,
            dst_ref=o_ref.at[source],
            send_sem=send_sem.at[0],
            recv_sem=recv_sem.at[source],
            device_id=(row, source),
            device_id_type=MESH,
        ).wait_recv()


def inl_gather(shards, ways):
    return pl.pallas_call(
        functools.partial(inl_gather_kernel, ways),
        out_shape=jax.ShapeDtypeStruct((ways,) + shards.shape, shards.dtype),
        in_specs=[pl.BlockSpec(memory_space=pltpu.VMEM)],
        out_specs=pl.BlockSpec(memory_space=pltpu.VMEM),
        scratch_shapes=[pltpu.SemaphoreType.DMA((ways,)), pltpu.SemaphoreType.DMA((ways,))],
        compiler_params=pltpu.CompilerParams(collective_id=1, has_side_effects=True),
    )(shards)


def mttkrp_kernel(coords_ref, blk_ref, b_ref, c_ref, o_ref):
    chunk = 8
    _, a_n, b_n, c_n = blk_ref.shape
    b_rows = b_ref[0].astype(jnp.float32)
    c_rows = c_ref[0]

    def body(i, carry):
        start = pl.multiple_of(i * chunk, chunk)
        x = blk_ref[0, pl.ds(start, chunk)].reshape(chunk * b_n, c_n)
        y = jnp.dot(x, c_rows, preferred_element_type=jnp.float32)
        z = y.reshape(chunk, b_n, -1) * b_rows[None]
        z = z.reshape(chunk, b_n // 8, 8, z.shape[-1]).sum(axis=1)
        o_ref[0, pl.ds(start, chunk)] = z.sum(axis=1)
        return carry

    lax.fori_loop(0, a_n // chunk, body, 0)


def mttkrp_terms(blocks, coords, whole_b, whole_c):
    slot_count, a_n, b_n, c_n = blocks.shape
    rank_width = whole_b.shape[-1]
    grid_spec = pltpu.PrefetchScalarGridSpec(
        num_scalar_prefetch=1,
        grid=(slot_count,),
        in_specs=[
            pl.BlockSpec((1, a_n, b_n, c_n), lambda s, cr: (s, 0, 0, 0)),
            pl.BlockSpec((1, b_n, rank_width), lambda s, cr: (cr[s * 3 + 1], 0, 0)),
            pl.BlockSpec((1, c_n, rank_width), lambda s, cr: (cr[s * 3 + 2], 0, 0)),
        ],
        out_specs=pl.BlockSpec((1, a_n, rank_width), lambda s, cr: (s, 0, 0)),
    )
    return pl.pallas_call(
        mttkrp_kernel,
        grid_spec=grid_spec,
        out_shape=jax.ShapeDtypeStruct((slot_count, a_n, rank_width), jnp.float32),
        cost_estimate=pl.CostEstimate(
            flops=2 * slot_count * a_n * b_n * c_n * rank_width,
            bytes_accessed=blocks.size * 2 + slot_count * (b_n + c_n) * rank_width * 2,
            transcendentals=0,
        ),
    )(coords.reshape(-1), blocks, whole_b, whole_c)


def on_device(layer_count, inl_count, blocks, coords, filled, factor_b, factor_c):
    slot_count = blocks.shape[0]
    own_cells = blocks.shape[1]
    side_blocks = factor_b.shape[0]
    rank_width = factor_b.shape[2]
    ways = inl_count
    gathered = inl_gather(jnp.stack([factor_b, factor_c]), ways)
    whole = jnp.transpose(gathered, (1, 2, 0, 3, 4)).reshape(
        2, side_blocks, ways * factor_b.shape[1], rank_width
    )
    whole_b, whole_c = whole[0], whole[1]
    gram_parts = (
        self_gram(whole_b.reshape(-1, rank_width)),
        self_gram(whole_c.reshape(-1, rank_width)),
    )
    stacked_parts = mttkrp_terms(blocks, coords, whole_b, whole_c)
    live_mask = (jnp.arange(slot_count, dtype=jnp.int32) < filled[0]).astype(jnp.float32)
    selector = (coords[:, 0][:, None] == jnp.arange(side_blocks, dtype=jnp.int32)[None, :]).astype(
        jnp.float32
    )
    selector = selector * live_mask[:, None]
    buffer = jnp.einsum("sn,sxr->nxr", selector, stacked_parts, precision=lax.Precision.HIGHEST)
    row_totals = buffer.reshape(side_blocks * own_cells, rank_width)
    inverse = gram_inverse(gram_parts[0] * gram_parts[1])
    summed_all = layer_allreduce(row_totals, layer_count)
    solved = jnp.dot(summed_all, inverse, precision=lax.Precision.HIGHEST)
    return solved.reshape(side_blocks, own_cells, rank_width)


def solution(mesh):
    in_specs = (
        P("layer", "inl", None, None),
        P("layer", None),
        P("layer"),
        P(None, "inl", None),
        P(None, "inl", None),
    )
    out_specs = P(None, "inl", None)
    return jax.shard_map(
        functools.partial(on_device, mesh.shape["layer"], mesh.shape["inl"]),
        mesh=mesh,
        in_specs=in_specs,
        out_specs=out_specs,
        check_vma=False,
    )
```

```python
import functools

import jax
import jax.numpy as jnp
from jax import lax
from jax.experimental import pallas as pl
from jax.experimental.pallas import tpu as pltpu
from jax.sharding import PartitionSpec as P

INV_STEPS = 24
MESH = pl.DeviceIdType.MESH


def gram_inverse(gram):
    width = gram.shape[0]
    ident = jnp.eye(width, dtype=jnp.float32)
    start = ident / jnp.sqrt(jnp.sum(gram * gram))

    def refine(step_index, current):
        product = jnp.dot(gram, current, precision=lax.Precision.HIGHEST)
        return jnp.dot(current, 2.0 * ident - product, precision=lax.Precision.HIGHEST)

    return lax.fori_loop(0, INV_STEPS, refine, start)


def self_gram(factor_rows):
    return lax.dot_general(
        factor_rows, factor_rows, (((0,), (0,)), ((), ())), preferred_element_type=jnp.float32
    )


def contract_slot(block_slab, b_rows, c_rows):
    side_cells = b_rows.shape[0]
    rank_width = b_rows.shape[1]
    khatri = (b_rows[:, None, :] * c_rows[None, :, :]).reshape(side_cells * side_cells, rank_width)
    flat_slab = block_slab.reshape(block_slab.shape[0], side_cells * side_cells)
    return jnp.dot(flat_slab, khatri, preferred_element_type=jnp.float32)


def layer_allreduce_kernel(nbits, orders, ns_plan, x_ref, g_ref, x0_ref, o_ref, inv_ref, acc, gath, *rest):
    recv_bufs = rest[:nbits]
    send_sem, recv_sem = rest[nbits], rest[nbits + 1]
    me = lax.axis_index("layer")
    col = lax.axis_index("inl")
    core = me % 2

    barrier = pltpu.get_barrier_semaphore()
    for k in range(nbits):
        bit = (me // (1 << k)) % 2
        partner = me + (1 - 2 * bit) * (1 << k)
        pl.semaphore_signal(barrier, inc=1, device_id=(partner, col), device_id_type=MESH)
    pl.semaphore_wait(barrier, nbits)

    width = g_ref.shape[0]
    rows = lax.broadcasted_iota(jnp.int32, (width, width), 0)
    cols = lax.broadcasted_iota(jnp.int32, (width, width), 1)
    two_ident = jnp.where(rows == cols, 2.0, 0.0).astype(jnp.float32)
    inv_ref[...] = x0_ref[...]

    def ns_steps(count):
        for _ in range(count):
            current = inv_ref[...]
            product = jnp.dot(
                g_ref[...], current, precision=lax.Precision.HIGHEST,
                preferred_element_type=jnp.float32,
            )
            inv_ref[...] = jnp.dot(
                current, two_ident - product, precision=lax.Precision.HIGHEST,
                preferred_element_type=jnp.float32,
            )

    def partner_of(j):
        step = core * (1 << orders[1][j]) + (1 - core) * (1 << orders[0][j])
        bit = (me // step) % 2
        return me + (1 - 2 * bit) * step, bit

    acc[...] = x_ref[...]
    lo = 0
    size = acc.shape[0]
    spans = []
    for j in range(nbits):
        half = size // 2
        partner, bit = partner_of(j)
        keep_lo = lo + bit * half
        send_lo = lo + (1 - bit) * half
        copy = pltpu.make_async_remote_copy(
            src_ref=acc.at[pl.ds(send_lo, half)],
            dst_ref=recv_bufs[j],
            send_sem=send_sem.at[j],
            recv_sem=recv_sem.at[j],
            device_id=(partner, col),
            device_id_type=MESH,
        )
        copy.start()
        ns_steps(ns_plan[j])
        copy.wait()
        acc[pl.ds(keep_lo, half)] = acc[pl.ds(keep_lo, half)] + recv_bufs[j][...]
        spans.append((keep_lo, half))
        lo = keep_lo
        size = half

    gath[pl.ds(lo, size)] = acc[pl.ds(lo, size)]
    for j in reversed(range(nbits)):
        partner, _ = partner_of(j)
        keep_lo, half = spans[j]
        copy = pltpu.make_async_remote_copy(
            src_ref=gath.at[pl.ds(keep_lo, half)],
            dst_ref=gath.at[pl.ds(keep_lo, half)],
            send_sem=send_sem.at[nbits + j],
            recv_sem=recv_sem.at[nbits + j],
            device_id=(partner, col),
            device_id_type=MESH,
        )
        copy.start()
        ns_steps(ns_plan[2 * nbits - 1 - j])
        copy.wait()

    o_ref[...] = gath[...]


def layer_allreduce_solve(rows, gram, layer_count):
    nbits = layer_count.bit_length() - 1
    if nbits == 7:
        orders = ((0, 1, 5, 2, 6, 3, 4), (0, 5, 1, 6, 2, 3, 4))
    else:
        orders = (tuple(range(nbits)), tuple(range(nbits)))
    rounds = 2 * nbits
    ns_plan = [INV_STEPS // rounds + (1 if r < INV_STEPS % rounds else 0) for r in range(rounds)]
    total = rows.size
    pieces = rows.reshape(layer_count, total // (layer_count * 128), 128)
    width = gram.shape[0]
    start = jnp.eye(width, dtype=jnp.float32) / jnp.sqrt(jnp.sum(gram * gram))
    recv_shapes = [
        pltpu.VMEM((layer_count >> (k + 1),) + pieces.shape[1:], jnp.float32) for k in range(nbits)
    ]
    summed, inverse = pl.pallas_call(
        functools.partial(layer_allreduce_kernel, nbits, orders, ns_plan),
        out_shape=(
            jax.ShapeDtypeStruct(pieces.shape, jnp.float32),
            jax.ShapeDtypeStruct((width, width), jnp.float32),
        ),
        in_specs=[pl.BlockSpec(memory_space=pltpu.VMEM)] * 3,
        out_specs=(pl.BlockSpec(memory_space=pltpu.VMEM),) * 2,
        scratch_shapes=[pltpu.VMEM(pieces.shape, jnp.float32)] * 2
        + recv_shapes
        + [pltpu.SemaphoreType.DMA((2 * nbits,)), pltpu.SemaphoreType.DMA((2 * nbits,))],
        compiler_params=pltpu.CompilerParams(collective_id=0, has_side_effects=True),
    )(pieces, gram, start)
    return summed.reshape(rows.shape), inverse


def inl_gather_kernel(ways, x_ref, o_ref, send_sem, recv_sem):
    row = lax.axis_index("layer")
    col = lax.axis_index("inl")
    barrier = pltpu.get_barrier_semaphore()
    for step in range(1, ways):
        pl.semaphore_signal(
            barrier, inc=1, device_id=(row, (col + step) % ways), device_id_type=MESH
        )
    pl.semaphore_wait(barrier, ways - 1)
    copies = []
    for step in range(1, ways):
        copy = pltpu.make_async_remote_copy(
            src_ref=x_ref,
            dst_ref=o_ref.at[col],
            send_sem=send_sem.at[step],
            recv_sem=recv_sem.at[col],
            device_id=(row, (col + step) % ways),
            device_id_type=MESH,
        )
        copy.start()
        copies.append(copy)
    o_ref[col] = x_ref[...]
    for copy in copies:
        copy.wait_send()
    for step in range(1, ways):
        source = (col + step) % ways
        pltpu.make_async_remote_copy(
            src_ref=x_ref,
            dst_ref=o_ref.at[source],
            send_sem=send_sem.at[0],
            recv_sem=recv_sem.at[source],
            device_id=(row, source),
            device_id_type=MESH,
        ).wait_recv()


def inl_gather(shards, ways):
    return pl.pallas_call(
        functools.partial(inl_gather_kernel, ways),
        out_shape=jax.ShapeDtypeStruct((ways,) + shards.shape, shards.dtype),
        in_specs=[pl.BlockSpec(memory_space=pltpu.VMEM)],
        out_specs=pl.BlockSpec(memory_space=pltpu.VMEM),
        scratch_shapes=[pltpu.SemaphoreType.DMA((ways,)), pltpu.SemaphoreType.DMA((ways,))],
        compiler_params=pltpu.CompilerParams(collective_id=1, has_side_effects=True),
    )(shards)


def mttkrp_kernel(coords_ref, blk_ref, b_ref, c_ref, o_ref):
    chunk = 8
    _, a_n, b_n, c_n = blk_ref.shape
    b_rows = b_ref[0].astype(jnp.float32)
    c_rows = c_ref[0]

    def body(i, carry):
        start = pl.multiple_of(i * chunk, chunk)
        x = blk_ref[0, pl.ds(start, chunk)].reshape(chunk * b_n, c_n)
        y = jnp.dot(x, c_rows, preferred_element_type=jnp.float32)
        z = y.reshape(chunk, b_n, -1) * b_rows[None]
        z = z.reshape(chunk, b_n // 8, 8, z.shape[-1]).sum(axis=1)
        o_ref[0, pl.ds(start, chunk)] = z.sum(axis=1)
        return carry

    lax.fori_loop(0, a_n // chunk, body, 0)


def mttkrp_terms(blocks, coords, whole_b, whole_c):
    slot_count, a_n, b_n, c_n = blocks.shape
    rank_width = whole_b.shape[-1]
    grid_spec = pltpu.PrefetchScalarGridSpec(
        num_scalar_prefetch=1,
        grid=(slot_count,),
        in_specs=[
            pl.BlockSpec((1, a_n, b_n, c_n), lambda s, cr: (s, 0, 0, 0)),
            pl.BlockSpec((1, b_n, rank_width), lambda s, cr: (cr[s * 3 + 1], 0, 0)),
            pl.BlockSpec((1, c_n, rank_width), lambda s, cr: (cr[s * 3 + 2], 0, 0)),
        ],
        out_specs=pl.BlockSpec((1, a_n, rank_width), lambda s, cr: (s, 0, 0)),
    )
    return pl.pallas_call(
        mttkrp_kernel,
        grid_spec=grid_spec,
        out_shape=jax.ShapeDtypeStruct((slot_count, a_n, rank_width), jnp.float32),
        cost_estimate=pl.CostEstimate(
            flops=2 * slot_count * a_n * b_n * c_n * rank_width,
            bytes_accessed=blocks.size * 2 + slot_count * (b_n + c_n) * rank_width * 2,
            transcendentals=0,
        ),
    )(coords.reshape(-1), blocks, whole_b, whole_c)


def on_device(layer_count, inl_count, blocks, coords, filled, factor_b, factor_c):
    slot_count = blocks.shape[0]
    own_cells = blocks.shape[1]
    side_blocks = factor_b.shape[0]
    rank_width = factor_b.shape[2]
    ways = inl_count
    gathered = inl_gather(jnp.stack([factor_b, factor_c]), ways)
    whole = jnp.transpose(gathered, (1, 2, 0, 3, 4)).reshape(
        2, side_blocks, ways * factor_b.shape[1], rank_width
    )
    whole_b, whole_c = whole[0], whole[1]
    gram_parts = (
        self_gram(whole_b.reshape(-1, rank_width)),
        self_gram(whole_c.reshape(-1, rank_width)),
    )
    stacked_parts = mttkrp_terms(blocks, coords, whole_b, whole_c)
    live_mask = (jnp.arange(slot_count, dtype=jnp.int32) < filled[0]).astype(jnp.float32)
    selector = (coords[:, 0][:, None] == jnp.arange(side_blocks, dtype=jnp.int32)[None, :]).astype(
        jnp.float32
    )
    selector = selector * live_mask[:, None]
    buffer = jnp.einsum("sn,sxr->nxr", selector, stacked_parts, precision=lax.Precision.HIGHEST)
    row_totals = buffer.reshape(side_blocks * own_cells, rank_width)
    summed_all, inverse = layer_allreduce_solve(
        row_totals, gram_parts[0] * gram_parts[1], layer_count
    )
    solved = jnp.dot(summed_all, inverse, precision=lax.Precision.HIGHEST)
    return solved.reshape(side_blocks, own_cells, rank_width)


def solution(mesh):
    in_specs = (
        P("layer", "inl", None, None),
        P("layer", None),
        P("layer"),
        P(None, "inl", None),
        P(None, "inl", None),
    )
    out_specs = P(None, "inl", None)
    return jax.shard_map(
        functools.partial(on_device, mesh.shape["layer"], mesh.shape["inl"]),
        mesh=mesh,
        in_specs=in_specs,
        out_specs=out_specs,
        check_vma=False,
    )
```

```python
import functools

import jax
import jax.numpy as jnp
from jax import lax
from jax.experimental import pallas as pl
from jax.experimental.pallas import tpu as pltpu
from jax.sharding import PartitionSpec as P

INV_STEPS = 24
MESH = pl.DeviceIdType.MESH


def gram_inverse(gram):
    width = gram.shape[0]
    ident = jnp.eye(width, dtype=jnp.float32)
    start = ident / jnp.sqrt(jnp.sum(gram * gram))

    def refine(step_index, current):
        product = jnp.dot(gram, current, precision=lax.Precision.HIGHEST)
        return jnp.dot(current, 2.0 * ident - product, precision=lax.Precision.HIGHEST)

    return lax.fori_loop(0, INV_STEPS, refine, start)


def self_gram(factor_rows):
    return lax.dot_general(
        factor_rows, factor_rows, (((0,), (0,)), ((), ())), preferred_element_type=jnp.float32
    )


def contract_slot(block_slab, b_rows, c_rows):
    side_cells = b_rows.shape[0]
    rank_width = b_rows.shape[1]
    khatri = (b_rows[:, None, :] * c_rows[None, :, :]).reshape(side_cells * side_cells, rank_width)
    flat_slab = block_slab.reshape(block_slab.shape[0], side_cells * side_cells)
    return jnp.dot(flat_slab, khatri, preferred_element_type=jnp.float32)


def layer_allreduce_kernel(nbits, orders, far, ns_plan, x_ref, g_ref, x0_ref, o_ref, inv_ref, acc, gath, *rest):
    rounds = len(orders[0])
    recv_bufs = rest[:rounds]
    far_buf, send_sem, recv_sem, far_send, far_recv = rest[rounds:]
    me = lax.axis_index("layer")
    col = lax.axis_index("inl")
    core = me % 2
    far_ways = far_buf.shape[0]
    far_low = far[0] if far else 0
    far_me = (me // (1 << far_low)) % far_ways

    def far_partner(other):
        return me + (other - far_me) * (1 << far_low)

    barrier = pltpu.get_barrier_semaphore()
    near_bits = [k for k in range(nbits) if k not in far]
    for k in near_bits:
        bit = (me // (1 << k)) % 2
        partner = me + (1 - 2 * bit) * (1 << k)
        pl.semaphore_signal(barrier, inc=1, device_id=(partner, col), device_id_type=MESH)
    for m in range(1, far_ways):
        pl.semaphore_signal(
            barrier, inc=1, device_id=(far_partner((far_me + m) % far_ways), col),
            device_id_type=MESH,
        )
    pl.semaphore_wait(barrier, len(near_bits) + far_ways - 1)

    width = g_ref.shape[0]
    rows = lax.broadcasted_iota(jnp.int32, (width, width), 0)
    cols = lax.broadcasted_iota(jnp.int32, (width, width), 1)
    two_ident = jnp.where(rows == cols, 2.0, 0.0).astype(jnp.float32)
    inv_ref[...] = x0_ref[...]

    def ns_steps(count):
        for _ in range(count):
            current = inv_ref[...]
            product = jnp.dot(
                g_ref[...], current, precision=lax.Precision.HIGHEST,
                preferred_element_type=jnp.float32,
            )
            inv_ref[...] = jnp.dot(
                current, two_ident - product, precision=lax.Precision.HIGHEST,
                preferred_element_type=jnp.float32,
            )

    def partner_of(j):
        step = core * (1 << orders[1][j]) + (1 - core) * (1 << orders[0][j])
        bit = (me // step) % 2
        return me + (1 - 2 * bit) * step, bit

    acc[...] = x_ref[...]
    lo = 0
    size = acc.shape[0]
    spans = []
    plan = iter(ns_plan)
    for j in range(rounds):
        half = size // 2
        partner, bit = partner_of(j)
        keep_lo = lo + bit * half
        send_lo = lo + (1 - bit) * half
        copy = pltpu.make_async_remote_copy(
            src_ref=acc.at[pl.ds(send_lo, half)],
            dst_ref=recv_bufs[j],
            send_sem=send_sem.at[j],
            recv_sem=recv_sem.at[j],
            device_id=(partner, col),
            device_id_type=MESH,
        )
        copy.start()
        ns_steps(next(plan))
        copy.wait()
        acc[pl.ds(keep_lo, half)] = acc[pl.ds(keep_lo, half)] + recv_bufs[j][...]
        spans.append((keep_lo, half))
        lo = keep_lo
        size = half

    if far_ways > 1:
        far_buf[far_me] = acc[pl.ds(lo, size)]
        copies = []
        for m in range(1, far_ways):
            copy = pltpu.make_async_remote_copy(
                src_ref=acc.at[pl.ds(lo, size)],
                dst_ref=far_buf.at[far_me],
                send_sem=far_send.at[m],
                recv_sem=far_recv.at[far_me],
                device_id=(far_partner((far_me + m) % far_ways), col),
                device_id_type=MESH,
            )
            copy.start()
            copies.append(copy)
        ns_steps(next(plan))
        for copy in copies:
            copy.wait_send()
        for m in range(1, far_ways):
            source = (far_me + m) % far_ways
            pltpu.make_async_remote_copy(
                src_ref=acc.at[pl.ds(lo, size)],
                dst_ref=far_buf.at[source],
                send_sem=far_send.at[0],
                recv_sem=far_recv.at[source],
                device_id=(far_partner(source), col),
                device_id_type=MESH,
            ).wait_recv()
        total = far_buf[0]
        for index in range(1, far_ways):
            total = total + far_buf[index]
        gath[pl.ds(lo, size)] = total
    else:
        ns_steps(next(plan))
        gath[pl.ds(lo, size)] = acc[pl.ds(lo, size)]

    for j in reversed(range(rounds)):
        partner, _ = partner_of(j)
        keep_lo, half = spans[j]
        copy = pltpu.make_async_remote_copy(
            src_ref=gath.at[pl.ds(keep_lo, half)],
            dst_ref=gath.at[pl.ds(keep_lo, half)],
            send_sem=send_sem.at[rounds + j],
            recv_sem=recv_sem.at[rounds + j],
            device_id=(partner, col),
            device_id_type=MESH,
        )
        copy.start()
        ns_steps(next(plan))
        copy.wait()

    o_ref[...] = gath[...]


def layer_allreduce_solve(rows, gram, layer_count):
    nbits = layer_count.bit_length() - 1
    far = (3, 4) if nbits >= 5 else ()
    near = [k for k in range(nbits) if k not in far]
    if nbits == 7:
        orders = ((0, 1, 5, 2, 6), (0, 5, 1, 6, 2))
    else:
        orders = (tuple(near), tuple(near))
    rounds = len(near)
    far_ways = 1 << len(far)
    slots = 2 * rounds + 1
    ns_plan = [INV_STEPS // slots + (1 if r < INV_STEPS % slots else 0) for r in range(slots)]
    total = rows.size
    pieces = rows.reshape(layer_count, total // (layer_count * 128), 128)
    width = gram.shape[0]
    start = jnp.eye(width, dtype=jnp.float32) / jnp.sqrt(jnp.sum(gram * gram))
    recv_shapes = [
        pltpu.VMEM((layer_count >> (k + 1),) + pieces.shape[1:], jnp.float32) for k in range(rounds)
    ]
    segment = layer_count >> rounds
    summed, inverse = pl.pallas_call(
        functools.partial(layer_allreduce_kernel, nbits, orders, far, ns_plan),
        out_shape=(
            jax.ShapeDtypeStruct(pieces.shape, jnp.float32),
            jax.ShapeDtypeStruct((width, width), jnp.float32),
        ),
        in_specs=[pl.BlockSpec(memory_space=pltpu.VMEM)] * 3,
        out_specs=(pl.BlockSpec(memory_space=pltpu.VMEM),) * 2,
        scratch_shapes=[pltpu.VMEM(pieces.shape, jnp.float32)] * 2
        + recv_shapes
        + [
            pltpu.VMEM((far_ways, segment) + pieces.shape[1:], jnp.float32),
            pltpu.SemaphoreType.DMA((2 * rounds,)),
            pltpu.SemaphoreType.DMA((2 * rounds,)),
            pltpu.SemaphoreType.DMA((far_ways,)),
            pltpu.SemaphoreType.DMA((far_ways,)),
        ],
        compiler_params=pltpu.CompilerParams(collective_id=0, has_side_effects=True),
    )(pieces, gram, start)
    return summed.reshape(rows.shape), inverse


def inl_gather_kernel(ways, x_ref, o_ref, send_sem, recv_sem):
    row = lax.axis_index("layer")
    col = lax.axis_index("inl")
    barrier = pltpu.get_barrier_semaphore()
    for step in range(1, ways):
        pl.semaphore_signal(
            barrier, inc=1, device_id=(row, (col + step) % ways), device_id_type=MESH
        )
    pl.semaphore_wait(barrier, ways - 1)
    copies = []
    for step in range(1, ways):
        copy = pltpu.make_async_remote_copy(
            src_ref=x_ref,
            dst_ref=o_ref.at[col],
            send_sem=send_sem.at[step],
            recv_sem=recv_sem.at[col],
            device_id=(row, (col + step) % ways),
            device_id_type=MESH,
        )
        copy.start()
        copies.append(copy)
    o_ref[col] = x_ref[...]
    for copy in copies:
        copy.wait_send()
    for step in range(1, ways):
        source = (col + step) % ways
        pltpu.make_async_remote_copy(
            src_ref=x_ref,
            dst_ref=o_ref.at[source],
            send_sem=send_sem.at[0],
            recv_sem=recv_sem.at[source],
            device_id=(row, source),
            device_id_type=MESH,
        ).wait_recv()


def inl_gather(shards, ways):
    return pl.pallas_call(
        functools.partial(inl_gather_kernel, ways),
        out_shape=jax.ShapeDtypeStruct((ways,) + shards.shape, shards.dtype),
        in_specs=[pl.BlockSpec(memory_space=pltpu.VMEM)],
        out_specs=pl.BlockSpec(memory_space=pltpu.VMEM),
        scratch_shapes=[pltpu.SemaphoreType.DMA((ways,)), pltpu.SemaphoreType.DMA((ways,))],
        compiler_params=pltpu.CompilerParams(collective_id=1, has_side_effects=True),
    )(shards)


def mttkrp_kernel(coords_ref, blk_ref, b_ref, c_ref, o_ref):
    chunk = 8
    _, a_n, b_n, c_n = blk_ref.shape
    b_rows = b_ref[0].astype(jnp.float32)
    c_rows = c_ref[0]

    def body(i, carry):
        start = pl.multiple_of(i * chunk, chunk)
        x = blk_ref[0, pl.ds(start, chunk)].reshape(chunk * b_n, c_n)
        y = jnp.dot(x, c_rows, preferred_element_type=jnp.float32)
        z = y.reshape(chunk, b_n, -1) * b_rows[None]
        z = z.reshape(chunk, b_n // 8, 8, z.shape[-1]).sum(axis=1)
        o_ref[0, pl.ds(start, chunk)] = z.sum(axis=1)
        return carry

    lax.fori_loop(0, a_n // chunk, body, 0)


def mttkrp_terms(blocks, coords, whole_b, whole_c):
    slot_count, a_n, b_n, c_n = blocks.shape
    rank_width = whole_b.shape[-1]
    grid_spec = pltpu.PrefetchScalarGridSpec(
        num_scalar_prefetch=1,
        grid=(slot_count,),
        in_specs=[
            pl.BlockSpec((1, a_n, b_n, c_n), lambda s, cr: (s, 0, 0, 0)),
            pl.BlockSpec((1, b_n, rank_width), lambda s, cr: (cr[s * 3 + 1], 0, 0)),
            pl.BlockSpec((1, c_n, rank_width), lambda s, cr: (cr[s * 3 + 2], 0, 0)),
        ],
        out_specs=pl.BlockSpec((1, a_n, rank_width), lambda s, cr: (s, 0, 0)),
    )
    return pl.pallas_call(
        mttkrp_kernel,
        grid_spec=grid_spec,
        out_shape=jax.ShapeDtypeStruct((slot_count, a_n, rank_width), jnp.float32),
        cost_estimate=pl.CostEstimate(
            flops=2 * slot_count * a_n * b_n * c_n * rank_width,
            bytes_accessed=blocks.size * 2 + slot_count * (b_n + c_n) * rank_width * 2,
            transcendentals=0,
        ),
    )(coords.reshape(-1), blocks, whole_b, whole_c)


def on_device(layer_count, inl_count, blocks, coords, filled, factor_b, factor_c):
    slot_count = blocks.shape[0]
    own_cells = blocks.shape[1]
    side_blocks = factor_b.shape[0]
    rank_width = factor_b.shape[2]
    ways = inl_count
    gathered = inl_gather(jnp.stack([factor_b, factor_c]), ways)
    whole = jnp.transpose(gathered, (1, 2, 0, 3, 4)).reshape(
        2, side_blocks, ways * factor_b.shape[1], rank_width
    )
    whole_b, whole_c = whole[0], whole[1]
    gram_parts = (
        self_gram(whole_b.reshape(-1, rank_width)),
        self_gram(whole_c.reshape(-1, rank_width)),
    )
    stacked_parts = mttkrp_terms(blocks, coords, whole_b, whole_c)
    live_mask = (jnp.arange(slot_count, dtype=jnp.int32) < filled[0]).astype(jnp.float32)
    selector = (coords[:, 0][:, None] == jnp.arange(side_blocks, dtype=jnp.int32)[None, :]).astype(
        jnp.float32
    )
    selector = selector * live_mask[:, None]
    buffer = jnp.einsum("sn,sxr->nxr", selector, stacked_parts, precision=lax.Precision.HIGHEST)
    row_totals = buffer.reshape(side_blocks * own_cells, rank_width)
    summed_all, inverse = layer_allreduce_solve(
        row_totals, gram_parts[0] * gram_parts[1], layer_count
    )
    solved = jnp.dot(summed_all, inverse, precision=lax.Precision.HIGHEST)
    return solved.reshape(side_blocks, own_cells, rank_width)


def solution(mesh):
    in_specs = (
        P("layer", "inl", None, None),
        P("layer", None),
        P("layer"),
        P(None, "inl", None),
        P(None, "inl", None),
    )
    out_specs = P(None, "inl", None)
    return jax.shard_map(
        functools.partial(on_device, mesh.shape["layer"], mesh.shape["inl"]),
        mesh=mesh,
        in_specs=in_specs,
        out_specs=out_specs,
        check_vma=False,
    )
```

```python
import functools

import jax
import jax.numpy as jnp
from jax import lax
from jax.experimental import pallas as pl
from jax.experimental.pallas import tpu as pltpu
from jax.sharding import PartitionSpec as P

INV_STEPS = 24
MESH = pl.DeviceIdType.MESH


def gram_inverse(gram):
    width = gram.shape[0]
    ident = jnp.eye(width, dtype=jnp.float32)
    start = ident / jnp.sqrt(jnp.sum(gram * gram))

    def refine(step_index, current):
        product = jnp.dot(gram, current, precision=lax.Precision.HIGHEST)
        return jnp.dot(current, 2.0 * ident - product, precision=lax.Precision.HIGHEST)

    return lax.fori_loop(0, INV_STEPS, refine, start)


def self_gram(factor_rows):
    return lax.dot_general(
        factor_rows, factor_rows, (((0,), (0,)), ((), ())), preferred_element_type=jnp.float32
    )


def contract_slot(block_slab, b_rows, c_rows):
    side_cells = b_rows.shape[0]
    rank_width = b_rows.shape[1]
    khatri = (b_rows[:, None, :] * c_rows[None, :, :]).reshape(side_cells * side_cells, rank_width)
    flat_slab = block_slab.reshape(block_slab.shape[0], side_cells * side_cells)
    return jnp.dot(flat_slab, khatri, preferred_element_type=jnp.float32)


def layer_allreduce_kernel(nbits, orders, far, ns_plan, x_ref, g_ref, x0_ref, o_ref, inv_ref, acc, gath, *rest):
    rounds = len(orders[0])
    recv_bufs = rest[:rounds]
    far_buf, send_sem, recv_sem, far_send, far_recv = rest[rounds:]
    me = lax.axis_index("layer")
    col = lax.axis_index("inl")
    core = me % 2
    far_ways = far_buf.shape[0]
    far_low = far[0] if far else 0
    far_me = (me // (1 << far_low)) % far_ways

    def far_partner(other):
        return me + (other - far_me) * (1 << far_low)

    barrier = pltpu.get_barrier_semaphore()
    near_bits = [k for k in range(nbits) if k not in far]
    for k in near_bits:
        bit = (me // (1 << k)) % 2
        partner = me + (1 - 2 * bit) * (1 << k)
        pl.semaphore_signal(barrier, inc=1, device_id=(partner, col), device_id_type=MESH)
    for m in range(1, far_ways):
        pl.semaphore_signal(
            barrier, inc=1, device_id=(far_partner((far_me + m) % far_ways), col),
            device_id_type=MESH,
        )
    pl.semaphore_wait(barrier, len(near_bits) + far_ways - 1)

    width = g_ref.shape[0]
    rows = lax.broadcasted_iota(jnp.int32, (width, width), 0)
    cols = lax.broadcasted_iota(jnp.int32, (width, width), 1)
    two_ident = jnp.where(rows == cols, 2.0, 0.0).astype(jnp.float32)
    inv_ref[...] = x0_ref[...]

    def ns_steps(count):
        for _ in range(count):
            current = inv_ref[...]
            product = jnp.dot(
                g_ref[...], current, precision=lax.Precision.HIGHEST,
                preferred_element_type=jnp.float32,
            )
            inv_ref[...] = jnp.dot(
                current, two_ident - product, precision=lax.Precision.HIGHEST,
                preferred_element_type=jnp.float32,
            )

    def partner_of(j):
        step = core * (1 << orders[1][j]) + (1 - core) * (1 << orders[0][j])
        bit = (me // step) % 2
        return me + (1 - 2 * bit) * step, bit

    acc[...] = x_ref[...]
    lo = 0
    size = acc.shape[0]
    spans = []
    plan = iter(ns_plan)
    for j in range(rounds):
        half = size // 2
        partner, bit = partner_of(j)
        keep_lo = lo + bit * half
        send_lo = lo + (1 - bit) * half
        copy = pltpu.make_async_remote_copy(
            src_ref=acc.at[pl.ds(send_lo, half)],
            dst_ref=recv_bufs[j],
            send_sem=send_sem.at[j],
            recv_sem=recv_sem.at[j],
            device_id=(partner, col),
            device_id_type=MESH,
        )
        copy.start()
        ns_steps(next(plan))
        copy.wait()
        acc[pl.ds(keep_lo, half)] = acc[pl.ds(keep_lo, half)] + recv_bufs[j][...]
        spans.append((keep_lo, half))
        lo = keep_lo
        size = half

    if far_ways > 1:
        far_buf[far_me] = acc[pl.ds(lo, size)]
        copies = []
        for m in range(1, far_ways):
            copy = pltpu.make_async_remote_copy(
                src_ref=acc.at[pl.ds(lo, size)],
                dst_ref=far_buf.at[far_me],
                send_sem=far_send.at[m],
                recv_sem=far_recv.at[far_me],
                device_id=(far_partner((far_me + m) % far_ways), col),
                device_id_type=MESH,
            )
            copy.start()
            copies.append(copy)
        ns_steps(next(plan))
        for copy in copies:
            copy.wait_send()
        for m in range(1, far_ways):
            source = (far_me + m) % far_ways
            pltpu.make_async_remote_copy(
                src_ref=acc.at[pl.ds(lo, size)],
                dst_ref=far_buf.at[source],
                send_sem=far_send.at[0],
                recv_sem=far_recv.at[source],
                device_id=(far_partner(source), col),
                device_id_type=MESH,
            ).wait_recv()
        total = far_buf[0]
        for index in range(1, far_ways):
            total = total + far_buf[index]
        gath[pl.ds(lo, size)] = total
    else:
        ns_steps(next(plan))
        gath[pl.ds(lo, size)] = acc[pl.ds(lo, size)]

    for j in reversed(range(rounds)):
        partner, _ = partner_of(j)
        keep_lo, half = spans[j]
        copy = pltpu.make_async_remote_copy(
            src_ref=gath.at[pl.ds(keep_lo, half)],
            dst_ref=gath.at[pl.ds(keep_lo, half)],
            send_sem=send_sem.at[rounds + j],
            recv_sem=recv_sem.at[rounds + j],
            device_id=(partner, col),
            device_id_type=MESH,
        )
        copy.start()
        ns_steps(next(plan))
        copy.wait()

    o_ref[...] = gath[...]


def layer_allreduce_solve(rows, gram, layer_count):
    nbits = layer_count.bit_length() - 1
    far = (3, 4) if nbits >= 5 else ()
    near = [k for k in range(nbits) if k not in far]
    if nbits == 7:
        orders = ((0, 1, 5, 2, 6), (0, 5, 1, 6, 2))
    else:
        orders = (tuple(near), tuple(near))
    rounds = len(near)
    far_ways = 1 << len(far)
    slots = 2 * rounds + 1
    ns_plan = [INV_STEPS // slots + (1 if r < INV_STEPS % slots else 0) for r in range(slots)]
    total = rows.size
    pieces = rows.reshape(layer_count, total // (layer_count * 128), 128)
    width = gram.shape[0]
    start = jnp.eye(width, dtype=jnp.float32) / jnp.sqrt(jnp.sum(gram * gram))
    recv_shapes = [
        pltpu.VMEM((layer_count >> (k + 1),) + pieces.shape[1:], jnp.float32) for k in range(rounds)
    ]
    segment = layer_count >> rounds
    summed, inverse = pl.pallas_call(
        functools.partial(layer_allreduce_kernel, nbits, orders, far, ns_plan),
        out_shape=(
            jax.ShapeDtypeStruct(pieces.shape, jnp.float32),
            jax.ShapeDtypeStruct((width, width), jnp.float32),
        ),
        in_specs=[pl.BlockSpec(memory_space=pltpu.VMEM)] * 3,
        out_specs=(pl.BlockSpec(memory_space=pltpu.VMEM),) * 2,
        scratch_shapes=[pltpu.VMEM(pieces.shape, jnp.float32)] * 2
        + recv_shapes
        + [
            pltpu.VMEM((far_ways, segment) + pieces.shape[1:], jnp.float32),
            pltpu.SemaphoreType.DMA((2 * rounds,)),
            pltpu.SemaphoreType.DMA((2 * rounds,)),
            pltpu.SemaphoreType.DMA((far_ways,)),
            pltpu.SemaphoreType.DMA((far_ways,)),
        ],
        compiler_params=pltpu.CompilerParams(collective_id=0, has_side_effects=True),
    )(pieces, gram, start)
    return summed.reshape(rows.shape), inverse


def inl_gather_kernel(ways, x_ref, o_ref, send1, recv1, send2, recv2):
    row = lax.axis_index("layer")
    col = lax.axis_index("inl")
    core = row % 2
    sibling = row + 1 - 2 * core
    half = x_ref.shape[2] // 2
    mine = pl.ds(pl.multiple_of(core * half, half), half)
    theirs = pl.ds(pl.multiple_of((1 - core) * half, half), half)
    barrier = pltpu.get_barrier_semaphore()
    for step in range(1, ways):
        pl.semaphore_signal(
            barrier, inc=1, device_id=(row, (col + step) % ways), device_id_type=MESH
        )
    pl.semaphore_signal(barrier, inc=1, device_id=(sibling, col), device_id_type=MESH)
    pl.semaphore_wait(barrier, ways)
    copies = []
    for step in range(1, ways):
        copy = pltpu.make_async_remote_copy(
            src_ref=x_ref.at[:, :, mine],
            dst_ref=o_ref.at[:, :, col, mine],
            send_sem=send1.at[step],
            recv_sem=recv1.at[col],
            device_id=(row, (col + step) % ways),
            device_id_type=MESH,
        )
        copy.start()
        copies.append(copy)
    o_ref[:, :, col] = x_ref[...]
    forwards = []
    for step in range(1, ways):
        source = (col + step) % ways
        pltpu.make_async_remote_copy(
            src_ref=x_ref.at[:, :, mine],
            dst_ref=o_ref.at[:, :, source, mine],
            send_sem=send1.at[0],
            recv_sem=recv1.at[source],
            device_id=(row, source),
            device_id_type=MESH,
        ).wait_recv()
        forward = pltpu.make_async_remote_copy(
            src_ref=o_ref.at[:, :, source, mine],
            dst_ref=o_ref.at[:, :, source, mine],
            send_sem=send2.at[step],
            recv_sem=recv2.at[source],
            device_id=(sibling, col),
            device_id_type=MESH,
        )
        forward.start()
        forwards.append(forward)
    for copy in copies:
        copy.wait_send()
    for forward in forwards:
        forward.wait_send()
    for step in range(1, ways):
        source = (col + step) % ways
        pltpu.make_async_remote_copy(
            src_ref=o_ref.at[:, :, source, theirs],
            dst_ref=o_ref.at[:, :, source, theirs],
            send_sem=send2.at[0],
            recv_sem=recv2.at[source],
            device_id=(sibling, col),
            device_id_type=MESH,
        ).wait_recv()


def inl_gather(shards, ways):
    parts, blocks, cells, rank_width = shards.shape
    return pl.pallas_call(
        functools.partial(inl_gather_kernel, ways),
        out_shape=jax.ShapeDtypeStruct((parts, blocks, ways, cells, rank_width), shards.dtype),
        in_specs=[pl.BlockSpec(memory_space=pltpu.VMEM)],
        out_specs=pl.BlockSpec(memory_space=pltpu.VMEM),
        scratch_shapes=[pltpu.SemaphoreType.DMA((ways,))] * 4,
        compiler_params=pltpu.CompilerParams(collective_id=1, has_side_effects=True),
    )(shards)


def mttkrp_kernel(coords_ref, blk_ref, b_ref, c_ref, o_ref):
    chunk = 8
    _, a_n, b_n, c_n = blk_ref.shape
    b_rows = b_ref[0].astype(jnp.float32)
    c_rows = c_ref[0]

    def body(i, carry):
        start = pl.multiple_of(i * chunk, chunk)
        x = blk_ref[0, pl.ds(start, chunk)].reshape(chunk * b_n, c_n)
        y = jnp.dot(x, c_rows, preferred_element_type=jnp.float32)
        z = y.reshape(chunk, b_n, -1) * b_rows[None]
        z = z.reshape(chunk, b_n // 8, 8, z.shape[-1]).sum(axis=1)
        o_ref[0, pl.ds(start, chunk)] = z.sum(axis=1)
        return carry

    lax.fori_loop(0, a_n // chunk, body, 0)


def mttkrp_terms(blocks, coords, whole_b, whole_c):
    slot_count, a_n, b_n, c_n = blocks.shape
    rank_width = whole_b.shape[-1]
    grid_spec = pltpu.PrefetchScalarGridSpec(
        num_scalar_prefetch=1,
        grid=(slot_count,),
        in_specs=[
            pl.BlockSpec((1, a_n, b_n, c_n), lambda s, cr: (s, 0, 0, 0)),
            pl.BlockSpec((1, b_n, rank_width), lambda s, cr: (cr[s * 3 + 1], 0, 0)),
            pl.BlockSpec((1, c_n, rank_width), lambda s, cr: (cr[s * 3 + 2], 0, 0)),
        ],
        out_specs=pl.BlockSpec((1, a_n, rank_width), lambda s, cr: (s, 0, 0)),
    )
    return pl.pallas_call(
        mttkrp_kernel,
        grid_spec=grid_spec,
        out_shape=jax.ShapeDtypeStruct((slot_count, a_n, rank_width), jnp.float32),
        cost_estimate=pl.CostEstimate(
            flops=2 * slot_count * a_n * b_n * c_n * rank_width,
            bytes_accessed=blocks.size * 2 + slot_count * (b_n + c_n) * rank_width * 2,
            transcendentals=0,
        ),
    )(coords.reshape(-1), blocks, whole_b, whole_c)


def on_device(layer_count, inl_count, blocks, coords, filled, factor_b, factor_c):
    slot_count = blocks.shape[0]
    own_cells = blocks.shape[1]
    side_blocks = factor_b.shape[0]
    rank_width = factor_b.shape[2]
    ways = inl_count
    gathered = inl_gather(jnp.stack([factor_b, factor_c]), ways)
    whole = gathered.reshape(2, side_blocks, ways * factor_b.shape[1], rank_width)
    whole_b, whole_c = whole[0], whole[1]
    gram_parts = (
        self_gram(whole_b.reshape(-1, rank_width)),
        self_gram(whole_c.reshape(-1, rank_width)),
    )
    stacked_parts = mttkrp_terms(blocks, coords, whole_b, whole_c)
    live_mask = (jnp.arange(slot_count, dtype=jnp.int32) < filled[0]).astype(jnp.float32)
    selector = (coords[:, 0][:, None] == jnp.arange(side_blocks, dtype=jnp.int32)[None, :]).astype(
        jnp.float32
    )
    selector = selector * live_mask[:, None]
    buffer = jnp.einsum("sn,sxr->nxr", selector, stacked_parts, precision=lax.Precision.HIGHEST)
    row_totals = buffer.reshape(side_blocks * own_cells, rank_width)
    summed_all, inverse = layer_allreduce_solve(
        row_totals, gram_parts[0] * gram_parts[1], layer_count
    )
    solved = jnp.dot(summed_all, inverse, precision=lax.Precision.HIGHEST)
    return solved.reshape(side_blocks, own_cells, rank_width)


def solution(mesh):
    in_specs = (
        P("layer", "inl", None, None),
        P("layer", None),
        P("layer"),
        P(None, "inl", None),
        P(None, "inl", None),
    )
    out_specs = P(None, "inl", None)
    return jax.shard_map(
        functools.partial(on_device, mesh.shape["layer"], mesh.shape["inl"]),
        mesh=mesh,
        in_specs=in_specs,
        out_specs=out_specs,
        check_vma=False,
    )
```

```python
import functools

import jax
import jax.numpy as jnp
from jax import lax
from jax.experimental import pallas as pl
from jax.experimental.pallas import tpu as pltpu
from jax.sharding import PartitionSpec as P

INV_STEPS = 24
MESH = pl.DeviceIdType.MESH


def gram_inverse(gram):
    width = gram.shape[0]
    ident = jnp.eye(width, dtype=jnp.float32)
    start = ident / jnp.sqrt(jnp.sum(gram * gram))

    def refine(step_index, current):
        product = jnp.dot(gram, current, precision=lax.Precision.HIGHEST)
        return jnp.dot(current, 2.0 * ident - product, precision=lax.Precision.HIGHEST)

    return lax.fori_loop(0, INV_STEPS, refine, start)


def self_gram(factor_rows):
    return lax.dot_general(
        factor_rows, factor_rows, (((0,), (0,)), ((), ())), preferred_element_type=jnp.float32
    )


def contract_slot(block_slab, b_rows, c_rows):
    side_cells = b_rows.shape[0]
    rank_width = b_rows.shape[1]
    khatri = (b_rows[:, None, :] * c_rows[None, :, :]).reshape(side_cells * side_cells, rank_width)
    flat_slab = block_slab.reshape(block_slab.shape[0], side_cells * side_cells)
    return jnp.dot(flat_slab, khatri, preferred_element_type=jnp.float32)


def layer_allreduce_kernel(nbits, orders, far, ns_plan, x_ref, g_ref, x0_ref, o_ref, inv_ref, acc, gath, *rest):
    rounds = len(orders[0])
    recv_bufs = rest[:rounds]
    far_buf, send_sem, recv_sem, far_send, far_recv = rest[rounds:]
    me = lax.axis_index("layer")
    col = lax.axis_index("inl")
    core = me % 2
    far_ways = far_buf.shape[0]
    far_low = far[0] if far else 0
    far_me = (me // (1 << far_low)) % far_ways

    def far_partner(other):
        return me + (other - far_me) * (1 << far_low)

    barrier = pltpu.get_barrier_semaphore()
    near_bits = [k for k in range(nbits) if k not in far]
    for k in near_bits:
        bit = (me // (1 << k)) % 2
        partner = me + (1 - 2 * bit) * (1 << k)
        pl.semaphore_signal(barrier, inc=1, device_id=(partner, col), device_id_type=MESH)
    for m in range(1, far_ways):
        pl.semaphore_signal(
            barrier, inc=1, device_id=(far_partner((far_me + m) % far_ways), col),
            device_id_type=MESH,
        )
    pl.semaphore_wait(barrier, len(near_bits) + far_ways - 1)

    width = g_ref.shape[0]
    rows = lax.broadcasted_iota(jnp.int32, (width, width), 0)
    cols = lax.broadcasted_iota(jnp.int32, (width, width), 1)
    two_ident = jnp.where(rows == cols, 2.0, 0.0).astype(jnp.float32)
    inv_ref[...] = x0_ref[...]

    def ns_steps(count):
        for _ in range(count):
            current = inv_ref[...]
            product = jnp.dot(
                g_ref[...], current, precision=lax.Precision.HIGHEST,
                preferred_element_type=jnp.float32,
            )
            inv_ref[...] = jnp.dot(
                current, two_ident - product, precision=lax.Precision.HIGHEST,
                preferred_element_type=jnp.float32,
            )

    def partner_of(j):
        step = core * (1 << orders[1][j]) + (1 - core) * (1 << orders[0][j])
        bit = (me // step) % 2
        return me + (1 - 2 * bit) * step, bit

    acc[...] = x_ref[...]
    lo = 0
    size = acc.shape[0]
    spans = []
    plan = iter(ns_plan)
    for j in range(rounds):
        half = size // 2
        partner, bit = partner_of(j)
        keep_lo = lo + bit * half
        send_lo = lo + (1 - bit) * half
        copy = pltpu.make_async_remote_copy(
            src_ref=acc.at[pl.ds(send_lo, half)],
            dst_ref=recv_bufs[j],
            send_sem=send_sem.at[j],
            recv_sem=recv_sem.at[j],
            device_id=(partner, col),
            device_id_type=MESH,
        )
        copy.start()
        ns_steps(next(plan))
        copy.wait()
        acc[pl.ds(keep_lo, half)] = acc[pl.ds(keep_lo, half)] + recv_bufs[j][...]
        spans.append((keep_lo, half))
        lo = keep_lo
        size = half

    if far_ways > 1:
        far_buf[far_me] = acc[pl.ds(lo, size)]
        copies = []
        for m in range(1, far_ways):
            copy = pltpu.make_async_remote_copy(
                src_ref=acc.at[pl.ds(lo, size)],
                dst_ref=far_buf.at[far_me],
                send_sem=far_send.at[m],
                recv_sem=far_recv.at[far_me],
                device_id=(far_partner((far_me + m) % far_ways), col),
                device_id_type=MESH,
            )
            copy.start()
            copies.append(copy)
        ns_steps(next(plan))
        for copy in copies:
            copy.wait_send()
        for m in range(1, far_ways):
            source = (far_me + m) % far_ways
            pltpu.make_async_remote_copy(
                src_ref=acc.at[pl.ds(lo, size)],
                dst_ref=far_buf.at[source],
                send_sem=far_send.at[0],
                recv_sem=far_recv.at[source],
                device_id=(far_partner(source), col),
                device_id_type=MESH,
            ).wait_recv()
        total = far_buf[0]
        for index in range(1, far_ways):
            total = total + far_buf[index]
        gath[pl.ds(lo, size)] = total
    else:
        ns_steps(next(plan))
        gath[pl.ds(lo, size)] = acc[pl.ds(lo, size)]

    for j in reversed(range(rounds)):
        partner, _ = partner_of(j)
        keep_lo, half = spans[j]
        copy = pltpu.make_async_remote_copy(
            src_ref=gath.at[pl.ds(keep_lo, half)],
            dst_ref=gath.at[pl.ds(keep_lo, half)],
            send_sem=send_sem.at[rounds + j],
            recv_sem=recv_sem.at[rounds + j],
            device_id=(partner, col),
            device_id_type=MESH,
        )
        copy.start()
        ns_steps(next(plan))
        copy.wait()

    o_ref[...] = gath[...]


def layer_allreduce_solve(rows, gram, layer_count):
    nbits = layer_count.bit_length() - 1
    far = (3, 4) if nbits >= 5 else ()
    near = [k for k in range(nbits) if k not in far]
    if nbits == 7:
        orders = ((0, 1, 5, 2, 6), (0, 5, 1, 6, 2))
    else:
        orders = (tuple(near), tuple(near))
    rounds = len(near)
    far_ways = 1 << len(far)
    slots = 2 * rounds + 1
    ns_plan = [INV_STEPS // slots + (1 if r < INV_STEPS % slots else 0) for r in range(slots)]
    total = rows.size
    pieces = rows.reshape(layer_count, total // (layer_count * 128), 128)
    width = gram.shape[0]
    start = jnp.eye(width, dtype=jnp.float32) / jnp.sqrt(jnp.sum(gram * gram))
    recv_shapes = [
        pltpu.VMEM((layer_count >> (k + 1),) + pieces.shape[1:], jnp.float32) for k in range(rounds)
    ]
    segment = layer_count >> rounds
    summed, inverse = pl.pallas_call(
        functools.partial(layer_allreduce_kernel, nbits, orders, far, ns_plan),
        out_shape=(
            jax.ShapeDtypeStruct(pieces.shape, jnp.float32),
            jax.ShapeDtypeStruct((width, width), jnp.float32),
        ),
        in_specs=[pl.BlockSpec(memory_space=pltpu.VMEM)] * 3,
        out_specs=(pl.BlockSpec(memory_space=pltpu.VMEM),) * 2,
        scratch_shapes=[pltpu.VMEM(pieces.shape, jnp.float32)] * 2
        + recv_shapes
        + [
            pltpu.VMEM((far_ways, segment) + pieces.shape[1:], jnp.float32),
            pltpu.SemaphoreType.DMA((2 * rounds,)),
            pltpu.SemaphoreType.DMA((2 * rounds,)),
            pltpu.SemaphoreType.DMA((far_ways,)),
            pltpu.SemaphoreType.DMA((far_ways,)),
        ],
        compiler_params=pltpu.CompilerParams(collective_id=0, has_side_effects=True),
    )(pieces, gram, start)
    return summed.reshape(rows.shape), inverse


def inl_gather_kernel(ways, b_ref, c_ref, o_ref, send1, recv1, send2, recv2):
    row = lax.axis_index("layer")
    col = lax.axis_index("inl")
    core = row % 2
    sibling = row + 1 - 2 * core
    half = b_ref.shape[1] // 2
    parts = (b_ref, c_ref)
    mine = pl.ds(pl.multiple_of(core * half, half), half)
    theirs = pl.ds(pl.multiple_of((1 - core) * half, half), half)
    barrier = pltpu.get_barrier_semaphore()
    for step in range(1, ways):
        pl.semaphore_signal(
            barrier, inc=1, device_id=(row, (col + step) % ways), device_id_type=MESH
        )
    pl.semaphore_signal(barrier, inc=1, device_id=(sibling, col), device_id_type=MESH)
    pl.semaphore_wait(barrier, ways)
    copies = []
    for step in range(1, ways):
        for part, x_ref in enumerate(parts):
            copy = pltpu.make_async_remote_copy(
                src_ref=x_ref.at[:, mine],
                dst_ref=o_ref.at[part, :, col, mine],
                send_sem=send1.at[2 * step + part],
                recv_sem=recv1.at[2 * col + part],
                device_id=(row, (col + step) % ways),
                device_id_type=MESH,
            )
            copy.start()
            copies.append(copy)
    for part, x_ref in enumerate(parts):
        o_ref[part, :, col] = x_ref[...]
    forwards = []
    for step in range(1, ways):
        source = (col + step) % ways
        for part in range(2):
            pltpu.make_async_remote_copy(
                src_ref=o_ref.at[part, :, source, mine],
                dst_ref=o_ref.at[part, :, source, mine],
                send_sem=send1.at[part],
                recv_sem=recv1.at[2 * source + part],
                device_id=(row, source),
                device_id_type=MESH,
            ).wait_recv()
        forward = pltpu.make_async_remote_copy(
            src_ref=o_ref.at[:, :, source, mine],
            dst_ref=o_ref.at[:, :, source, mine],
            send_sem=send2.at[step],
            recv_sem=recv2.at[source],
            device_id=(sibling, col),
            device_id_type=MESH,
        )
        forward.start()
        forwards.append(forward)
    for copy in copies:
        copy.wait_send()
    for forward in forwards:
        forward.wait_send()
    for step in range(1, ways):
        source = (col + step) % ways
        pltpu.make_async_remote_copy(
            src_ref=o_ref.at[:, :, source, theirs],
            dst_ref=o_ref.at[:, :, source, theirs],
            send_sem=send2.at[0],
            recv_sem=recv2.at[source],
            device_id=(sibling, col),
            device_id_type=MESH,
        ).wait_recv()


def inl_gather(factor_b, factor_c, ways):
    blocks, cells, rank_width = factor_b.shape
    return pl.pallas_call(
        functools.partial(inl_gather_kernel, ways),
        out_shape=jax.ShapeDtypeStruct((2, blocks, ways, cells, rank_width), factor_b.dtype),
        in_specs=[pl.BlockSpec(memory_space=pltpu.VMEM)] * 2,
        out_specs=pl.BlockSpec(memory_space=pltpu.VMEM),
        scratch_shapes=[pltpu.SemaphoreType.DMA((2 * ways,))] * 2
        + [pltpu.SemaphoreType.DMA((ways,))] * 2,
        compiler_params=pltpu.CompilerParams(collective_id=1, has_side_effects=True),
    )(factor_b, factor_c)


def mttkrp_kernel(coords_ref, filled_ref, blk_ref, b_ref, c_ref, o_ref):
    chunk = 8
    slot = pl.program_id(0)
    _, a_n, b_n, c_n = blk_ref.shape

    @pl.when(slot == 0)
    def _():
        o_ref[...] = jnp.zeros_like(o_ref)

    @pl.when(slot < filled_ref[0])
    def _():
        target = coords_ref[slot * 3]
        b_rows = b_ref[0].astype(jnp.float32)
        c_rows = c_ref[0]

        def body(i, carry):
            start = pl.multiple_of(i * chunk, chunk)
            x = blk_ref[0, pl.ds(start, chunk)].reshape(chunk * b_n, c_n)
            y = jnp.dot(x, c_rows, preferred_element_type=jnp.float32)
            z = y.reshape(chunk, b_n, -1) * b_rows[None]
            z = z.reshape(chunk, b_n // 8, 8, z.shape[-1]).sum(axis=1)
            o_ref[target, pl.ds(start, chunk)] += z.sum(axis=1)
            return carry

        lax.fori_loop(0, a_n // chunk, body, 0)


def mttkrp_rows(blocks, coords, filled, whole_b, whole_c):
    slot_count, a_n, b_n, c_n = blocks.shape
    side_blocks, _, rank_width = whole_b.shape
    grid_spec = pltpu.PrefetchScalarGridSpec(
        num_scalar_prefetch=2,
        grid=(slot_count,),
        in_specs=[
            pl.BlockSpec((1, a_n, b_n, c_n), lambda s, cr, fl: (s, 0, 0, 0)),
            pl.BlockSpec((1, b_n, rank_width), lambda s, cr, fl: (cr[s * 3 + 1], 0, 0)),
            pl.BlockSpec((1, c_n, rank_width), lambda s, cr, fl: (cr[s * 3 + 2], 0, 0)),
        ],
        out_specs=pl.BlockSpec((side_blocks, a_n, rank_width), lambda s, cr, fl: (0, 0, 0)),
    )
    return pl.pallas_call(
        mttkrp_kernel,
        grid_spec=grid_spec,
        out_shape=jax.ShapeDtypeStruct((side_blocks, a_n, rank_width), jnp.float32),
        cost_estimate=pl.CostEstimate(
            flops=2 * slot_count * a_n * b_n * c_n * rank_width,
            bytes_accessed=blocks.size * 2 + slot_count * (b_n + c_n) * rank_width * 2,
            transcendentals=0,
        ),
    )(coords.reshape(-1), filled, blocks, whole_b, whole_c)


def on_device(layer_count, inl_count, blocks, coords, filled, factor_b, factor_c):
    slot_count = blocks.shape[0]
    own_cells = blocks.shape[1]
    side_blocks = factor_b.shape[0]
    rank_width = factor_b.shape[2]
    ways = inl_count
    gathered = inl_gather(factor_b, factor_c, ways)
    whole = gathered.reshape(2, side_blocks, ways * factor_b.shape[1], rank_width)
    whole_b, whole_c = whole[0], whole[1]
    gram_parts = (
        self_gram(whole_b.reshape(-1, rank_width)),
        self_gram(whole_c.reshape(-1, rank_width)),
    )
    buffer = mttkrp_rows(blocks, coords, filled, whole_b, whole_c)
    row_totals = buffer.reshape(side_blocks * own_cells, rank_width)
    summed_all, inverse = layer_allreduce_solve(
        row_totals, gram_parts[0] * gram_parts[1], layer_count
    )
    solved = jnp.dot(summed_all, inverse, precision=lax.Precision.HIGHEST)
    return solved.reshape(side_blocks, own_cells, rank_width)


def solution(mesh):
    in_specs = (
        P("layer", "inl", None, None),
        P("layer", None),
        P("layer"),
        P(None, "inl", None),
        P(None, "inl", None),
    )
    out_specs = P(None, "inl", None)
    return jax.shard_map(
        functools.partial(on_device, mesh.shape["layer"], mesh.shape["inl"]),
        mesh=mesh,
        in_specs=in_specs,
        out_specs=out_specs,
        check_vma=False,
    )
```

```python
import functools

import jax
import jax.numpy as jnp
from jax import lax
from jax.experimental import pallas as pl
from jax.experimental.pallas import tpu as pltpu
from jax.sharding import PartitionSpec as P

INV_STEPS = 24
MESH = pl.DeviceIdType.MESH


def gram_inverse(gram):
    width = gram.shape[0]
    ident = jnp.eye(width, dtype=jnp.float32)
    start = ident / jnp.sqrt(jnp.sum(gram * gram))

    def refine(step_index, current):
        product = jnp.dot(gram, current, precision=lax.Precision.HIGHEST)
        return jnp.dot(current, 2.0 * ident - product, precision=lax.Precision.HIGHEST)

    return lax.fori_loop(0, INV_STEPS, refine, start)


def self_gram(factor_rows):
    return lax.dot_general(
        factor_rows, factor_rows, (((0,), (0,)), ((), ())), preferred_element_type=jnp.float32
    )


def contract_slot(block_slab, b_rows, c_rows):
    side_cells = b_rows.shape[0]
    rank_width = b_rows.shape[1]
    khatri = (b_rows[:, None, :] * c_rows[None, :, :]).reshape(side_cells * side_cells, rank_width)
    flat_slab = block_slab.reshape(block_slab.shape[0], side_cells * side_cells)
    return jnp.dot(flat_slab, khatri, preferred_element_type=jnp.float32)


def layer_allreduce_kernel(stages, far, ns_plan, x_ref, g_ref, x0_ref, o_ref, inv_ref, acc, gath, *rest):
    count = len(stages)
    bufs = rest[:count]
    far_buf = rest[count]
    send_rs, recv_rs, send_ag, recv_ag, far_send, far_recv = rest[count + 1:]
    me = lax.axis_index("layer")
    col = lax.axis_index("inl")
    far_ways = far_buf.shape[0]

    def group_index(low, ways):
        return (me // (1 << low)) % ways

    def member(low, ways, other):
        return me + (other - group_index(low, ways)) * (1 << low)

    groups = [(low, 2 if kind == "bin" else 4) for kind, low in stages]
    if far:
        groups.append((far[0], far_ways))
    barrier = pltpu.get_barrier_semaphore()
    signals = 0
    for low, ways in groups:
        mine = group_index(low, ways)
        for m in range(1, ways):
            pl.semaphore_signal(
                barrier, inc=1, device_id=(member(low, ways, (mine + m) % ways), col),
                device_id_type=MESH,
            )
            signals += 1
    pl.semaphore_wait(barrier, signals)

    width = g_ref.shape[0]
    rows = lax.broadcasted_iota(jnp.int32, (width, width), 0)
    cols = lax.broadcasted_iota(jnp.int32, (width, width), 1)
    two_ident = jnp.where(rows == cols, 2.0, 0.0).astype(jnp.float32)
    inv_ref[...] = x0_ref[...]
    plan = iter(ns_plan)

    def ns_steps():
        for _ in range(next(plan)):
            current = inv_ref[...]
            product = jnp.dot(
                g_ref[...], current, precision=lax.Precision.HIGHEST,
                preferred_element_type=jnp.float32,
            )
            inv_ref[...] = jnp.dot(
                current, two_ident - product, precision=lax.Precision.HIGHEST,
                preferred_element_type=jnp.float32,
            )

    acc[...] = x_ref[...]
    lo = 0
    size = acc.shape[0]
    spans = []
    for j, (low, ways) in enumerate(groups[:count]):
        piece = size // ways
        mine = group_index(low, ways)
        copies = []
        for m in range(1, ways):
            other = (mine + m) % ways
            copy = pltpu.make_async_remote_copy(
                src_ref=acc.at[pl.ds(lo + other * piece, piece)],
                dst_ref=bufs[j].at[mine],
                send_sem=send_rs.at[4 * j + m],
                recv_sem=recv_rs.at[4 * j + mine],
                device_id=(member(low, ways, other), col),
                device_id_type=MESH,
            )
            copy.start()
            copies.append(copy)
        keep_lo = lo + mine * piece
        bufs[j][mine] = acc[pl.ds(keep_lo, piece)]
        ns_steps()
        for copy in copies:
            copy.wait_send()
        for m in range(1, ways):
            source = (mine + m) % ways
            pltpu.make_async_remote_copy(
                src_ref=bufs[j].at[source],
                dst_ref=bufs[j].at[source],
                send_sem=send_rs.at[4 * j],
                recv_sem=recv_rs.at[4 * j + source],
                device_id=(member(low, ways, source), col),
                device_id_type=MESH,
            ).wait_recv()
        total = bufs[j][0]
        for index in range(1, ways):
            total = total + bufs[j][index]
        acc[pl.ds(keep_lo, piece)] = total
        spans.append((lo, piece))
        lo = keep_lo
        size = piece

    if far:
        far_me = group_index(far[0], far_ways)
        far_buf[far_me] = acc[pl.ds(lo, size)]
        copies = []
        for m in range(1, far_ways):
            copy = pltpu.make_async_remote_copy(
                src_ref=acc.at[pl.ds(lo, size)],
                dst_ref=far_buf.at[far_me],
                send_sem=far_send.at[m],
                recv_sem=far_recv.at[far_me],
                device_id=(member(far[0], far_ways, (far_me + m) % far_ways), col),
                device_id_type=MESH,
            )
            copy.start()
            copies.append(copy)
        ns_steps()
        for copy in copies:
            copy.wait_send()
        for m in range(1, far_ways):
            source = (far_me + m) % far_ways
            pltpu.make_async_remote_copy(
                src_ref=far_buf.at[source],
                dst_ref=far_buf.at[source],
                send_sem=far_send.at[0],
                recv_sem=far_recv.at[source],
                device_id=(member(far[0], far_ways, source), col),
                device_id_type=MESH,
            ).wait_recv()
        total = far_buf[0]
        for index in range(1, far_ways):
            total = total + far_buf[index]
        gath[pl.ds(lo, size)] = total
    else:
        ns_steps()
        gath[pl.ds(lo, size)] = acc[pl.ds(lo, size)]

    for j in reversed(range(count)):
        low, ways = groups[j]
        base, piece = spans[j]
        mine = group_index(low, ways)
        own = pl.ds(base + mine * piece, piece)
        copies = []
        for m in range(1, ways):
            other = (mine + m) % ways
            copy = pltpu.make_async_remote_copy(
                src_ref=gath.at[own],
                dst_ref=gath.at[own],
                send_sem=send_ag.at[4 * j + m],
                recv_sem=recv_ag.at[4 * j + mine],
                device_id=(member(low, ways, other), col),
                device_id_type=MESH,
            )
            copy.start()
            copies.append(copy)
        ns_steps()
        for copy in copies:
            copy.wait_send()
        for m in range(1, ways):
            source = (mine + m) % ways
            theirs = pl.ds(base + source * piece, piece)
            pltpu.make_async_remote_copy(
                src_ref=gath.at[theirs],
                dst_ref=gath.at[theirs],
                send_sem=send_ag.at[4 * j],
                recv_sem=recv_ag.at[4 * j + source],
                device_id=(member(low, ways, source), col),
                device_id_type=MESH,
            ).wait_recv()

    o_ref[...] = gath[...]


def layer_allreduce_solve(rows, gram, layer_count):
    nbits = layer_count.bit_length() - 1
    if nbits == 7:
        stages, far = (("bin", 0), ("bin", 1), ("bin", 2), ("quad", 5)), (3, 4)
    elif nbits == 5:
        stages, far = (("bin", 0), ("quad", 1)), (3, 4)
    else:
        stages, far = tuple(("bin", k) for k in range(nbits)), ()
    count = len(stages)
    far_ways = 1 << len(far)
    slots = 2 * count + 1
    ns_plan = [INV_STEPS // slots + (1 if r < INV_STEPS % slots else 0) for r in range(slots)]
    total = rows.size
    pieces = rows.reshape(layer_count, total // (layer_count * 128), 128)
    width = gram.shape[0]
    start = jnp.eye(width, dtype=jnp.float32) / jnp.sqrt(jnp.sum(gram * gram))
    buf_shapes = []
    size = layer_count
    for kind, _ in stages:
        ways = 2 if kind == "bin" else 4
        size //= ways
        buf_shapes.append(pltpu.VMEM((ways, size) + pieces.shape[1:], jnp.float32))
    summed, inverse = pl.pallas_call(
        functools.partial(layer_allreduce_kernel, stages, far, ns_plan),
        out_shape=(
            jax.ShapeDtypeStruct(pieces.shape, jnp.float32),
            jax.ShapeDtypeStruct((width, width), jnp.float32),
        ),
        in_specs=[pl.BlockSpec(memory_space=pltpu.VMEM)] * 3,
        out_specs=(pl.BlockSpec(memory_space=pltpu.VMEM),) * 2,
        scratch_shapes=[pltpu.VMEM(pieces.shape, jnp.float32)] * 2
        + buf_shapes
        + [pltpu.VMEM((far_ways, size) + pieces.shape[1:], jnp.float32)]
        + [pltpu.SemaphoreType.DMA((4 * count,))] * 4
        + [pltpu.SemaphoreType.DMA((far_ways,))] * 2,
        compiler_params=pltpu.CompilerParams(collective_id=0, has_side_effects=True),
    )(pieces, gram, start)
    return summed.reshape(rows.shape), inverse


def inl_gather_kernel(ways, b_ref, c_ref, o_ref, send1, recv1, send2, recv2):
    row = lax.axis_index("layer")
    col = lax.axis_index("inl")
    core = row % 2
    sibling = row + 1 - 2 * core
    half = b_ref.shape[1] // 2
    parts = (b_ref, c_ref)
    mine = pl.ds(pl.multiple_of(core * half, half), half)
    theirs = pl.ds(pl.multiple_of((1 - core) * half, half), half)
    barrier = pltpu.get_barrier_semaphore()
    for step in range(1, ways):
        pl.semaphore_signal(
            barrier, inc=1, device_id=(row, (col + step) % ways), device_id_type=MESH
        )
    pl.semaphore_signal(barrier, inc=1, device_id=(sibling, col), device_id_type=MESH)
    pl.semaphore_wait(barrier, ways)
    copies = []
    for step in range(1, ways):
        for part, x_ref in enumerate(parts):
            copy = pltpu.make_async_remote_copy(
                src_ref=x_ref.at[:, mine],
                dst_ref=o_ref.at[part, :, col, mine],
                send_sem=send1.at[2 * step + part],
                recv_sem=recv1.at[2 * col + part],
                device_id=(row, (col + step) % ways),
                device_id_type=MESH,
            )
            copy.start()
            copies.append(copy)
    for part, x_ref in enumerate(parts):
        o_ref[part, :, col] = x_ref[...]
    forwards = []
    for step in range(1, ways):
        source = (col + step) % ways
        for part in range(2):
            pltpu.make_async_remote_copy(
                src_ref=o_ref.at[part, :, source, mine],
                dst_ref=o_ref.at[part, :, source, mine],
                send_sem=send1.at[part],
                recv_sem=recv1.at[2 * source + part],
                device_id=(row, source),
                device_id_type=MESH,
            ).wait_recv()
        forward = pltpu.make_async_remote_copy(
            src_ref=o_ref.at[:, :, source, mine],
            dst_ref=o_ref.at[:, :, source, mine],
            send_sem=send2.at[step],
            recv_sem=recv2.at[source],
            device_id=(sibling, col),
            device_id_type=MESH,
        )
        forward.start()
        forwards.append(forward)
    for copy in copies:
        copy.wait_send()
    for forward in forwards:
        forward.wait_send()
    for step in range(1, ways):
        source = (col + step) % ways
        pltpu.make_async_remote_copy(
            src_ref=o_ref.at[:, :, source, theirs],
            dst_ref=o_ref.at[:, :, source, theirs],
            send_sem=send2.at[0],
            recv_sem=recv2.at[source],
            device_id=(sibling, col),
            device_id_type=MESH,
        ).wait_recv()


def inl_gather(factor_b, factor_c, ways):
    blocks, cells, rank_width = factor_b.shape
    return pl.pallas_call(
        functools.partial(inl_gather_kernel, ways),
        out_shape=jax.ShapeDtypeStruct((2, blocks, ways, cells, rank_width), factor_b.dtype),
        in_specs=[pl.BlockSpec(memory_space=pltpu.VMEM)] * 2,
        out_specs=pl.BlockSpec(memory_space=pltpu.VMEM),
        scratch_shapes=[pltpu.SemaphoreType.DMA((2 * ways,))] * 2
        + [pltpu.SemaphoreType.DMA((ways,))] * 2,
        compiler_params=pltpu.CompilerParams(collective_id=1, has_side_effects=True),
    )(factor_b, factor_c)


def mttkrp_kernel(coords_ref, filled_ref, blk_ref, b_ref, c_ref, o_ref):
    chunk = 8
    slot = pl.program_id(0)
    _, a_n, b_n, c_n = blk_ref.shape

    @pl.when(slot == 0)
    def _():
        o_ref[...] = jnp.zeros_like(o_ref)

    @pl.when(slot < filled_ref[0])
    def _():
        target = coords_ref[slot * 3]
        b_rows = b_ref[0].astype(jnp.float32)
        c_rows = c_ref[0]

        def body(i, carry):
            start = pl.multiple_of(i * chunk, chunk)
            x = blk_ref[0, pl.ds(start, chunk)].reshape(chunk * b_n, c_n)
            y = jnp.dot(x, c_rows, preferred_element_type=jnp.float32)
            z = y.reshape(chunk, b_n, -1) * b_rows[None]
            z = z.reshape(chunk, b_n // 8, 8, z.shape[-1]).sum(axis=1)
            o_ref[target, pl.ds(start, chunk)] += z.sum(axis=1)
            return carry

        lax.fori_loop(0, a_n // chunk, body, 0)


def mttkrp_rows(blocks, coords, filled, whole_b, whole_c):
    slot_count, a_n, b_n, c_n = blocks.shape
    side_blocks, _, rank_width = whole_b.shape
    grid_spec = pltpu.PrefetchScalarGridSpec(
        num_scalar_prefetch=2,
        grid=(slot_count,),
        in_specs=[
            pl.BlockSpec((1, a_n, b_n, c_n), lambda s, cr, fl: (s, 0, 0, 0)),
            pl.BlockSpec((1, b_n, rank_width), lambda s, cr, fl: (cr[s * 3 + 1], 0, 0)),
            pl.BlockSpec((1, c_n, rank_width), lambda s, cr, fl: (cr[s * 3 + 2], 0, 0)),
        ],
        out_specs=pl.BlockSpec((side_blocks, a_n, rank_width), lambda s, cr, fl: (0, 0, 0)),
    )
    return pl.pallas_call(
        mttkrp_kernel,
        grid_spec=grid_spec,
        out_shape=jax.ShapeDtypeStruct((side_blocks, a_n, rank_width), jnp.float32),
        cost_estimate=pl.CostEstimate(
            flops=2 * slot_count * a_n * b_n * c_n * rank_width,
            bytes_accessed=blocks.size * 2 + slot_count * (b_n + c_n) * rank_width * 2,
            transcendentals=0,
        ),
    )(coords.reshape(-1), filled, blocks, whole_b, whole_c)


def on_device(layer_count, inl_count, blocks, coords, filled, factor_b, factor_c):
    slot_count = blocks.shape[0]
    own_cells = blocks.shape[1]
    side_blocks = factor_b.shape[0]
    rank_width = factor_b.shape[2]
    ways = inl_count
    gathered = inl_gather(factor_b, factor_c, ways)
    whole = gathered.reshape(2, side_blocks, ways * factor_b.shape[1], rank_width)
    whole_b, whole_c = whole[0], whole[1]
    gram_parts = (
        self_gram(whole_b.reshape(-1, rank_width)),
        self_gram(whole_c.reshape(-1, rank_width)),
    )
    buffer = mttkrp_rows(blocks, coords, filled, whole_b, whole_c)
    row_totals = buffer.reshape(side_blocks * own_cells, rank_width)
    summed_all, inverse = layer_allreduce_solve(
        row_totals, gram_parts[0] * gram_parts[1], layer_count
    )
    solved = jnp.dot(summed_all, inverse, precision=lax.Precision.HIGHEST)
    return solved.reshape(side_blocks, own_cells, rank_width)


def solution(mesh):
    in_specs = (
        P("layer", "inl", None, None),
        P("layer", None),
        P("layer"),
        P(None, "inl", None),
        P(None, "inl", None),
    )
    out_specs = P(None, "inl", None)
    return jax.shard_map(
        functools.partial(on_device, mesh.shape["layer"], mesh.shape["inl"]),
        mesh=mesh,
        in_specs=in_specs,
        out_specs=out_specs,
        check_vma=False,
    )
```

```python
import functools

import jax
import jax.numpy as jnp
from jax import lax
from jax.experimental import pallas as pl
from jax.experimental.pallas import tpu as pltpu
from jax.sharding import PartitionSpec as P

INV_STEPS = 24
MESH = pl.DeviceIdType.MESH


def self_gram(factor_rows):
    return lax.dot_general(
        factor_rows, factor_rows, (((0,), (0,)), ((), ())), preferred_element_type=jnp.float32
    )


def layer_allreduce_kernel(stages, far, ns_plan, x_ref, g_ref, x0_ref, o_ref, inv_ref, acc, gath, *rest):
    count = len(stages)
    bufs = rest[:count]
    far_buf = rest[count]
    send_rs, recv_rs, send_ag, recv_ag, far_send, far_recv = rest[count + 1:]
    me = lax.axis_index("layer")
    col = lax.axis_index("inl")
    far_ways = far_buf.shape[0]

    def group_index(low, ways):
        return (me // (1 << low)) % ways

    def member(low, ways, other):
        return me + (other - group_index(low, ways)) * (1 << low)

    groups = [(low, 2 if kind == "bin" else 4) for kind, low in stages]
    if far:
        groups.append((far[0], far_ways))
    barrier = pltpu.get_barrier_semaphore()
    signals = 0
    for low, ways in groups:
        mine = group_index(low, ways)
        for m in range(1, ways):
            pl.semaphore_signal(
                barrier, inc=1, device_id=(member(low, ways, (mine + m) % ways), col),
                device_id_type=MESH,
            )
            signals += 1
    pl.semaphore_wait(barrier, signals)

    width = g_ref.shape[0]
    rows = lax.broadcasted_iota(jnp.int32, (width, width), 0)
    cols = lax.broadcasted_iota(jnp.int32, (width, width), 1)
    two_ident = jnp.where(rows == cols, 2.0, 0.0).astype(jnp.float32)
    inv_ref[...] = x0_ref[...]
    plan = iter(ns_plan)

    def ns_steps():
        for _ in range(next(plan)):
            current = inv_ref[...]
            product = jnp.dot(
                g_ref[...], current, precision=lax.Precision.HIGHEST,
                preferred_element_type=jnp.float32,
            )
            inv_ref[...] = jnp.dot(
                current, two_ident - product, precision=lax.Precision.HIGHEST,
                preferred_element_type=jnp.float32,
            )

    acc[...] = x_ref[...]
    lo = 0
    size = acc.shape[0]
    spans = []
    for j, (low, ways) in enumerate(groups[:count]):
        piece = size // ways
        mine = group_index(low, ways)
        copies = []
        for m in range(1, ways):
            other = (mine + m) % ways
            copy = pltpu.make_async_remote_copy(
                src_ref=acc.at[pl.ds(pl.multiple_of(lo + other * piece, 8), piece)],
                dst_ref=bufs[j].at[mine],
                send_sem=send_rs.at[4 * j + m],
                recv_sem=recv_rs.at[4 * j + mine],
                device_id=(member(low, ways, other), col),
                device_id_type=MESH,
            )
            copy.start()
            copies.append(copy)
        keep_lo = pl.multiple_of(lo + mine * piece, 8)
        bufs[j][mine] = acc[pl.ds(keep_lo, piece)]
        ns_steps()
        for copy in copies:
            copy.wait_send()
        for m in range(1, ways):
            source = (mine + m) % ways
            pltpu.make_async_remote_copy(
                src_ref=bufs[j].at[source],
                dst_ref=bufs[j].at[source],
                send_sem=send_rs.at[4 * j],
                recv_sem=recv_rs.at[4 * j + source],
                device_id=(member(low, ways, source), col),
                device_id_type=MESH,
            ).wait_recv()
        total = bufs[j][0]
        for index in range(1, ways):
            total = total + bufs[j][index]
        acc[pl.ds(keep_lo, piece)] = total
        spans.append((lo, piece))
        lo = keep_lo
        size = piece

    if far:
        far_me = group_index(far[0], far_ways)
        far_buf[far_me] = acc[pl.ds(lo, size)]
        copies = []
        for m in range(1, far_ways):
            copy = pltpu.make_async_remote_copy(
                src_ref=acc.at[pl.ds(lo, size)],
                dst_ref=far_buf.at[far_me],
                send_sem=far_send.at[m],
                recv_sem=far_recv.at[far_me],
                device_id=(member(far[0], far_ways, (far_me + m) % far_ways), col),
                device_id_type=MESH,
            )
            copy.start()
            copies.append(copy)
        ns_steps()
        for copy in copies:
            copy.wait_send()
        for m in range(1, far_ways):
            source = (far_me + m) % far_ways
            pltpu.make_async_remote_copy(
                src_ref=far_buf.at[source],
                dst_ref=far_buf.at[source],
                send_sem=far_send.at[0],
                recv_sem=far_recv.at[source],
                device_id=(member(far[0], far_ways, source), col),
                device_id_type=MESH,
            ).wait_recv()
        total = far_buf[0]
        for index in range(1, far_ways):
            total = total + far_buf[index]
        gath[pl.ds(lo, size)] = total
    else:
        ns_steps()
        gath[pl.ds(lo, size)] = acc[pl.ds(lo, size)]

    for j in reversed(range(count)):
        low, ways = groups[j]
        base, piece = spans[j]
        mine = group_index(low, ways)
        own = pl.ds(pl.multiple_of(base + mine * piece, 8), piece)
        copies = []
        for m in range(1, ways):
            other = (mine + m) % ways
            copy = pltpu.make_async_remote_copy(
                src_ref=gath.at[own],
                dst_ref=gath.at[own],
                send_sem=send_ag.at[4 * j + m],
                recv_sem=recv_ag.at[4 * j + mine],
                device_id=(member(low, ways, other), col),
                device_id_type=MESH,
            )
            copy.start()
            copies.append(copy)
        ns_steps()
        for copy in copies:
            copy.wait_send()
        for m in range(1, ways):
            source = (mine + m) % ways
            theirs = pl.ds(pl.multiple_of(base + source * piece, 8), piece)
            pltpu.make_async_remote_copy(
                src_ref=gath.at[theirs],
                dst_ref=gath.at[theirs],
                send_sem=send_ag.at[4 * j],
                recv_sem=recv_ag.at[4 * j + source],
                device_id=(member(low, ways, source), col),
                device_id_type=MESH,
            ).wait_recv()

    o_ref[...] = jnp.dot(
        gath[...], inv_ref[...], precision=lax.Precision.HIGHEST,
        preferred_element_type=jnp.float32,
    )


def layer_allreduce_solve(rows, gram, layer_count):
    nbits = layer_count.bit_length() - 1
    if nbits == 7:
        stages, far = (("bin", 0), ("bin", 1), ("bin", 2), ("quad", 5)), (3, 4)
    elif nbits == 5:
        stages, far = (("bin", 0), ("quad", 1)), (3, 4)
    else:
        stages, far = tuple(("bin", k) for k in range(nbits)), ()
    count = len(stages)
    far_ways = 1 << len(far)
    slots = 2 * count + 1
    ns_plan = [INV_STEPS // slots + (1 if r < INV_STEPS % slots else 0) for r in range(slots)]
    pieces = rows
    width = gram.shape[0]
    start = jnp.eye(width, dtype=jnp.float32) / jnp.sqrt(jnp.sum(gram * gram))
    buf_shapes = []
    size = rows.shape[0]
    for kind, _ in stages:
        ways = 2 if kind == "bin" else 4
        size //= ways
        buf_shapes.append(pltpu.VMEM((ways, size) + pieces.shape[1:], jnp.float32))
    solved, inverse = pl.pallas_call(
        functools.partial(layer_allreduce_kernel, stages, far, ns_plan),
        out_shape=(
            jax.ShapeDtypeStruct(pieces.shape, jnp.float32),
            jax.ShapeDtypeStruct((width, width), jnp.float32),
        ),
        in_specs=[pl.BlockSpec(memory_space=pltpu.VMEM)] * 3,
        out_specs=(pl.BlockSpec(memory_space=pltpu.VMEM),) * 2,
        scratch_shapes=[pltpu.VMEM(pieces.shape, jnp.float32)] * 2
        + buf_shapes
        + [pltpu.VMEM((far_ways, size) + pieces.shape[1:], jnp.float32)]
        + [pltpu.SemaphoreType.DMA((4 * count,))] * 4
        + [pltpu.SemaphoreType.DMA((far_ways,))] * 2,
        compiler_params=pltpu.CompilerParams(collective_id=0, has_side_effects=True),
    )(pieces, gram, start)
    return solved


def inl_gather_kernel(ways, b_ref, c_ref, o_ref, send1, recv1, send2, recv2):
    row = lax.axis_index("layer")
    col = lax.axis_index("inl")
    core = row % 2
    sibling = row + 1 - 2 * core
    half = b_ref.shape[1] // 2
    parts = (b_ref, c_ref)
    mine = pl.ds(pl.multiple_of(core * half, half), half)
    theirs = pl.ds(pl.multiple_of((1 - core) * half, half), half)
    barrier = pltpu.get_barrier_semaphore()
    for step in range(1, ways):
        pl.semaphore_signal(
            barrier, inc=1, device_id=(row, (col + step) % ways), device_id_type=MESH
        )
    pl.semaphore_signal(barrier, inc=1, device_id=(sibling, col), device_id_type=MESH)
    pl.semaphore_wait(barrier, ways)
    copies = []
    for step in range(1, ways):
        for part, x_ref in enumerate(parts):
            copy = pltpu.make_async_remote_copy(
                src_ref=x_ref.at[:, mine],
                dst_ref=o_ref.at[part, :, col, mine],
                send_sem=send1.at[2 * step + part],
                recv_sem=recv1.at[2 * col + part],
                device_id=(row, (col + step) % ways),
                device_id_type=MESH,
            )
            copy.start()
            copies.append(copy)
    for part, x_ref in enumerate(parts):
        o_ref[part, :, col] = x_ref[...]
    forwards = []
    for step in range(1, ways):
        source = (col + step) % ways
        for part in range(2):
            pltpu.make_async_remote_copy(
                src_ref=o_ref.at[part, :, source, mine],
                dst_ref=o_ref.at[part, :, source, mine],
                send_sem=send1.at[part],
                recv_sem=recv1.at[2 * source + part],
                device_id=(row, source),
                device_id_type=MESH,
            ).wait_recv()
        forward = pltpu.make_async_remote_copy(
            src_ref=o_ref.at[:, :, source, mine],
            dst_ref=o_ref.at[:, :, source, mine],
            send_sem=send2.at[step],
            recv_sem=recv2.at[source],
            device_id=(sibling, col),
            device_id_type=MESH,
        )
        forward.start()
        forwards.append(forward)
    for copy in copies:
        copy.wait_send()
    for forward in forwards:
        forward.wait_send()
    for step in range(1, ways):
        source = (col + step) % ways
        pltpu.make_async_remote_copy(
            src_ref=o_ref.at[:, :, source, theirs],
            dst_ref=o_ref.at[:, :, source, theirs],
            send_sem=send2.at[0],
            recv_sem=recv2.at[source],
            device_id=(sibling, col),
            device_id_type=MESH,
        ).wait_recv()


def inl_gather(factor_b, factor_c, ways):
    blocks, cells, rank_width = factor_b.shape
    return pl.pallas_call(
        functools.partial(inl_gather_kernel, ways),
        out_shape=jax.ShapeDtypeStruct((2, blocks, ways, cells, rank_width), factor_b.dtype),
        in_specs=[pl.BlockSpec(memory_space=pltpu.VMEM)] * 2,
        out_specs=pl.BlockSpec(memory_space=pltpu.VMEM),
        scratch_shapes=[pltpu.SemaphoreType.DMA((2 * ways,))] * 2
        + [pltpu.SemaphoreType.DMA((ways,))] * 2,
        compiler_params=pltpu.CompilerParams(collective_id=1, has_side_effects=True),
    )(factor_b, factor_c)


def mttkrp_kernel(coords_ref, filled_ref, blk_ref, b_ref, c_ref, o_ref):
    chunk = 8
    slot = pl.program_id(0)
    _, a_n, b_n, c_n = blk_ref.shape

    @pl.when(slot == 0)
    def _():
        o_ref[...] = jnp.zeros_like(o_ref)

    @pl.when(slot < filled_ref[0])
    def _():
        target = coords_ref[slot, 0]
        b_rows = b_ref[0].astype(jnp.float32)
        c_rows = c_ref[0]

        def body(i, carry):
            start = pl.multiple_of(i * chunk, chunk)
            x = blk_ref[0, pl.ds(start, chunk)].reshape(chunk * b_n, c_n)
            y = jnp.dot(x, c_rows, preferred_element_type=jnp.float32)
            z = y.reshape(chunk, b_n, -1) * b_rows[None]
            z = z.reshape(chunk, b_n // 8, 8, z.shape[-1]).sum(axis=1)
            o_ref[target, pl.ds(start, chunk)] += z.sum(axis=1)
            return carry

        lax.fori_loop(0, a_n // chunk, body, 0)


def mttkrp_rows(blocks, coords, filled, whole_b, whole_c):
    slot_count, a_n, b_n, c_n = blocks.shape
    side_blocks, _, rank_width = whole_b.shape
    grid_spec = pltpu.PrefetchScalarGridSpec(
        num_scalar_prefetch=2,
        grid=(slot_count,),
        in_specs=[
            pl.BlockSpec((1, a_n, b_n, c_n), lambda s, cr, fl: (s, 0, 0, 0)),
            pl.BlockSpec((1, b_n, rank_width), lambda s, cr, fl: (cr[s, 1], 0, 0)),
            pl.BlockSpec((1, c_n, rank_width), lambda s, cr, fl: (cr[s, 2], 0, 0)),
        ],
        out_specs=pl.BlockSpec((side_blocks, a_n, rank_width), lambda s, cr, fl: (0, 0, 0)),
    )
    return pl.pallas_call(
        mttkrp_kernel,
        grid_spec=grid_spec,
        out_shape=jax.ShapeDtypeStruct((side_blocks, a_n, rank_width), jnp.float32),
        cost_estimate=pl.CostEstimate(
            flops=2 * slot_count * a_n * b_n * c_n * rank_width,
            bytes_accessed=blocks.size * 2 + slot_count * (b_n + c_n) * rank_width * 2,
            transcendentals=0,
        ),
    )(coords, filled, blocks, whole_b, whole_c)


def on_device(layer_count, inl_count, blocks, coords, filled, factor_b, factor_c):
    slot_count = blocks.shape[0]
    own_cells = blocks.shape[1]
    side_blocks = factor_b.shape[0]
    rank_width = factor_b.shape[2]
    ways = inl_count
    gathered = inl_gather(factor_b, factor_c, ways)
    whole = gathered.reshape(2, side_blocks, ways * factor_b.shape[1], rank_width)
    whole_b, whole_c = whole[0], whole[1]
    gram_parts = (
        self_gram(whole_b.reshape(-1, rank_width)),
        self_gram(whole_c.reshape(-1, rank_width)),
    )
    buffer = mttkrp_rows(blocks, coords, filled, whole_b, whole_c)
    row_totals = buffer.reshape(side_blocks * own_cells, rank_width)
    solved = layer_allreduce_solve(row_totals, gram_parts[0] * gram_parts[1], layer_count)
    return solved.reshape(side_blocks, own_cells, rank_width)


def solution(mesh):
    in_specs = (
        P("layer", "inl", None, None),
        P("layer", None),
        P("layer"),
        P(None, "inl", None),
        P(None, "inl", None),
    )
    out_specs = P(None, "inl", None)
    return jax.shard_map(
        functools.partial(on_device, mesh.shape["layer"], mesh.shape["inl"]),
        mesh=mesh,
        in_specs=in_specs,
        out_specs=out_specs,
        check_vma=False,
    )
```

```python
import functools

import jax
import jax.numpy as jnp
from jax import lax
from jax.experimental import pallas as pl
from jax.experimental.pallas import tpu as pltpu
from jax.sharding import PartitionSpec as P

INV_STEPS = 24
MESH = pl.DeviceIdType.MESH


def self_gram(factor_rows):
    return lax.dot_general(
        factor_rows, factor_rows, (((0,), (0,)), ((), ())), preferred_element_type=jnp.float32
    )


def layer_allreduce_kernel(stages, far, ns_plan, x_ref, g_ref, x0_ref, o_ref, inv_ref, acc, gath, *rest):
    count = len(stages)
    bufs = rest[:count]
    far_buf = rest[count]
    send_rs, recv_rs, send_ag, recv_ag, far_send, far_recv = rest[count + 1:]
    me = lax.axis_index("layer")
    col = lax.axis_index("inl")
    far_ways = far_buf.shape[0]

    def group_index(low, ways):
        return (me // (1 << low)) % ways

    def member(low, ways, other):
        return me + (other - group_index(low, ways)) * (1 << low)

    groups = [(low, 2 if kind == "bin" else 4) for kind, low in stages]
    if far:
        groups.append((far[0], far_ways))
    barrier = pltpu.get_barrier_semaphore()
    signals = 0
    for low, ways in groups:
        mine = group_index(low, ways)
        for m in range(1, ways):
            pl.semaphore_signal(
                barrier, inc=1, device_id=(member(low, ways, (mine + m) % ways), col),
                device_id_type=MESH,
            )
            signals += 1
    pl.semaphore_wait(barrier, signals)

    width = g_ref.shape[0]
    rows = lax.broadcasted_iota(jnp.int32, (width, width), 0)
    cols = lax.broadcasted_iota(jnp.int32, (width, width), 1)
    two_ident = jnp.where(rows == cols, 2.0, 0.0).astype(jnp.float32)
    inv_ref[...] = x0_ref[...]
    plan = iter(ns_plan)

    def ns_steps():
        for _ in range(next(plan)):
            current = inv_ref[...]
            product = jnp.dot(
                g_ref[...], current, precision=lax.Precision.HIGHEST,
                preferred_element_type=jnp.float32,
            )
            inv_ref[...] = jnp.dot(
                current, two_ident - product, precision=lax.Precision.HIGHEST,
                preferred_element_type=jnp.float32,
            )

    acc[...] = x_ref[...]
    lo = 0
    size = acc.shape[0]
    spans = []
    for j, (low, ways) in enumerate(groups[:count]):
        piece = size // ways
        mine = group_index(low, ways)
        copies = []
        for m in range(1, ways):
            other = (mine + m) % ways
            copy = pltpu.make_async_remote_copy(
                src_ref=acc.at[pl.ds(pl.multiple_of(lo + other * piece, 8), piece)],
                dst_ref=bufs[j].at[mine],
                send_sem=send_rs.at[4 * j + m],
                recv_sem=recv_rs.at[4 * j + mine],
                device_id=(member(low, ways, other), col),
                device_id_type=MESH,
            )
            copy.start()
            copies.append(copy)
        keep_lo = pl.multiple_of(lo + mine * piece, 8)
        bufs[j][mine] = acc[pl.ds(keep_lo, piece)]
        ns_steps()
        for copy in copies:
            copy.wait_send()
        for m in range(1, ways):
            source = (mine + m) % ways
            pltpu.make_async_remote_copy(
                src_ref=bufs[j].at[source],
                dst_ref=bufs[j].at[source],
                send_sem=send_rs.at[4 * j],
                recv_sem=recv_rs.at[4 * j + source],
                device_id=(member(low, ways, source), col),
                device_id_type=MESH,
            ).wait_recv()
        total = bufs[j][0]
        for index in range(1, ways):
            total = total + bufs[j][index]
        acc[pl.ds(keep_lo, piece)] = total
        spans.append((lo, piece))
        lo = keep_lo
        size = piece

    if far:
        far_me = group_index(far[0], far_ways)
        far_buf[far_me] = acc[pl.ds(lo, size)]
        copies = []
        for m in range(1, far_ways):
            copy = pltpu.make_async_remote_copy(
                src_ref=acc.at[pl.ds(lo, size)],
                dst_ref=far_buf.at[far_me],
                send_sem=far_send.at[m],
                recv_sem=far_recv.at[far_me],
                device_id=(member(far[0], far_ways, (far_me + m) % far_ways), col),
                device_id_type=MESH,
            )
            copy.start()
            copies.append(copy)
        ns_steps()
        for copy in copies:
            copy.wait_send()
        for m in range(1, far_ways):
            source = (far_me + m) % far_ways
            pltpu.make_async_remote_copy(
                src_ref=far_buf.at[source],
                dst_ref=far_buf.at[source],
                send_sem=far_send.at[0],
                recv_sem=far_recv.at[source],
                device_id=(member(far[0], far_ways, source), col),
                device_id_type=MESH,
            ).wait_recv()
        total = far_buf[0]
        for index in range(1, far_ways):
            total = total + far_buf[index]
        gath[pl.ds(lo, size)] = total
    else:
        ns_steps()
        gath[pl.ds(lo, size)] = acc[pl.ds(lo, size)]

    for j in reversed(range(count)):
        low, ways = groups[j]
        base, piece = spans[j]
        mine = group_index(low, ways)
        own = pl.ds(pl.multiple_of(base + mine * piece, 8), piece)
        copies = []
        for m in range(1, ways):
            other = (mine + m) % ways
            copy = pltpu.make_async_remote_copy(
                src_ref=gath.at[own],
                dst_ref=gath.at[own],
                send_sem=send_ag.at[4 * j + m],
                recv_sem=recv_ag.at[4 * j + mine],
                device_id=(member(low, ways, other), col),
                device_id_type=MESH,
            )
            copy.start()
            copies.append(copy)
        ns_steps()
        for copy in copies:
            copy.wait_send()
        for m in range(1, ways):
            source = (mine + m) % ways
            theirs = pl.ds(pl.multiple_of(base + source * piece, 8), piece)
            pltpu.make_async_remote_copy(
                src_ref=gath.at[theirs],
                dst_ref=gath.at[theirs],
                send_sem=send_ag.at[4 * j],
                recv_sem=recv_ag.at[4 * j + source],
                device_id=(member(low, ways, source), col),
                device_id_type=MESH,
            ).wait_recv()

    o_ref[...] = jnp.dot(
        gath[...], inv_ref[...], precision=lax.Precision.HIGHEST,
        preferred_element_type=jnp.float32,
    )


def layer_allreduce_solve(rows, gram, layer_count):
    nbits = layer_count.bit_length() - 1
    if nbits == 7:
        stages, far = (("bin", 0), ("bin", 1), ("bin", 2), ("quad", 5)), (3, 4)
    elif nbits == 5:
        stages, far = (("bin", 0), ("quad", 1)), (3, 4)
    else:
        stages, far = tuple(("bin", k) for k in range(nbits)), ()
    count = len(stages)
    far_ways = 1 << len(far)
    slots = 2 * count + 1
    ns_plan = [INV_STEPS // slots + (1 if r < INV_STEPS % slots else 0) for r in range(slots)]
    pieces = rows
    width = gram.shape[0]
    start = jnp.eye(width, dtype=jnp.float32) / jnp.sqrt(jnp.sum(gram * gram))
    buf_shapes = []
    size = rows.shape[0]
    for kind, _ in stages:
        ways = 2 if kind == "bin" else 4
        size //= ways
        buf_shapes.append(pltpu.VMEM((ways, size) + pieces.shape[1:], jnp.float32))
    solved, inverse = pl.pallas_call(
        functools.partial(layer_allreduce_kernel, stages, far, ns_plan),
        out_shape=(
            jax.ShapeDtypeStruct(pieces.shape, jnp.float32),
            jax.ShapeDtypeStruct((width, width), jnp.float32),
        ),
        in_specs=[pl.BlockSpec(memory_space=pltpu.VMEM)] * 3,
        out_specs=(pl.BlockSpec(memory_space=pltpu.VMEM),) * 2,
        scratch_shapes=[pltpu.VMEM(pieces.shape, jnp.float32)] * 2
        + buf_shapes
        + [pltpu.VMEM((far_ways, size) + pieces.shape[1:], jnp.float32)]
        + [pltpu.SemaphoreType.DMA((4 * count,))] * 4
        + [pltpu.SemaphoreType.DMA((far_ways,))] * 2,
        compiler_params=pltpu.CompilerParams(collective_id=0, has_side_effects=True),
    )(pieces, gram, start)
    return solved


def inl_gather_kernel(ways, b_ref, c_ref, o_ref, send1, recv1, send2, recv2):
    row = lax.axis_index("layer")
    col = lax.axis_index("inl")
    core = row % 2
    sibling = row + 1 - 2 * core
    half = b_ref.shape[1] // 2
    parts = (b_ref, c_ref)
    mine = pl.ds(pl.multiple_of(core * half, half), half)
    theirs = pl.ds(pl.multiple_of((1 - core) * half, half), half)
    barrier = pltpu.get_barrier_semaphore()
    for step in range(1, ways):
        pl.semaphore_signal(
            barrier, inc=1, device_id=(row, (col + step) % ways), device_id_type=MESH
        )
    pl.semaphore_signal(barrier, inc=1, device_id=(sibling, col), device_id_type=MESH)
    pl.semaphore_wait(barrier, ways)
    copies = []
    for step in range(1, ways):
        for part, x_ref in enumerate(parts):
            copy = pltpu.make_async_remote_copy(
                src_ref=x_ref.at[:, mine],
                dst_ref=o_ref.at[part, :, col, mine],
                send_sem=send1.at[2 * step + part],
                recv_sem=recv1.at[2 * col + part],
                device_id=(row, (col + step) % ways),
                device_id_type=MESH,
            )
            copy.start()
            copies.append(copy)
    for part, x_ref in enumerate(parts):
        o_ref[part, :, col] = x_ref[...]
    forwards = []
    for step in range(1, ways):
        source = (col + step) % ways
        for part in range(2):
            pltpu.make_async_remote_copy(
                src_ref=o_ref.at[part, :, source, mine],
                dst_ref=o_ref.at[part, :, source, mine],
                send_sem=send1.at[part],
                recv_sem=recv1.at[2 * source + part],
                device_id=(row, source),
                device_id_type=MESH,
            ).wait_recv()
        forward = pltpu.make_async_remote_copy(
            src_ref=o_ref.at[:, :, source, mine],
            dst_ref=o_ref.at[:, :, source, mine],
            send_sem=send2.at[step],
            recv_sem=recv2.at[source],
            device_id=(sibling, col),
            device_id_type=MESH,
        )
        forward.start()
        forwards.append(forward)
    for copy in copies:
        copy.wait_send()
    for forward in forwards:
        forward.wait_send()
    for step in range(1, ways):
        source = (col + step) % ways
        pltpu.make_async_remote_copy(
            src_ref=o_ref.at[:, :, source, theirs],
            dst_ref=o_ref.at[:, :, source, theirs],
            send_sem=send2.at[0],
            recv_sem=recv2.at[source],
            device_id=(sibling, col),
            device_id_type=MESH,
        ).wait_recv()


def inl_gather(factor_b, factor_c, ways):
    blocks, cells, rank_width = factor_b.shape
    return pl.pallas_call(
        functools.partial(inl_gather_kernel, ways),
        out_shape=jax.ShapeDtypeStruct((2, blocks, ways, cells, rank_width), factor_b.dtype),
        in_specs=[pl.BlockSpec(memory_space=pltpu.VMEM)] * 2,
        out_specs=pl.BlockSpec(memory_space=pltpu.VMEM),
        scratch_shapes=[pltpu.SemaphoreType.DMA((2 * ways,))] * 2
        + [pltpu.SemaphoreType.DMA((ways,))] * 2,
        compiler_params=pltpu.CompilerParams(collective_id=1, has_side_effects=True),
    )(factor_b, factor_c)


def mttkrp_kernel(coords_ref, filled_ref, blk_ref, b_ref, c_ref, o_ref):
    chunk = 32
    slot = pl.program_id(0)
    _, a_n, b_n, c_n = blk_ref.shape

    @pl.when(slot == 0)
    def _():
        o_ref[...] = jnp.zeros_like(o_ref)

    @pl.when(slot < filled_ref[0])
    def _():
        target = coords_ref[slot, 0]
        b_rows = b_ref[0].astype(jnp.float32)
        c_rows = c_ref[0]

        def body(i, carry):
            start = pl.multiple_of(i * chunk, chunk)
            x = blk_ref[0, pl.ds(start, chunk)].reshape(chunk * b_n, c_n)
            y = jnp.dot(x, c_rows, preferred_element_type=jnp.float32)
            z = y.reshape(chunk, b_n, -1) * b_rows[None]
            z = z.reshape(chunk, b_n // 8, 8, z.shape[-1]).sum(axis=1)
            o_ref[target, pl.ds(start, chunk)] += z.sum(axis=1)
            return carry

        lax.fori_loop(0, a_n // chunk, body, 0)


def mttkrp_rows(blocks, coords, filled, whole_b, whole_c):
    slot_count, a_n, b_n, c_n = blocks.shape
    side_blocks, _, rank_width = whole_b.shape
    grid_spec = pltpu.PrefetchScalarGridSpec(
        num_scalar_prefetch=2,
        grid=(slot_count,),
        in_specs=[
            pl.BlockSpec((1, a_n, b_n, c_n), lambda s, cr, fl: (s, 0, 0, 0)),
            pl.BlockSpec((1, b_n, rank_width), lambda s, cr, fl: (cr[s, 1], 0, 0)),
            pl.BlockSpec((1, c_n, rank_width), lambda s, cr, fl: (cr[s, 2], 0, 0)),
        ],
        out_specs=pl.BlockSpec((side_blocks, a_n, rank_width), lambda s, cr, fl: (0, 0, 0)),
    )
    return pl.pallas_call(
        mttkrp_kernel,
        grid_spec=grid_spec,
        out_shape=jax.ShapeDtypeStruct((side_blocks, a_n, rank_width), jnp.float32),
        cost_estimate=pl.CostEstimate(
            flops=2 * slot_count * a_n * b_n * c_n * rank_width,
            bytes_accessed=blocks.size * 2 + slot_count * (b_n + c_n) * rank_width * 2,
            transcendentals=0,
        ),
    )(coords, filled, blocks, whole_b, whole_c)


def on_device(layer_count, inl_count, blocks, coords, filled, factor_b, factor_c):
    slot_count = blocks.shape[0]
    own_cells = blocks.shape[1]
    side_blocks = factor_b.shape[0]
    rank_width = factor_b.shape[2]
    ways = inl_count
    gathered = inl_gather(factor_b, factor_c, ways)
    whole = gathered.reshape(2, side_blocks, ways * factor_b.shape[1], rank_width)
    whole_b, whole_c = whole[0], whole[1]
    gram_parts = (
        self_gram(whole_b.reshape(-1, rank_width)),
        self_gram(whole_c.reshape(-1, rank_width)),
    )
    buffer = mttkrp_rows(blocks, coords, filled, whole_b, whole_c)
    row_totals = buffer.reshape(side_blocks * own_cells, rank_width)
    solved = layer_allreduce_solve(row_totals, gram_parts[0] * gram_parts[1], layer_count)
    return solved.reshape(side_blocks, own_cells, rank_width)


def solution(mesh):
    in_specs = (
        P("layer", "inl", None, None),
        P("layer", None),
        P("layer"),
        P(None, "inl", None),
        P(None, "inl", None),
    )
    out_specs = P(None, "inl", None)
    return jax.shard_map(
        functools.partial(on_device, mesh.shape["layer"], mesh.shape["inl"]),
        mesh=mesh,
        in_specs=in_specs,
        out_specs=out_specs,
        check_vma=False,
    )
```

```python
import functools

import jax
import jax.numpy as jnp
from jax import lax
from jax.experimental import pallas as pl
from jax.experimental.pallas import tpu as pltpu
from jax.sharding import PartitionSpec as P

INV_STEPS = 24
MESH = pl.DeviceIdType.MESH


def layer_allreduce_kernel(stages, far, ns_plan, x_ref, g_ref, x0_ref, o_ref, inv_ref, acc, gath, *rest):
    count = len(stages)
    bufs = rest[:count]
    far_buf = rest[count]
    send_rs, recv_rs, send_ag, recv_ag, far_send, far_recv = rest[count + 1:]
    me = lax.axis_index("layer")
    col = lax.axis_index("inl")
    far_ways = far_buf.shape[0]

    def group_index(low, ways):
        return (me // (1 << low)) % ways

    def member(low, ways, other):
        return me + (other - group_index(low, ways)) * (1 << low)

    groups = [(low, 2 if kind == "bin" else 4) for kind, low in stages]
    if far:
        groups.append((far[0], far_ways))
    barrier = pltpu.get_barrier_semaphore()
    signals = 0
    for low, ways in groups:
        mine = group_index(low, ways)
        for m in range(1, ways):
            pl.semaphore_signal(
                barrier, inc=1, device_id=(member(low, ways, (mine + m) % ways), col),
                device_id_type=MESH,
            )
            signals += 1
    pl.semaphore_wait(barrier, signals)

    width = g_ref.shape[0]
    rows = lax.broadcasted_iota(jnp.int32, (width, width), 0)
    cols = lax.broadcasted_iota(jnp.int32, (width, width), 1)
    two_ident = jnp.where(rows == cols, 2.0, 0.0).astype(jnp.float32)
    inv_ref[...] = x0_ref[...]
    plan = iter(ns_plan)

    def ns_steps():
        for _ in range(next(plan)):
            current = inv_ref[...]
            product = jnp.dot(
                g_ref[...], current, precision=lax.Precision.HIGHEST,
                preferred_element_type=jnp.float32,
            )
            inv_ref[...] = jnp.dot(
                current, two_ident - product, precision=lax.Precision.HIGHEST,
                preferred_element_type=jnp.float32,
            )

    acc[...] = x_ref[...]
    lo = 0
    size = acc.shape[0]
    spans = []
    for j, (low, ways) in enumerate(groups[:count]):
        piece = size // ways
        mine = group_index(low, ways)
        copies = []
        for m in range(1, ways):
            other = (mine + m) % ways
            copy = pltpu.make_async_remote_copy(
                src_ref=acc.at[pl.ds(pl.multiple_of(lo + other * piece, 8), piece)],
                dst_ref=bufs[j].at[mine],
                send_sem=send_rs.at[4 * j + m],
                recv_sem=recv_rs.at[4 * j + mine],
                device_id=(member(low, ways, other), col),
                device_id_type=MESH,
            )
            copy.start()
            copies.append(copy)
        keep_lo = pl.multiple_of(lo + mine * piece, 8)
        bufs[j][mine] = acc[pl.ds(keep_lo, piece)]
        ns_steps()
        for copy in copies:
            copy.wait_send()
        for m in range(1, ways):
            source = (mine + m) % ways
            pltpu.make_async_remote_copy(
                src_ref=bufs[j].at[source],
                dst_ref=bufs[j].at[source],
                send_sem=send_rs.at[4 * j],
                recv_sem=recv_rs.at[4 * j + source],
                device_id=(member(low, ways, source), col),
                device_id_type=MESH,
            ).wait_recv()
        total = bufs[j][0]
        for index in range(1, ways):
            total = total + bufs[j][index]
        acc[pl.ds(keep_lo, piece)] = total
        spans.append((lo, piece))
        lo = keep_lo
        size = piece

    if far:
        far_me = group_index(far[0], far_ways)
        far_buf[far_me] = acc[pl.ds(lo, size)]
        copies = []
        for m in range(1, far_ways):
            copy = pltpu.make_async_remote_copy(
                src_ref=acc.at[pl.ds(lo, size)],
                dst_ref=far_buf.at[far_me],
                send_sem=far_send.at[m],
                recv_sem=far_recv.at[far_me],
                device_id=(member(far[0], far_ways, (far_me + m) % far_ways), col),
                device_id_type=MESH,
            )
            copy.start()
            copies.append(copy)
        ns_steps()
        for copy in copies:
            copy.wait_send()
        for m in range(1, far_ways):
            source = (far_me + m) % far_ways
            pltpu.make_async_remote_copy(
                src_ref=far_buf.at[source],
                dst_ref=far_buf.at[source],
                send_sem=far_send.at[0],
                recv_sem=far_recv.at[source],
                device_id=(member(far[0], far_ways, source), col),
                device_id_type=MESH,
            ).wait_recv()
        total = far_buf[0]
        for index in range(1, far_ways):
            total = total + far_buf[index]
        gath[pl.ds(lo, size)] = total
    else:
        ns_steps()
        gath[pl.ds(lo, size)] = acc[pl.ds(lo, size)]

    for j in reversed(range(count)):
        low, ways = groups[j]
        base, piece = spans[j]
        mine = group_index(low, ways)
        own = pl.ds(pl.multiple_of(base + mine * piece, 8), piece)
        copies = []
        for m in range(1, ways):
            other = (mine + m) % ways
            copy = pltpu.make_async_remote_copy(
                src_ref=gath.at[own],
                dst_ref=gath.at[own],
                send_sem=send_ag.at[4 * j + m],
                recv_sem=recv_ag.at[4 * j + mine],
                device_id=(member(low, ways, other), col),
                device_id_type=MESH,
            )
            copy.start()
            copies.append(copy)
        ns_steps()
        for copy in copies:
            copy.wait_send()
        for m in range(1, ways):
            source = (mine + m) % ways
            theirs = pl.ds(pl.multiple_of(base + source * piece, 8), piece)
            pltpu.make_async_remote_copy(
                src_ref=gath.at[theirs],
                dst_ref=gath.at[theirs],
                send_sem=send_ag.at[4 * j],
                recv_sem=recv_ag.at[4 * j + source],
                device_id=(member(low, ways, source), col),
                device_id_type=MESH,
            ).wait_recv()

    o_ref[...] = jnp.dot(
        gath[...], inv_ref[...], precision=lax.Precision.HIGHEST,
        preferred_element_type=jnp.float32,
    )


def layer_allreduce_solve(rows, gram, layer_count):
    nbits = layer_count.bit_length() - 1
    if nbits == 7:
        stages, far = (("bin", 0), ("bin", 1), ("bin", 2), ("quad", 5)), (3, 4)
    elif nbits == 5:
        stages, far = (("bin", 0), ("quad", 1)), (3, 4)
    else:
        stages, far = tuple(("bin", k) for k in range(nbits)), ()
    count = len(stages)
    far_ways = 1 << len(far)
    slots = 2 * count + 1
    ns_plan = [INV_STEPS // slots + (1 if r < INV_STEPS % slots else 0) for r in range(slots)]
    pieces = rows
    width = gram.shape[0]
    start = jnp.eye(width, dtype=jnp.float32) / jnp.sqrt(jnp.sum(gram * gram))
    buf_shapes = []
    size = rows.shape[0]
    for kind, _ in stages:
        ways = 2 if kind == "bin" else 4
        size //= ways
        buf_shapes.append(pltpu.VMEM((ways, size) + pieces.shape[1:], jnp.float32))
    solved, inverse = pl.pallas_call(
        functools.partial(layer_allreduce_kernel, stages, far, ns_plan),
        out_shape=(
            jax.ShapeDtypeStruct(pieces.shape, jnp.float32),
            jax.ShapeDtypeStruct((width, width), jnp.float32),
        ),
        in_specs=[pl.BlockSpec(memory_space=pltpu.VMEM)] * 3,
        out_specs=(pl.BlockSpec(memory_space=pltpu.VMEM),) * 2,
        scratch_shapes=[pltpu.VMEM(pieces.shape, jnp.float32)] * 2
        + buf_shapes
        + [pltpu.VMEM((far_ways, size) + pieces.shape[1:], jnp.float32)]
        + [pltpu.SemaphoreType.DMA((4 * count,))] * 4
        + [pltpu.SemaphoreType.DMA((far_ways,))] * 2,
        compiler_params=pltpu.CompilerParams(collective_id=0, has_side_effects=True),
    )(pieces, gram, start)
    return solved


def inl_gather_kernel(ways, b_ref, c_ref, o_ref, send1, recv1, send2, recv2):
    row = lax.axis_index("layer")
    col = lax.axis_index("inl")
    core = row % 2
    sibling = row + 1 - 2 * core
    half = b_ref.shape[1] // 2
    parts = (b_ref, c_ref)
    mine = pl.ds(pl.multiple_of(core * half, half), half)
    theirs = pl.ds(pl.multiple_of((1 - core) * half, half), half)
    barrier = pltpu.get_barrier_semaphore()
    for step in range(1, ways):
        pl.semaphore_signal(
            barrier, inc=1, device_id=(row, (col + step) % ways), device_id_type=MESH
        )
    pl.semaphore_signal(barrier, inc=1, device_id=(sibling, col), device_id_type=MESH)
    pl.semaphore_wait(barrier, ways)
    copies = []
    for step in range(1, ways):
        for part, x_ref in enumerate(parts):
            copy = pltpu.make_async_remote_copy(
                src_ref=x_ref.at[:, mine],
                dst_ref=o_ref.at[part, :, col, mine],
                send_sem=send1.at[2 * step + part],
                recv_sem=recv1.at[2 * col + part],
                device_id=(row, (col + step) % ways),
                device_id_type=MESH,
            )
            copy.start()
            copies.append(copy)
    for part, x_ref in enumerate(parts):
        o_ref[part, :, col] = x_ref[...]
    forwards = []
    for step in range(1, ways):
        source = (col + step) % ways
        for part in range(2):
            pltpu.make_async_remote_copy(
                src_ref=o_ref.at[part, :, source, mine],
                dst_ref=o_ref.at[part, :, source, mine],
                send_sem=send1.at[part],
                recv_sem=recv1.at[2 * source + part],
                device_id=(row, source),
                device_id_type=MESH,
            ).wait_recv()
        forward = pltpu.make_async_remote_copy(
            src_ref=o_ref.at[:, :, source, mine],
            dst_ref=o_ref.at[:, :, source, mine],
            send_sem=send2.at[step],
            recv_sem=recv2.at[source],
            device_id=(sibling, col),
            device_id_type=MESH,
        )
        forward.start()
        forwards.append(forward)
    for copy in copies:
        copy.wait_send()
    for forward in forwards:
        forward.wait_send()
    for step in range(1, ways):
        source = (col + step) % ways
        pltpu.make_async_remote_copy(
            src_ref=o_ref.at[:, :, source, theirs],
            dst_ref=o_ref.at[:, :, source, theirs],
            send_sem=send2.at[0],
            recv_sem=recv2.at[source],
            device_id=(sibling, col),
            device_id_type=MESH,
        ).wait_recv()


def inl_gather(factor_b, factor_c, ways):
    blocks, cells, rank_width = factor_b.shape
    return pl.pallas_call(
        functools.partial(inl_gather_kernel, ways),
        out_shape=jax.ShapeDtypeStruct((2, blocks, ways, cells, rank_width), factor_b.dtype),
        in_specs=[pl.BlockSpec(memory_space=pltpu.VMEM)] * 2,
        out_specs=pl.BlockSpec(memory_space=pltpu.VMEM),
        scratch_shapes=[pltpu.SemaphoreType.DMA((2 * ways,))] * 2
        + [pltpu.SemaphoreType.DMA((ways,))] * 2,
        compiler_params=pltpu.CompilerParams(collective_id=1, has_side_effects=True),
    )(factor_b, factor_c)


def mttkrp_kernel(coords_ref, filled_ref, blk_ref, b_ref, c_ref, o_ref):
    chunk = 32
    slot = pl.program_id(0)
    _, a_n, b_n, c_n = blk_ref.shape

    @pl.when(slot == 0)
    def _():
        o_ref[...] = jnp.zeros_like(o_ref)

    @pl.when(slot < filled_ref[0])
    def _():
        target = coords_ref[slot, 0]
        b_rows = b_ref[0].astype(jnp.float32)
        c_rows = c_ref[0]

        def body(i, carry):
            start = pl.multiple_of(i * chunk, chunk)
            x = blk_ref[0, pl.ds(start, chunk)].reshape(chunk * b_n, c_n)
            y = jnp.dot(x, c_rows, preferred_element_type=jnp.float32)
            z = y.reshape(chunk, b_n, -1) * b_rows[None]
            z = z.reshape(chunk, b_n // 8, 8, z.shape[-1]).sum(axis=1)
            o_ref[target, pl.ds(start, chunk)] += z.sum(axis=1)
            return carry

        lax.fori_loop(0, a_n // chunk, body, 0)


def mttkrp_rows(blocks, coords, filled, whole):
    slot_count, a_n, b_n, c_n = blocks.shape
    _, side_blocks, _, rank_width = whole.shape
    grid_spec = pltpu.PrefetchScalarGridSpec(
        num_scalar_prefetch=2,
        grid=(slot_count,),
        in_specs=[
            pl.BlockSpec((1, a_n, b_n, c_n), lambda s, cr, fl: (s, 0, 0, 0)),
            pl.BlockSpec((None, 1, b_n, rank_width), lambda s, cr, fl: (0, cr[s, 1], 0, 0)),
            pl.BlockSpec((None, 1, c_n, rank_width), lambda s, cr, fl: (1, cr[s, 2], 0, 0)),
        ],
        out_specs=pl.BlockSpec((side_blocks, a_n, rank_width), lambda s, cr, fl: (0, 0, 0)),
    )
    return pl.pallas_call(
        mttkrp_kernel,
        grid_spec=grid_spec,
        out_shape=jax.ShapeDtypeStruct((side_blocks, a_n, rank_width), jnp.float32),
        cost_estimate=pl.CostEstimate(
            flops=2 * slot_count * a_n * b_n * c_n * rank_width,
            bytes_accessed=blocks.size * 2 + slot_count * (b_n + c_n) * rank_width * 2,
            transcendentals=0,
        ),
    )(coords, filled, blocks, whole, whole)


def on_device(layer_count, inl_count, blocks, coords, filled, factor_b, factor_c):
    slot_count = blocks.shape[0]
    own_cells = blocks.shape[1]
    side_blocks = factor_b.shape[0]
    rank_width = factor_b.shape[2]
    ways = inl_count
    gathered = inl_gather(factor_b, factor_c, ways)
    whole = gathered.reshape(2, side_blocks, ways * factor_b.shape[1], rank_width)
    flat = whole.reshape(2, -1, rank_width)
    gram_parts = lax.dot_general(
        flat, flat, (((1,), (1,)), ((0,), (0,))), preferred_element_type=jnp.float32
    )
    buffer = mttkrp_rows(blocks, coords, filled, whole)
    row_totals = buffer.reshape(side_blocks * own_cells, rank_width)
    solved = layer_allreduce_solve(row_totals, gram_parts[0] * gram_parts[1], layer_count)
    return solved.reshape(side_blocks, own_cells, rank_width)


def solution(mesh):
    in_specs = (
        P("layer", "inl", None, None),
        P("layer", None),
        P("layer"),
        P(None, "inl", None),
        P(None, "inl", None),
    )
    out_specs = P(None, "inl", None)
    return jax.shard_map(
        functools.partial(on_device, mesh.shape["layer"], mesh.shape["inl"]),
        mesh=mesh,
        in_specs=in_specs,
        out_specs=out_specs,
        check_vma=False,
    )
```

```python
import functools

import jax
import jax.numpy as jnp
from jax import lax
from jax.experimental import pallas as pl
from jax.experimental.pallas import tpu as pltpu
from jax.sharding import PartitionSpec as P

INV_STEPS = 24
MESH = pl.DeviceIdType.MESH


def layer_allreduce_kernel(stages, far, ns_plan, x_ref, grams_ref, o_ref, inv_ref, acc, gath, g_ref, *rest):
    count = len(stages)
    bufs = rest[:count]
    far_buf = rest[count]
    send_rs, recv_rs, send_ag, recv_ag, far_send, far_recv = rest[count + 1:]
    me = lax.axis_index("layer")
    col = lax.axis_index("inl")
    far_ways = far_buf.shape[0]

    def group_index(low, ways):
        return (me // (1 << low)) % ways

    def member(low, ways, other):
        return me + (other - group_index(low, ways)) * (1 << low)

    groups = [(low, 2 if kind == "bin" else 4) for kind, low in stages]
    if far:
        groups.append((far[0], far_ways))
    barrier = pltpu.get_barrier_semaphore()
    signals = 0
    for low, ways in groups:
        mine = group_index(low, ways)
        for m in range(1, ways):
            pl.semaphore_signal(
                barrier, inc=1, device_id=(member(low, ways, (mine + m) % ways), col),
                device_id_type=MESH,
            )
            signals += 1
    pl.semaphore_wait(barrier, signals)

    width = g_ref.shape[0]
    rows = lax.broadcasted_iota(jnp.int32, (width, width), 0)
    cols = lax.broadcasted_iota(jnp.int32, (width, width), 1)
    two_ident = jnp.where(rows == cols, 2.0, 0.0).astype(jnp.float32)
    plan = iter(ns_plan)

    def ns_start():
        gram = grams_ref[0] * grams_ref[1]
        g_ref[...] = gram
        norm_sq = jnp.sum(jnp.sum(gram * gram, axis=1, keepdims=True), axis=0, keepdims=True)
        inv_ref[...] = (0.5 * two_ident) / jnp.sqrt(norm_sq)

    def ns_steps():
        for _ in range(next(plan)):
            current = inv_ref[...]
            product = jnp.dot(
                g_ref[...], current, precision=lax.Precision.HIGHEST,
                preferred_element_type=jnp.float32,
            )
            inv_ref[...] = jnp.dot(
                current, two_ident - product, precision=lax.Precision.HIGHEST,
                preferred_element_type=jnp.float32,
            )

    acc[...] = x_ref[...]
    lo = 0
    size = acc.shape[0]
    spans = []
    for j, (low, ways) in enumerate(groups[:count]):
        piece = size // ways
        mine = group_index(low, ways)
        copies = []
        for m in range(1, ways):
            other = (mine + m) % ways
            copy = pltpu.make_async_remote_copy(
                src_ref=acc.at[pl.ds(pl.multiple_of(lo + other * piece, 8), piece)],
                dst_ref=bufs[j].at[mine],
                send_sem=send_rs.at[4 * j + m],
                recv_sem=recv_rs.at[4 * j + mine],
                device_id=(member(low, ways, other), col),
                device_id_type=MESH,
            )
            copy.start()
            copies.append(copy)
        keep_lo = pl.multiple_of(lo + mine * piece, 8)
        bufs[j][mine] = acc[pl.ds(keep_lo, piece)]
        if j == 0:
            ns_start()
        ns_steps()
        for copy in copies:
            copy.wait_send()
        for m in range(1, ways):
            source = (mine + m) % ways
            pltpu.make_async_remote_copy(
                src_ref=bufs[j].at[source],
                dst_ref=bufs[j].at[source],
                send_sem=send_rs.at[4 * j],
                recv_sem=recv_rs.at[4 * j + source],
                device_id=(member(low, ways, source), col),
                device_id_type=MESH,
            ).wait_recv()
        total = bufs[j][0]
        for index in range(1, ways):
            total = total + bufs[j][index]
        acc[pl.ds(keep_lo, piece)] = total
        spans.append((lo, piece))
        lo = keep_lo
        size = piece

    if far:
        far_me = group_index(far[0], far_ways)
        far_buf[far_me] = acc[pl.ds(lo, size)]
        copies = []
        for m in range(1, far_ways):
            copy = pltpu.make_async_remote_copy(
                src_ref=acc.at[pl.ds(lo, size)],
                dst_ref=far_buf.at[far_me],
                send_sem=far_send.at[m],
                recv_sem=far_recv.at[far_me],
                device_id=(member(far[0], far_ways, (far_me + m) % far_ways), col),
                device_id_type=MESH,
            )
            copy.start()
            copies.append(copy)
        ns_steps()
        for copy in copies:
            copy.wait_send()
        for m in range(1, far_ways):
            source = (far_me + m) % far_ways
            pltpu.make_async_remote_copy(
                src_ref=far_buf.at[source],
                dst_ref=far_buf.at[source],
                send_sem=far_send.at[0],
                recv_sem=far_recv.at[source],
                device_id=(member(far[0], far_ways, source), col),
                device_id_type=MESH,
            ).wait_recv()
        total = far_buf[0]
        for index in range(1, far_ways):
            total = total + far_buf[index]
        gath[pl.ds(lo, size)] = total
    else:
        ns_steps()
        gath[pl.ds(lo, size)] = acc[pl.ds(lo, size)]

    for j in reversed(range(count)):
        low, ways = groups[j]
        base, piece = spans[j]
        mine = group_index(low, ways)
        own = pl.ds(pl.multiple_of(base + mine * piece, 8), piece)
        copies = []
        for m in range(1, ways):
            other = (mine + m) % ways
            copy = pltpu.make_async_remote_copy(
                src_ref=gath.at[own],
                dst_ref=gath.at[own],
                send_sem=send_ag.at[4 * j + m],
                recv_sem=recv_ag.at[4 * j + mine],
                device_id=(member(low, ways, other), col),
                device_id_type=MESH,
            )
            copy.start()
            copies.append(copy)
        ns_steps()
        for copy in copies:
            copy.wait_send()
        for m in range(1, ways):
            source = (mine + m) % ways
            theirs = pl.ds(pl.multiple_of(base + source * piece, 8), piece)
            pltpu.make_async_remote_copy(
                src_ref=gath.at[theirs],
                dst_ref=gath.at[theirs],
                send_sem=send_ag.at[4 * j],
                recv_sem=recv_ag.at[4 * j + source],
                device_id=(member(low, ways, source), col),
                device_id_type=MESH,
            ).wait_recv()

    o_ref[...] = jnp.dot(
        gath[...], inv_ref[...], precision=lax.Precision.HIGHEST,
        preferred_element_type=jnp.float32,
    )


def layer_allreduce_solve(rows, grams, layer_count):
    nbits = layer_count.bit_length() - 1
    if nbits == 7:
        stages, far = (("bin", 0), ("bin", 1), ("bin", 2), ("quad", 5)), (3, 4)
    elif nbits == 5:
        stages, far = (("bin", 0), ("quad", 1)), (3, 4)
    else:
        stages, far = tuple(("bin", k) for k in range(nbits)), ()
    count = len(stages)
    far_ways = 1 << len(far)
    slots = 2 * count + 1
    ns_plan = [INV_STEPS // slots + (1 if r < INV_STEPS % slots else 0) for r in range(slots)]
    pieces = rows
    width = grams.shape[-1]
    buf_shapes = []
    size = rows.shape[0]
    for kind, _ in stages:
        ways = 2 if kind == "bin" else 4
        size //= ways
        buf_shapes.append(pltpu.VMEM((ways, size) + pieces.shape[1:], jnp.float32))
    solved, inverse = pl.pallas_call(
        functools.partial(layer_allreduce_kernel, stages, far, ns_plan),
        out_shape=(
            jax.ShapeDtypeStruct(pieces.shape, jnp.float32),
            jax.ShapeDtypeStruct((width, width), jnp.float32),
        ),
        in_specs=[pl.BlockSpec(memory_space=pltpu.VMEM)] * 2,
        out_specs=(pl.BlockSpec(memory_space=pltpu.VMEM),) * 2,
        scratch_shapes=[pltpu.VMEM(pieces.shape, jnp.float32)] * 2
        + [pltpu.VMEM((width, width), jnp.float32)]
        + buf_shapes
        + [pltpu.VMEM((far_ways, size) + pieces.shape[1:], jnp.float32)]
        + [pltpu.SemaphoreType.DMA((4 * count,))] * 4
        + [pltpu.SemaphoreType.DMA((far_ways,))] * 2,
        compiler_params=pltpu.CompilerParams(collective_id=0, has_side_effects=True),
    )(pieces, grams)
    return solved


def inl_gather_kernel(ways, b_ref, c_ref, o_ref, send1, recv1, send2, recv2):
    row = lax.axis_index("layer")
    col = lax.axis_index("inl")
    core = row % 2
    sibling = row + 1 - 2 * core
    half = b_ref.shape[1] // 2
    parts = (b_ref, c_ref)
    mine = pl.ds(pl.multiple_of(core * half, half), half)
    theirs = pl.ds(pl.multiple_of((1 - core) * half, half), half)
    barrier = pltpu.get_barrier_semaphore()
    for step in range(1, ways):
        pl.semaphore_signal(
            barrier, inc=1, device_id=(row, (col + step) % ways), device_id_type=MESH
        )
    pl.semaphore_signal(barrier, inc=1, device_id=(sibling, col), device_id_type=MESH)
    pl.semaphore_wait(barrier, ways)
    copies = []
    for step in range(1, ways):
        for part, x_ref in enumerate(parts):
            copy = pltpu.make_async_remote_copy(
                src_ref=x_ref.at[:, mine],
                dst_ref=o_ref.at[part, :, col, mine],
                send_sem=send1.at[2 * step + part],
                recv_sem=recv1.at[2 * col + part],
                device_id=(row, (col + step) % ways),
                device_id_type=MESH,
            )
            copy.start()
            copies.append(copy)
    for part, x_ref in enumerate(parts):
        o_ref[part, :, col] = x_ref[...]
    forwards = []
    for step in range(1, ways):
        source = (col + step) % ways
        for part in range(2):
            pltpu.make_async_remote_copy(
                src_ref=o_ref.at[part, :, source, mine],
                dst_ref=o_ref.at[part, :, source, mine],
                send_sem=send1.at[part],
                recv_sem=recv1.at[2 * source + part],
                device_id=(row, source),
                device_id_type=MESH,
            ).wait_recv()
        forward = pltpu.make_async_remote_copy(
            src_ref=o_ref.at[:, :, source, mine],
            dst_ref=o_ref.at[:, :, source, mine],
            send_sem=send2.at[step],
            recv_sem=recv2.at[source],
            device_id=(sibling, col),
            device_id_type=MESH,
        )
        forward.start()
        forwards.append(forward)
    for copy in copies:
        copy.wait_send()
    for forward in forwards:
        forward.wait_send()
    for step in range(1, ways):
        source = (col + step) % ways
        pltpu.make_async_remote_copy(
            src_ref=o_ref.at[:, :, source, theirs],
            dst_ref=o_ref.at[:, :, source, theirs],
            send_sem=send2.at[0],
            recv_sem=recv2.at[source],
            device_id=(sibling, col),
            device_id_type=MESH,
        ).wait_recv()


def inl_gather(factor_b, factor_c, ways):
    blocks, cells, rank_width = factor_b.shape
    return pl.pallas_call(
        functools.partial(inl_gather_kernel, ways),
        out_shape=jax.ShapeDtypeStruct((2, blocks, ways, cells, rank_width), factor_b.dtype),
        in_specs=[pl.BlockSpec(memory_space=pltpu.VMEM)] * 2,
        out_specs=pl.BlockSpec(memory_space=pltpu.VMEM),
        scratch_shapes=[pltpu.SemaphoreType.DMA((2 * ways,))] * 2
        + [pltpu.SemaphoreType.DMA((ways,))] * 2,
        compiler_params=pltpu.CompilerParams(collective_id=1, has_side_effects=True),
    )(factor_b, factor_c)


def mttkrp_kernel(coords_ref, filled_ref, blk_ref, b_ref, c_ref, o_ref):
    chunk = 32
    slot = pl.program_id(0)
    _, a_n, b_n, c_n = blk_ref.shape

    @pl.when(slot == 0)
    def _():
        o_ref[...] = jnp.zeros_like(o_ref)

    @pl.when(slot < filled_ref[0])
    def _():
        target = coords_ref[slot, 0]
        b_rows = b_ref[0].astype(jnp.float32)
        c_rows = c_ref[0]

        def body(i, carry):
            start = pl.multiple_of(i * chunk, chunk)
            x = blk_ref[0, pl.ds(start, chunk)].reshape(chunk * b_n, c_n)
            y = jnp.dot(x, c_rows, preferred_element_type=jnp.float32)
            z = y.reshape(chunk, b_n, -1) * b_rows[None]
            z = z.reshape(chunk, b_n // 8, 8, z.shape[-1]).sum(axis=1)
            o_ref[target, pl.ds(start, chunk)] += z.sum(axis=1)
            return carry

        lax.fori_loop(0, a_n // chunk, body, 0)


def mttkrp_rows(blocks, coords, filled, whole):
    slot_count, a_n, b_n, c_n = blocks.shape
    _, side_blocks, _, rank_width = whole.shape
    grid_spec = pltpu.PrefetchScalarGridSpec(
        num_scalar_prefetch=2,
        grid=(slot_count,),
        in_specs=[
            pl.BlockSpec((1, a_n, b_n, c_n), lambda s, cr, fl: (s, 0, 0, 0)),
            pl.BlockSpec((None, 1, b_n, rank_width), lambda s, cr, fl: (0, cr[s, 1], 0, 0)),
            pl.BlockSpec((None, 1, c_n, rank_width), lambda s, cr, fl: (1, cr[s, 2], 0, 0)),
        ],
        out_specs=pl.BlockSpec((side_blocks, a_n, rank_width), lambda s, cr, fl: (0, 0, 0)),
    )
    return pl.pallas_call(
        mttkrp_kernel,
        grid_spec=grid_spec,
        out_shape=jax.ShapeDtypeStruct((side_blocks, a_n, rank_width), jnp.float32),
        cost_estimate=pl.CostEstimate(
            flops=2 * slot_count * a_n * b_n * c_n * rank_width,
            bytes_accessed=blocks.size * 2 + slot_count * (b_n + c_n) * rank_width * 2,
            transcendentals=0,
        ),
    )(coords, filled, blocks, whole, whole)


def on_device(layer_count, inl_count, blocks, coords, filled, factor_b, factor_c):
    slot_count = blocks.shape[0]
    own_cells = blocks.shape[1]
    side_blocks = factor_b.shape[0]
    rank_width = factor_b.shape[2]
    ways = inl_count
    gathered = inl_gather(factor_b, factor_c, ways)
    whole = gathered.reshape(2, side_blocks, ways * factor_b.shape[1], rank_width)
    flat = whole.reshape(2, -1, rank_width)
    gram_parts = lax.dot_general(
        flat, flat, (((1,), (1,)), ((0,), (0,))), preferred_element_type=jnp.float32
    )
    buffer = mttkrp_rows(blocks, coords, filled, whole)
    row_totals = buffer.reshape(side_blocks * own_cells, rank_width)
    solved = layer_allreduce_solve(row_totals, gram_parts, layer_count)
    return solved.reshape(side_blocks, own_cells, rank_width)


def solution(mesh):
    in_specs = (
        P("layer", "inl", None, None),
        P("layer", None),
        P("layer"),
        P(None, "inl", None),
        P(None, "inl", None),
    )
    out_specs = P(None, "inl", None)
    return jax.shard_map(
        functools.partial(on_device, mesh.shape["layer"], mesh.shape["inl"]),
        mesh=mesh,
        in_specs=in_specs,
        out_specs=out_specs,
        check_vma=False,
    )
```

```python
import functools

import jax
import jax.numpy as jnp
from jax import lax
from jax.experimental import pallas as pl
from jax.experimental.pallas import tpu as pltpu
from jax.sharding import PartitionSpec as P

INV_STEPS = 24
MESH = pl.DeviceIdType.MESH


def layer_allreduce_kernel(stages, far, ns_plan, x_ref, grams_ref, o_ref, inv_ref, acc, gath, g_ref, *rest):
    count = len(stages[0])
    bufs = rest[:count]
    far_buf = rest[count]
    send_rs, recv_rs, send_ag, recv_ag, far_send, far_recv = rest[count + 1:]
    me = lax.axis_index("layer")
    col = lax.axis_index("inl")
    far_ways = far_buf.shape[0]

    core = me % 2

    def group_index(step, ways):
        return (me // step) % ways

    def member(step, ways, other):
        return me + (other - group_index(step, ways)) * step

    groups = [
        (core * (1 << low1) + (1 - core) * (1 << low0), 2 if kind == "bin" else 4)
        for (kind, low0), (_, low1) in zip(stages[0], stages[1])
    ]
    far_step = 1 << far[0] if far else 1
    if far:
        groups.append((far_step, far_ways))
    barrier = pltpu.get_barrier_semaphore()
    signals = 0
    for low, ways in groups:
        mine = group_index(low, ways)
        for m in range(1, ways):
            pl.semaphore_signal(
                barrier, inc=1, device_id=(member(low, ways, (mine + m) % ways), col),
                device_id_type=MESH,
            )
            signals += 1
    pl.semaphore_wait(barrier, signals)

    width = g_ref.shape[0]
    rows = lax.broadcasted_iota(jnp.int32, (width, width), 0)
    cols = lax.broadcasted_iota(jnp.int32, (width, width), 1)
    two_ident = jnp.where(rows == cols, 2.0, 0.0).astype(jnp.float32)
    plan = iter(ns_plan)

    def ns_start():
        gram = grams_ref[0] * grams_ref[1]
        g_ref[...] = gram
        norm_sq = jnp.sum(jnp.sum(gram * gram, axis=1, keepdims=True), axis=0, keepdims=True)
        inv_ref[...] = (0.5 * two_ident) / jnp.sqrt(norm_sq)

    def ns_steps():
        for _ in range(next(plan)):
            current = inv_ref[...]
            product = jnp.dot(
                g_ref[...], current, precision=lax.Precision.HIGHEST,
                preferred_element_type=jnp.float32,
            )
            inv_ref[...] = jnp.dot(
                current, two_ident - product, precision=lax.Precision.HIGHEST,
                preferred_element_type=jnp.float32,
            )

    acc[...] = x_ref[...]
    lo = 0
    size = acc.shape[0]
    spans = []
    for j, (low, ways) in enumerate(groups[:count]):
        piece = size // ways
        mine = group_index(low, ways)
        copies = []
        for m in range(1, ways):
            other = (mine + m) % ways
            copy = pltpu.make_async_remote_copy(
                src_ref=acc.at[pl.ds(pl.multiple_of(lo + other * piece, 8), piece)],
                dst_ref=bufs[j].at[mine],
                send_sem=send_rs.at[4 * j + m],
                recv_sem=recv_rs.at[4 * j + mine],
                device_id=(member(low, ways, other), col),
                device_id_type=MESH,
            )
            copy.start()
            copies.append(copy)
        keep_lo = pl.multiple_of(lo + mine * piece, 8)
        bufs[j][mine] = acc[pl.ds(keep_lo, piece)]
        if j == 0:
            ns_start()
        ns_steps()
        for copy in copies:
            copy.wait_send()
        for m in range(1, ways):
            source = (mine + m) % ways
            pltpu.make_async_remote_copy(
                src_ref=bufs[j].at[source],
                dst_ref=bufs[j].at[source],
                send_sem=send_rs.at[4 * j],
                recv_sem=recv_rs.at[4 * j + source],
                device_id=(member(low, ways, source), col),
                device_id_type=MESH,
            ).wait_recv()
        total = bufs[j][0]
        for index in range(1, ways):
            total = total + bufs[j][index]
        acc[pl.ds(keep_lo, piece)] = total
        spans.append((lo, piece))
        lo = keep_lo
        size = piece

    if far:
        far_me = group_index(far_step, far_ways)
        far_buf[far_me] = acc[pl.ds(lo, size)]
        copies = []
        for m in range(1, far_ways):
            copy = pltpu.make_async_remote_copy(
                src_ref=acc.at[pl.ds(lo, size)],
                dst_ref=far_buf.at[far_me],
                send_sem=far_send.at[m],
                recv_sem=far_recv.at[far_me],
                device_id=(member(far_step, far_ways, (far_me + m) % far_ways), col),
                device_id_type=MESH,
            )
            copy.start()
            copies.append(copy)
        ns_steps()
        for copy in copies:
            copy.wait_send()
        for m in range(1, far_ways):
            source = (far_me + m) % far_ways
            pltpu.make_async_remote_copy(
                src_ref=far_buf.at[source],
                dst_ref=far_buf.at[source],
                send_sem=far_send.at[0],
                recv_sem=far_recv.at[source],
                device_id=(member(far_step, far_ways, source), col),
                device_id_type=MESH,
            ).wait_recv()
        total = far_buf[0]
        for index in range(1, far_ways):
            total = total + far_buf[index]
        gath[pl.ds(lo, size)] = total
    else:
        ns_steps()
        gath[pl.ds(lo, size)] = acc[pl.ds(lo, size)]

    for j in reversed(range(count)):
        low, ways = groups[j]
        base, piece = spans[j]
        mine = group_index(low, ways)
        own = pl.ds(pl.multiple_of(base + mine * piece, 8), piece)
        copies = []
        for m in range(1, ways):
            other = (mine + m) % ways
            copy = pltpu.make_async_remote_copy(
                src_ref=gath.at[own],
                dst_ref=gath.at[own],
                send_sem=send_ag.at[4 * j + m],
                recv_sem=recv_ag.at[4 * j + mine],
                device_id=(member(low, ways, other), col),
                device_id_type=MESH,
            )
            copy.start()
            copies.append(copy)
        ns_steps()
        for copy in copies:
            copy.wait_send()
        for m in range(1, ways):
            source = (mine + m) % ways
            theirs = pl.ds(pl.multiple_of(base + source * piece, 8), piece)
            pltpu.make_async_remote_copy(
                src_ref=gath.at[theirs],
                dst_ref=gath.at[theirs],
                send_sem=send_ag.at[4 * j],
                recv_sem=recv_ag.at[4 * j + source],
                device_id=(member(low, ways, source), col),
                device_id_type=MESH,
            ).wait_recv()

    o_ref[...] = jnp.dot(
        gath[...], inv_ref[...], precision=lax.Precision.HIGHEST,
        preferred_element_type=jnp.float32,
    )


def layer_allreduce_solve(rows, grams, layer_count):
    nbits = layer_count.bit_length() - 1
    if nbits == 7:
        stages = (
            (("bin", 0), ("bin", 1), ("bin", 2), ("quad", 5)),
            (("bin", 0), ("bin", 5), ("bin", 6), ("quad", 1)),
        )
        far = (3, 4)
    elif nbits == 5:
        stages = ((("bin", 0), ("bin", 1), ("bin", 2)), (("bin", 0), ("bin", 2), ("bin", 1)))
        far = (3, 4)
    else:
        stages = (tuple(("bin", k) for k in range(nbits)),) * 2
        far = ()
    count = len(stages[0])
    far_ways = 1 << len(far)
    slots = 2 * count + 1
    ns_plan = [INV_STEPS // slots + (1 if r < INV_STEPS % slots else 0) for r in range(slots)]
    pieces = rows
    width = grams.shape[-1]
    buf_shapes = []
    size = rows.shape[0]
    for kind, _ in stages[0]:
        ways = 2 if kind == "bin" else 4
        size //= ways
        buf_shapes.append(pltpu.VMEM((ways, size) + pieces.shape[1:], jnp.float32))
    solved, inverse = pl.pallas_call(
        functools.partial(layer_allreduce_kernel, stages, far, ns_plan),
        out_shape=(
            jax.ShapeDtypeStruct(pieces.shape, jnp.float32),
            jax.ShapeDtypeStruct((width, width), jnp.float32),
        ),
        in_specs=[pl.BlockSpec(memory_space=pltpu.VMEM)] * 2,
        out_specs=(pl.BlockSpec(memory_space=pltpu.VMEM),) * 2,
        scratch_shapes=[pltpu.VMEM(pieces.shape, jnp.float32)] * 2
        + [pltpu.VMEM((width, width), jnp.float32)]
        + buf_shapes
        + [pltpu.VMEM((far_ways, size) + pieces.shape[1:], jnp.float32)]
        + [pltpu.SemaphoreType.DMA((4 * count,))] * 4
        + [pltpu.SemaphoreType.DMA((far_ways,))] * 2,
        compiler_params=pltpu.CompilerParams(collective_id=0, has_side_effects=True),
    )(pieces, grams)
    return solved


def inl_gather_kernel(ways, b_ref, c_ref, o_ref, send1, recv1, send2, recv2):
    row = lax.axis_index("layer")
    col = lax.axis_index("inl")
    core = row % 2
    sibling = row + 1 - 2 * core
    half = b_ref.shape[1] // 2
    parts = (b_ref, c_ref)
    mine = pl.ds(pl.multiple_of(core * half, half), half)
    theirs = pl.ds(pl.multiple_of((1 - core) * half, half), half)
    barrier = pltpu.get_barrier_semaphore()
    for step in range(1, ways):
        pl.semaphore_signal(
            barrier, inc=1, device_id=(row, (col + step) % ways), device_id_type=MESH
        )
    pl.semaphore_signal(barrier, inc=1, device_id=(sibling, col), device_id_type=MESH)
    pl.semaphore_wait(barrier, ways)
    copies = []
    for step in range(1, ways):
        for part, x_ref in enumerate(parts):
            copy = pltpu.make_async_remote_copy(
                src_ref=x_ref.at[:, mine],
                dst_ref=o_ref.at[part, :, col, mine],
                send_sem=send1.at[2 * step + part],
                recv_sem=recv1.at[2 * col + part],
                device_id=(row, (col + step) % ways),
                device_id_type=MESH,
            )
            copy.start()
            copies.append(copy)
    for part, x_ref in enumerate(parts):
        o_ref[part, :, col] = x_ref[...]
    forwards = []
    for step in range(1, ways):
        source = (col + step) % ways
        for part in range(2):
            pltpu.make_async_remote_copy(
                src_ref=o_ref.at[part, :, source, mine],
                dst_ref=o_ref.at[part, :, source, mine],
                send_sem=send1.at[part],
                recv_sem=recv1.at[2 * source + part],
                device_id=(row, source),
                device_id_type=MESH,
            ).wait_recv()
        forward = pltpu.make_async_remote_copy(
            src_ref=o_ref.at[:, :, source, mine],
            dst_ref=o_ref.at[:, :, source, mine],
            send_sem=send2.at[step],
            recv_sem=recv2.at[source],
            device_id=(sibling, col),
            device_id_type=MESH,
        )
        forward.start()
        forwards.append(forward)
    for copy in copies:
        copy.wait_send()
    for forward in forwards:
        forward.wait_send()
    for step in range(1, ways):
        source = (col + step) % ways
        pltpu.make_async_remote_copy(
            src_ref=o_ref.at[:, :, source, theirs],
            dst_ref=o_ref.at[:, :, source, theirs],
            send_sem=send2.at[0],
            recv_sem=recv2.at[source],
            device_id=(sibling, col),
            device_id_type=MESH,
        ).wait_recv()


def inl_gather(factor_b, factor_c, ways):
    blocks, cells, rank_width = factor_b.shape
    return pl.pallas_call(
        functools.partial(inl_gather_kernel, ways),
        out_shape=jax.ShapeDtypeStruct((2, blocks, ways, cells, rank_width), factor_b.dtype),
        in_specs=[pl.BlockSpec(memory_space=pltpu.VMEM)] * 2,
        out_specs=pl.BlockSpec(memory_space=pltpu.VMEM),
        scratch_shapes=[pltpu.SemaphoreType.DMA((2 * ways,))] * 2
        + [pltpu.SemaphoreType.DMA((ways,))] * 2,
        compiler_params=pltpu.CompilerParams(collective_id=1, has_side_effects=True),
    )(factor_b, factor_c)


def mttkrp_kernel(coords_ref, filled_ref, blk_ref, b_ref, c_ref, o_ref):
    chunk = 32
    slot = pl.program_id(0)
    _, a_n, b_n, c_n = blk_ref.shape

    @pl.when(slot == 0)
    def _():
        o_ref[...] = jnp.zeros_like(o_ref)

    @pl.when(slot < filled_ref[0])
    def _():
        target = coords_ref[slot, 0]
        b_rows = b_ref[0].astype(jnp.float32)
        c_rows = c_ref[0]

        def body(i, carry):
            start = pl.multiple_of(i * chunk, chunk)
            x = blk_ref[0, pl.ds(start, chunk)].reshape(chunk * b_n, c_n)
            y = jnp.dot(x, c_rows, preferred_element_type=jnp.float32)
            z = y.reshape(chunk, b_n, -1) * b_rows[None]
            z = z.reshape(chunk, b_n // 8, 8, z.shape[-1]).sum(axis=1)
            o_ref[target, pl.ds(start, chunk)] += z.sum(axis=1)
            return carry

        lax.fori_loop(0, a_n // chunk, body, 0)


def mttkrp_rows(blocks, coords, filled, whole):
    slot_count, a_n, b_n, c_n = blocks.shape
    _, side_blocks, _, rank_width = whole.shape
    grid_spec = pltpu.PrefetchScalarGridSpec(
        num_scalar_prefetch=2,
        grid=(slot_count,),
        in_specs=[
            pl.BlockSpec((1, a_n, b_n, c_n), lambda s, cr, fl: (s, 0, 0, 0)),
            pl.BlockSpec((None, 1, b_n, rank_width), lambda s, cr, fl: (0, cr[s, 1], 0, 0)),
            pl.BlockSpec((None, 1, c_n, rank_width), lambda s, cr, fl: (1, cr[s, 2], 0, 0)),
        ],
        out_specs=pl.BlockSpec((side_blocks, a_n, rank_width), lambda s, cr, fl: (0, 0, 0)),
    )
    return pl.pallas_call(
        mttkrp_kernel,
        grid_spec=grid_spec,
        out_shape=jax.ShapeDtypeStruct((side_blocks, a_n, rank_width), jnp.float32),
        cost_estimate=pl.CostEstimate(
            flops=2 * slot_count * a_n * b_n * c_n * rank_width,
            bytes_accessed=blocks.size * 2 + slot_count * (b_n + c_n) * rank_width * 2,
            transcendentals=0,
        ),
    )(coords, filled, blocks, whole, whole)


def on_device(layer_count, inl_count, blocks, coords, filled, factor_b, factor_c):
    slot_count = blocks.shape[0]
    own_cells = blocks.shape[1]
    side_blocks = factor_b.shape[0]
    rank_width = factor_b.shape[2]
    ways = inl_count
    gathered = inl_gather(factor_b, factor_c, ways)
    whole = gathered.reshape(2, side_blocks, ways * factor_b.shape[1], rank_width)
    flat = whole.reshape(2, -1, rank_width)
    gram_parts = lax.dot_general(
        flat, flat, (((1,), (1,)), ((0,), (0,))), preferred_element_type=jnp.float32
    )
    buffer = mttkrp_rows(blocks, coords, filled, whole)
    row_totals = buffer.reshape(side_blocks * own_cells, rank_width)
    solved = layer_allreduce_solve(row_totals, gram_parts, layer_count)
    return solved.reshape(side_blocks, own_cells, rank_width)


def solution(mesh):
    in_specs = (
        P("layer", "inl", None, None),
        P("layer", None),
        P("layer"),
        P(None, "inl", None),
        P(None, "inl", None),
    )
    out_specs = P(None, "inl", None)
    return jax.shard_map(
        functools.partial(on_device, mesh.shape["layer"], mesh.shape["inl"]),
        mesh=mesh,
        in_specs=in_specs,
        out_specs=out_specs,
        check_vma=False,
    )
```

```python
import functools

import jax
import jax.numpy as jnp
from jax import lax
from jax.experimental import pallas as pl
from jax.experimental.pallas import tpu as pltpu
from jax.sharding import PartitionSpec as P

INV_STEPS = 24
MESH = pl.DeviceIdType.MESH


def layer_allreduce_kernel(stages, far, ns_plan, x_ref, grams_ref, o_ref, inv_ref, acc, gath, g_ref, *rest):
    count = len(stages[0])
    bufs = rest[:count]
    far_buf = rest[count]
    send_rs, recv_rs, send_ag, recv_ag, far_send, far_recv = rest[count + 1:]
    me = lax.axis_index("layer")
    col = lax.axis_index("inl")
    far_ways = far_buf.shape[0]

    core = me % 2

    def group_index(step, ways):
        return (me // step) % ways

    def member(step, ways, other):
        return me + (other - group_index(step, ways)) * step

    groups = [
        (core * (1 << low1) + (1 - core) * (1 << low0), 2 if kind == "bin" else 4)
        for (kind, low0), (_, low1) in zip(stages[0], stages[1])
    ]
    far_step = 1 << far[0] if far else 1
    if far:
        groups.append((far_step, far_ways))
    barrier = pltpu.get_barrier_semaphore()
    signals = 0
    for low, ways in groups:
        mine = group_index(low, ways)
        for m in range(1, ways):
            pl.semaphore_signal(
                barrier, inc=1, device_id=(member(low, ways, (mine + m) % ways), col),
                device_id_type=MESH,
            )
            signals += 1
    pl.semaphore_wait(barrier, signals)

    width = g_ref.shape[0]
    rows = lax.broadcasted_iota(jnp.int32, (width, width), 0)
    cols = lax.broadcasted_iota(jnp.int32, (width, width), 1)
    two_ident = jnp.where(rows == cols, 2.0, 0.0).astype(jnp.float32)
    plan = iter(ns_plan)

    def ns_start():
        gram = grams_ref[0] * grams_ref[1]
        g_ref[...] = gram
        norm_sq = jnp.sum(jnp.sum(gram * gram, axis=1, keepdims=True), axis=0, keepdims=True)
        inv_ref[...] = (0.5 * two_ident) / jnp.sqrt(norm_sq)

    done = [0]

    def ns_steps():
        for _ in range(next(plan)):
            precision = (
                lax.Precision.HIGH if done[0] < INV_STEPS - 4
                else lax.Precision.HIGHEST
            )
            done[0] += 1
            current = inv_ref[...]
            product = jnp.dot(
                g_ref[...], current, precision=precision,
                preferred_element_type=jnp.float32,
            )
            inv_ref[...] = jnp.dot(
                current, two_ident - product, precision=precision,
                preferred_element_type=jnp.float32,
            )

    acc[...] = x_ref[...]
    lo = 0
    size = acc.shape[0]
    spans = []
    for j, (low, ways) in enumerate(groups[:count]):
        piece = size // ways
        mine = group_index(low, ways)
        copies = []
        for m in range(1, ways):
            other = (mine + m) % ways
            copy = pltpu.make_async_remote_copy(
                src_ref=acc.at[pl.ds(pl.multiple_of(lo + other * piece, 8), piece)],
                dst_ref=bufs[j].at[mine],
                send_sem=send_rs.at[4 * j + m],
                recv_sem=recv_rs.at[4 * j + mine],
                device_id=(member(low, ways, other), col),
                device_id_type=MESH,
            )
            copy.start()
            copies.append(copy)
        keep_lo = pl.multiple_of(lo + mine * piece, 8)
        bufs[j][mine] = acc[pl.ds(keep_lo, piece)]
        if j == 0:
            ns_start()
        ns_steps()
        for copy in copies:
            copy.wait_send()
        for m in range(1, ways):
            source = (mine + m) % ways
            pltpu.make_async_remote_copy(
                src_ref=bufs[j].at[source],
                dst_ref=bufs[j].at[source],
                send_sem=send_rs.at[4 * j],
                recv_sem=recv_rs.at[4 * j + source],
                device_id=(member(low, ways, source), col),
                device_id_type=MESH,
            ).wait_recv()
        total = bufs[j][0]
        for index in range(1, ways):
            total = total + bufs[j][index]
        acc[pl.ds(keep_lo, piece)] = total
        spans.append((lo, piece))
        lo = keep_lo
        size = piece

    if far:
        far_me = group_index(far_step, far_ways)
        far_buf[far_me] = acc[pl.ds(lo, size)]
        copies = []
        for m in range(1, far_ways):
            copy = pltpu.make_async_remote_copy(
                src_ref=acc.at[pl.ds(lo, size)],
                dst_ref=far_buf.at[far_me],
                send_sem=far_send.at[m],
                recv_sem=far_recv.at[far_me],
                device_id=(member(far_step, far_ways, (far_me + m) % far_ways), col),
                device_id_type=MESH,
            )
            copy.start()
            copies.append(copy)
        ns_steps()
        for copy in copies:
            copy.wait_send()
        for m in range(1, far_ways):
            source = (far_me + m) % far_ways
            pltpu.make_async_remote_copy(
                src_ref=far_buf.at[source],
                dst_ref=far_buf.at[source],
                send_sem=far_send.at[0],
                recv_sem=far_recv.at[source],
                device_id=(member(far_step, far_ways, source), col),
                device_id_type=MESH,
            ).wait_recv()
        total = far_buf[0]
        for index in range(1, far_ways):
            total = total + far_buf[index]
        gath[pl.ds(lo, size)] = total
    else:
        ns_steps()
        gath[pl.ds(lo, size)] = acc[pl.ds(lo, size)]

    for j in reversed(range(count)):
        low, ways = groups[j]
        base, piece = spans[j]
        mine = group_index(low, ways)
        own = pl.ds(pl.multiple_of(base + mine * piece, 8), piece)
        copies = []
        for m in range(1, ways):
            other = (mine + m) % ways
            copy = pltpu.make_async_remote_copy(
                src_ref=gath.at[own],
                dst_ref=gath.at[own],
                send_sem=send_ag.at[4 * j + m],
                recv_sem=recv_ag.at[4 * j + mine],
                device_id=(member(low, ways, other), col),
                device_id_type=MESH,
            )
            copy.start()
            copies.append(copy)
        ns_steps()
        for copy in copies:
            copy.wait_send()
        for m in range(1, ways):
            source = (mine + m) % ways
            theirs = pl.ds(pl.multiple_of(base + source * piece, 8), piece)
            pltpu.make_async_remote_copy(
                src_ref=gath.at[theirs],
                dst_ref=gath.at[theirs],
                send_sem=send_ag.at[4 * j],
                recv_sem=recv_ag.at[4 * j + source],
                device_id=(member(low, ways, source), col),
                device_id_type=MESH,
            ).wait_recv()

    o_ref[...] = jnp.dot(
        gath[...], inv_ref[...], precision=lax.Precision.HIGHEST,
        preferred_element_type=jnp.float32,
    )


def layer_allreduce_solve(rows, grams, layer_count):
    nbits = layer_count.bit_length() - 1
    if nbits == 7:
        stages = (
            (("bin", 0), ("bin", 1), ("bin", 2), ("quad", 5)),
            (("bin", 0), ("bin", 5), ("bin", 6), ("quad", 1)),
        )
        far = (3, 4)
    elif nbits == 5:
        stages = ((("bin", 0), ("bin", 1), ("bin", 2)), (("bin", 0), ("bin", 2), ("bin", 1)))
        far = (3, 4)
    else:
        stages = (tuple(("bin", k) for k in range(nbits)),) * 2
        far = ()
    count = len(stages[0])
    far_ways = 1 << len(far)
    slots = 2 * count + 1
    ns_plan = [INV_STEPS // slots + (1 if r < INV_STEPS % slots else 0) for r in range(slots)]
    pieces = rows
    width = grams.shape[-1]
    buf_shapes = []
    size = rows.shape[0]
    for kind, _ in stages[0]:
        ways = 2 if kind == "bin" else 4
        size //= ways
        buf_shapes.append(pltpu.VMEM((ways, size) + pieces.shape[1:], jnp.float32))
    solved, inverse = pl.pallas_call(
        functools.partial(layer_allreduce_kernel, stages, far, ns_plan),
        out_shape=(
            jax.ShapeDtypeStruct(pieces.shape, jnp.float32),
            jax.ShapeDtypeStruct((width, width), jnp.float32),
        ),
        in_specs=[pl.BlockSpec(memory_space=pltpu.VMEM)] * 2,
        out_specs=(pl.BlockSpec(memory_space=pltpu.VMEM),) * 2,
        scratch_shapes=[pltpu.VMEM(pieces.shape, jnp.float32)] * 2
        + [pltpu.VMEM((width, width), jnp.float32)]
        + buf_shapes
        + [pltpu.VMEM((far_ways, size) + pieces.shape[1:], jnp.float32)]
        + [pltpu.SemaphoreType.DMA((4 * count,))] * 4
        + [pltpu.SemaphoreType.DMA((far_ways,))] * 2,
        compiler_params=pltpu.CompilerParams(collective_id=0, has_side_effects=True),
    )(pieces, grams)
    return solved


def inl_gather_kernel(ways, b_ref, c_ref, o_ref, send1, recv1, send2, recv2):
    row = lax.axis_index("layer")
    col = lax.axis_index("inl")
    core = row % 2
    sibling = row + 1 - 2 * core
    half = b_ref.shape[1] // 2
    parts = (b_ref, c_ref)
    mine = pl.ds(pl.multiple_of(core * half, half), half)
    theirs = pl.ds(pl.multiple_of((1 - core) * half, half), half)
    barrier = pltpu.get_barrier_semaphore()
    for step in range(1, ways):
        pl.semaphore_signal(
            barrier, inc=1, device_id=(row, (col + step) % ways), device_id_type=MESH
        )
    pl.semaphore_signal(barrier, inc=1, device_id=(sibling, col), device_id_type=MESH)
    pl.semaphore_wait(barrier, ways)
    copies = []
    for step in range(1, ways):
        for part, x_ref in enumerate(parts):
            copy = pltpu.make_async_remote_copy(
                src_ref=x_ref.at[:, mine],
                dst_ref=o_ref.at[part, :, col, mine],
                send_sem=send1.at[2 * step + part],
                recv_sem=recv1.at[2 * col + part],
                device_id=(row, (col + step) % ways),
                device_id_type=MESH,
            )
            copy.start()
            copies.append(copy)
    for part, x_ref in enumerate(parts):
        o_ref[part, :, col] = x_ref[...]
    forwards = []
    for step in range(1, ways):
        source = (col + step) % ways
        for part in range(2):
            pltpu.make_async_remote_copy(
                src_ref=o_ref.at[part, :, source, mine],
                dst_ref=o_ref.at[part, :, source, mine],
                send_sem=send1.at[part],
                recv_sem=recv1.at[2 * source + part],
                device_id=(row, source),
                device_id_type=MESH,
            ).wait_recv()
        forward = pltpu.make_async_remote_copy(
            src_ref=o_ref.at[:, :, source, mine],
            dst_ref=o_ref.at[:, :, source, mine],
            send_sem=send2.at[step],
            recv_sem=recv2.at[source],
            device_id=(sibling, col),
            device_id_type=MESH,
        )
        forward.start()
        forwards.append(forward)
    for copy in copies:
        copy.wait_send()
    for forward in forwards:
        forward.wait_send()
    for step in range(1, ways):
        source = (col + step) % ways
        pltpu.make_async_remote_copy(
            src_ref=o_ref.at[:, :, source, theirs],
            dst_ref=o_ref.at[:, :, source, theirs],
            send_sem=send2.at[0],
            recv_sem=recv2.at[source],
            device_id=(sibling, col),
            device_id_type=MESH,
        ).wait_recv()


def inl_gather(factor_b, factor_c, ways):
    blocks, cells, rank_width = factor_b.shape
    return pl.pallas_call(
        functools.partial(inl_gather_kernel, ways),
        out_shape=jax.ShapeDtypeStruct((2, blocks, ways, cells, rank_width), factor_b.dtype),
        in_specs=[pl.BlockSpec(memory_space=pltpu.VMEM)] * 2,
        out_specs=pl.BlockSpec(memory_space=pltpu.VMEM),
        scratch_shapes=[pltpu.SemaphoreType.DMA((2 * ways,))] * 2
        + [pltpu.SemaphoreType.DMA((ways,))] * 2,
        compiler_params=pltpu.CompilerParams(collective_id=1, has_side_effects=True),
    )(factor_b, factor_c)


def mttkrp_kernel(coords_ref, filled_ref, blk_ref, b_ref, c_ref, o_ref):
    chunk = 32
    slot = pl.program_id(0)
    _, a_n, b_n, c_n = blk_ref.shape

    @pl.when(slot == 0)
    def _():
        o_ref[...] = jnp.zeros_like(o_ref)

    @pl.when(slot < filled_ref[0])
    def _():
        target = coords_ref[slot, 0]
        b_rows = b_ref[0].astype(jnp.float32)
        c_rows = c_ref[0]

        def body(i, carry):
            start = pl.multiple_of(i * chunk, chunk)
            x = blk_ref[0, pl.ds(start, chunk)].reshape(chunk * b_n, c_n)
            y = jnp.dot(x, c_rows, preferred_element_type=jnp.float32)
            z = y.reshape(chunk, b_n, -1) * b_rows[None]
            z = z.reshape(chunk, b_n // 8, 8, z.shape[-1]).sum(axis=1)
            o_ref[target, pl.ds(start, chunk)] += z.sum(axis=1)
            return carry

        lax.fori_loop(0, a_n // chunk, body, 0)


def mttkrp_rows(blocks, coords, filled, whole):
    slot_count, a_n, b_n, c_n = blocks.shape
    _, side_blocks, _, rank_width = whole.shape
    grid_spec = pltpu.PrefetchScalarGridSpec(
        num_scalar_prefetch=2,
        grid=(slot_count,),
        in_specs=[
            pl.BlockSpec((1, a_n, b_n, c_n), lambda s, cr, fl: (s, 0, 0, 0)),
            pl.BlockSpec((None, 1, b_n, rank_width), lambda s, cr, fl: (0, cr[s, 1], 0, 0)),
            pl.BlockSpec((None, 1, c_n, rank_width), lambda s, cr, fl: (1, cr[s, 2], 0, 0)),
        ],
        out_specs=pl.BlockSpec((side_blocks, a_n, rank_width), lambda s, cr, fl: (0, 0, 0)),
    )
    return pl.pallas_call(
        mttkrp_kernel,
        grid_spec=grid_spec,
        out_shape=jax.ShapeDtypeStruct((side_blocks, a_n, rank_width), jnp.float32),
        cost_estimate=pl.CostEstimate(
            flops=2 * slot_count * a_n * b_n * c_n * rank_width,
            bytes_accessed=blocks.size * 2 + slot_count * (b_n + c_n) * rank_width * 2,
            transcendentals=0,
        ),
    )(coords, filled, blocks, whole, whole)


def on_device(layer_count, inl_count, blocks, coords, filled, factor_b, factor_c):
    slot_count = blocks.shape[0]
    own_cells = blocks.shape[1]
    side_blocks = factor_b.shape[0]
    rank_width = factor_b.shape[2]
    ways = inl_count
    gathered = inl_gather(factor_b, factor_c, ways)
    whole = gathered.reshape(2, side_blocks, ways * factor_b.shape[1], rank_width)
    flat = whole.reshape(2, -1, rank_width)
    gram_parts = lax.dot_general(
        flat, flat, (((1,), (1,)), ((0,), (0,))), preferred_element_type=jnp.float32
    )
    buffer = mttkrp_rows(blocks, coords, filled, whole)
    row_totals = buffer.reshape(side_blocks * own_cells, rank_width)
    solved = layer_allreduce_solve(row_totals, gram_parts, layer_count)
    return solved.reshape(side_blocks, own_cells, rank_width)


def solution(mesh):
    in_specs = (
        P("layer", "inl", None, None),
        P("layer", None),
        P("layer"),
        P(None, "inl", None),
        P(None, "inl", None),
    )
    out_specs = P(None, "inl", None)
    return jax.shard_map(
        functools.partial(on_device, mesh.shape["layer"], mesh.shape["inl"]),
        mesh=mesh,
        in_specs=in_specs,
        out_specs=out_specs,
        check_vma=False,
    )
```

```python
import functools

import jax
import jax.numpy as jnp
from jax import lax
from jax.experimental import pallas as pl
from jax.experimental.pallas import tpu as pltpu
from jax.sharding import PartitionSpec as P

INV_STEPS = 24
MESH = pl.DeviceIdType.MESH


def layer_allreduce_kernel(stages, far, ns_plan, x_ref, grams_ref, o_ref, inv_ref, acc, gath, g_ref, *rest):
    count = len(stages[0])
    bufs = rest[:count]
    far_buf = rest[count]
    send_rs, recv_rs, send_ag, recv_ag, far_send, far_recv = rest[count + 1:]
    me = lax.axis_index("layer")
    col = lax.axis_index("inl")
    far_ways = far_buf.shape[0]

    core = me % 2

    def group_index(step, ways):
        return (me // step) % ways

    def member(step, ways, other):
        return me + (other - group_index(step, ways)) * step

    groups = [
        (core * (1 << low1) + (1 - core) * (1 << low0), 2 if kind == "bin" else 4)
        for (kind, low0), (_, low1) in zip(stages[0], stages[1])
    ]
    far_step = 1 << far[0] if far else 1
    if far:
        groups.append((far_step, far_ways))
    barrier = pltpu.get_barrier_semaphore()
    signals = 0
    for low, ways in groups:
        mine = group_index(low, ways)
        for m in range(1, ways):
            pl.semaphore_signal(
                barrier, inc=1, device_id=(member(low, ways, (mine + m) % ways), col),
                device_id_type=MESH,
            )
            signals += 1
    pl.semaphore_wait(barrier, signals)

    width = g_ref.shape[0]
    rows = lax.broadcasted_iota(jnp.int32, (width, width), 0)
    cols = lax.broadcasted_iota(jnp.int32, (width, width), 1)
    two_ident = jnp.where(rows == cols, 2.0, 0.0).astype(jnp.float32)
    plan = iter(ns_plan)

    def ns_start():
        gram = grams_ref[0] * grams_ref[1]
        g_ref[...] = gram
        norm_sq = jnp.sum(jnp.sum(gram * gram, axis=1, keepdims=True), axis=0, keepdims=True)
        inv_ref[...] = (0.5 * two_ident) / jnp.sqrt(norm_sq)

    done = [0]

    def ns_steps():
        for _ in range(next(plan)):
            precision = (
                lax.Precision.HIGH if done[0] < INV_STEPS - 4
                else lax.Precision.HIGHEST
            )
            done[0] += 1
            current = inv_ref[...]
            product = jnp.dot(
                g_ref[...], current, precision=precision,
                preferred_element_type=jnp.float32,
            )
            inv_ref[...] = jnp.dot(
                current, two_ident - product, precision=precision,
                preferred_element_type=jnp.float32,
            )

    acc[...] = x_ref[...]
    lo = 0
    size = acc.shape[0]
    spans = []
    for j, (low, ways) in enumerate(groups[:count]):
        piece = size // ways
        mine = group_index(low, ways)
        copies = []
        for m in range(1, ways):
            other = (mine + m) % ways
            copy = pltpu.make_async_remote_copy(
                src_ref=acc.at[pl.ds(pl.multiple_of(lo + other * piece, 8), piece)],
                dst_ref=bufs[j].at[mine],
                send_sem=send_rs.at[4 * j + m],
                recv_sem=recv_rs.at[4 * j + mine],
                device_id=(member(low, ways, other), col),
                device_id_type=MESH,
            )
            copy.start()
            copies.append(copy)
        keep_lo = pl.multiple_of(lo + mine * piece, 8)
        if j == 0:
            ns_start()
        ns_steps()
        for copy in copies:
            copy.wait_send()
        for m in range(1, ways):
            source = (mine + m) % ways
            pltpu.make_async_remote_copy(
                src_ref=bufs[j].at[source],
                dst_ref=bufs[j].at[source],
                send_sem=send_rs.at[4 * j],
                recv_sem=recv_rs.at[4 * j + source],
                device_id=(member(low, ways, source), col),
                device_id_type=MESH,
            ).wait_recv()
        total = acc[pl.ds(keep_lo, piece)]
        for m in range(1, ways):
            total = total + bufs[j][(mine + m) % ways]
        acc[pl.ds(keep_lo, piece)] = total
        spans.append((lo, piece))
        lo = keep_lo
        size = piece

    if far:
        far_me = group_index(far_step, far_ways)
        far_buf[far_me] = acc[pl.ds(lo, size)]
        copies = []
        for m in range(1, far_ways):
            copy = pltpu.make_async_remote_copy(
                src_ref=acc.at[pl.ds(lo, size)],
                dst_ref=far_buf.at[far_me],
                send_sem=far_send.at[m],
                recv_sem=far_recv.at[far_me],
                device_id=(member(far_step, far_ways, (far_me + m) % far_ways), col),
                device_id_type=MESH,
            )
            copy.start()
            copies.append(copy)
        ns_steps()
        for copy in copies:
            copy.wait_send()
        for m in range(1, far_ways):
            source = (far_me + m) % far_ways
            pltpu.make_async_remote_copy(
                src_ref=far_buf.at[source],
                dst_ref=far_buf.at[source],
                send_sem=far_send.at[0],
                recv_sem=far_recv.at[source],
                device_id=(member(far_step, far_ways, source), col),
                device_id_type=MESH,
            ).wait_recv()
        total = far_buf[0]
        for index in range(1, far_ways):
            total = total + far_buf[index]
        gath[pl.ds(lo, size)] = total
    else:
        ns_steps()
        gath[pl.ds(lo, size)] = acc[pl.ds(lo, size)]

    for j in reversed(range(count)):
        low, ways = groups[j]
        base, piece = spans[j]
        mine = group_index(low, ways)
        own = pl.ds(pl.multiple_of(base + mine * piece, 8), piece)
        copies = []
        for m in range(1, ways):
            other = (mine + m) % ways
            copy = pltpu.make_async_remote_copy(
                src_ref=gath.at[own],
                dst_ref=gath.at[own],
                send_sem=send_ag.at[4 * j + m],
                recv_sem=recv_ag.at[4 * j + mine],
                device_id=(member(low, ways, other), col),
                device_id_type=MESH,
            )
            copy.start()
            copies.append(copy)
        ns_steps()
        for copy in copies:
            copy.wait_send()
        for m in range(1, ways):
            source = (mine + m) % ways
            theirs = pl.ds(pl.multiple_of(base + source * piece, 8), piece)
            pltpu.make_async_remote_copy(
                src_ref=gath.at[theirs],
                dst_ref=gath.at[theirs],
                send_sem=send_ag.at[4 * j],
                recv_sem=recv_ag.at[4 * j + source],
                device_id=(member(low, ways, source), col),
                device_id_type=MESH,
            ).wait_recv()

    o_ref[...] = jnp.dot(
        gath[...], inv_ref[...], precision=lax.Precision.HIGHEST,
        preferred_element_type=jnp.float32,
    )


def layer_allreduce_solve(rows, grams, layer_count):
    nbits = layer_count.bit_length() - 1
    if nbits == 7:
        stages = (
            (("bin", 0), ("bin", 1), ("bin", 2), ("quad", 5)),
            (("bin", 0), ("bin", 5), ("bin", 6), ("quad", 1)),
        )
        far = (3, 4)
    elif nbits == 5:
        stages = ((("bin", 0), ("bin", 1), ("bin", 2)), (("bin", 0), ("bin", 2), ("bin", 1)))
        far = (3, 4)
    else:
        stages = (tuple(("bin", k) for k in range(nbits)),) * 2
        far = ()
    count = len(stages[0])
    far_ways = 1 << len(far)
    slots = 2 * count + 1
    ns_plan = [INV_STEPS // slots + (1 if r < INV_STEPS % slots else 0) for r in range(slots)]
    pieces = rows
    width = grams.shape[-1]
    buf_shapes = []
    size = rows.shape[0]
    for kind, _ in stages[0]:
        ways = 2 if kind == "bin" else 4
        size //= ways
        buf_shapes.append(pltpu.VMEM((ways, size) + pieces.shape[1:], jnp.float32))
    solved, inverse = pl.pallas_call(
        functools.partial(layer_allreduce_kernel, stages, far, ns_plan),
        out_shape=(
            jax.ShapeDtypeStruct(pieces.shape, jnp.float32),
            jax.ShapeDtypeStruct((width, width), jnp.float32),
        ),
        in_specs=[pl.BlockSpec(memory_space=pltpu.VMEM)] * 2,
        out_specs=(pl.BlockSpec(memory_space=pltpu.VMEM),) * 2,
        scratch_shapes=[pltpu.VMEM(pieces.shape, jnp.float32)] * 2
        + [pltpu.VMEM((width, width), jnp.float32)]
        + buf_shapes
        + [pltpu.VMEM((far_ways, size) + pieces.shape[1:], jnp.float32)]
        + [pltpu.SemaphoreType.DMA((4 * count,))] * 4
        + [pltpu.SemaphoreType.DMA((far_ways,))] * 2,
        compiler_params=pltpu.CompilerParams(collective_id=0, has_side_effects=True),
    )(pieces, grams)
    return solved


def inl_gather_kernel(ways, b_ref, c_ref, o_ref, send1, recv1, send2, recv2):
    row = lax.axis_index("layer")
    col = lax.axis_index("inl")
    core = row % 2
    sibling = row + 1 - 2 * core
    half = b_ref.shape[1] // 2
    parts = (b_ref, c_ref)
    mine = pl.ds(pl.multiple_of(core * half, half), half)
    theirs = pl.ds(pl.multiple_of((1 - core) * half, half), half)
    barrier = pltpu.get_barrier_semaphore()
    for step in range(1, ways):
        pl.semaphore_signal(
            barrier, inc=1, device_id=(row, (col + step) % ways), device_id_type=MESH
        )
    pl.semaphore_signal(barrier, inc=1, device_id=(sibling, col), device_id_type=MESH)
    pl.semaphore_wait(barrier, ways)
    copies = []
    for step in range(1, ways):
        for part, x_ref in enumerate(parts):
            copy = pltpu.make_async_remote_copy(
                src_ref=x_ref.at[:, mine],
                dst_ref=o_ref.at[part, :, col, mine],
                send_sem=send1.at[2 * step + part],
                recv_sem=recv1.at[2 * col + part],
                device_id=(row, (col + step) % ways),
                device_id_type=MESH,
            )
            copy.start()
            copies.append(copy)
    for part, x_ref in enumerate(parts):
        o_ref[part, :, col] = x_ref[...]
    forwards = []
    for step in range(1, ways):
        source = (col + step) % ways
        for part in range(2):
            pltpu.make_async_remote_copy(
                src_ref=o_ref.at[part, :, source, mine],
                dst_ref=o_ref.at[part, :, source, mine],
                send_sem=send1.at[part],
                recv_sem=recv1.at[2 * source + part],
                device_id=(row, source),
                device_id_type=MESH,
            ).wait_recv()
        forward = pltpu.make_async_remote_copy(
            src_ref=o_ref.at[:, :, source, mine],
            dst_ref=o_ref.at[:, :, source, mine],
            send_sem=send2.at[step],
            recv_sem=recv2.at[source],
            device_id=(sibling, col),
            device_id_type=MESH,
        )
        forward.start()
        forwards.append(forward)
    for copy in copies:
        copy.wait_send()
    for forward in forwards:
        forward.wait_send()
    for step in range(1, ways):
        source = (col + step) % ways
        pltpu.make_async_remote_copy(
            src_ref=o_ref.at[:, :, source, theirs],
            dst_ref=o_ref.at[:, :, source, theirs],
            send_sem=send2.at[0],
            recv_sem=recv2.at[source],
            device_id=(sibling, col),
            device_id_type=MESH,
        ).wait_recv()


def inl_gather(factor_b, factor_c, ways):
    blocks, cells, rank_width = factor_b.shape
    return pl.pallas_call(
        functools.partial(inl_gather_kernel, ways),
        out_shape=jax.ShapeDtypeStruct((2, blocks, ways, cells, rank_width), factor_b.dtype),
        in_specs=[pl.BlockSpec(memory_space=pltpu.VMEM)] * 2,
        out_specs=pl.BlockSpec(memory_space=pltpu.VMEM),
        scratch_shapes=[pltpu.SemaphoreType.DMA((2 * ways,))] * 2
        + [pltpu.SemaphoreType.DMA((ways,))] * 2,
        compiler_params=pltpu.CompilerParams(collective_id=1, has_side_effects=True),
    )(factor_b, factor_c)


def mttkrp_kernel(coords_ref, filled_ref, blk_ref, b_ref, c_ref, o_ref):
    chunk = 32
    slot = pl.program_id(0)
    _, a_n, b_n, c_n = blk_ref.shape

    @pl.when(slot == 0)
    def _():
        o_ref[...] = jnp.zeros_like(o_ref)

    @pl.when(slot < filled_ref[0])
    def _():
        target = coords_ref[slot, 0]
        b_rows = b_ref[0].astype(jnp.float32)
        c_rows = c_ref[0]

        def body(i, carry):
            start = pl.multiple_of(i * chunk, chunk)
            x = blk_ref[0, pl.ds(start, chunk)].reshape(chunk * b_n, c_n)
            y = jnp.dot(x, c_rows, preferred_element_type=jnp.float32)
            z = y.reshape(chunk, b_n, -1) * b_rows[None]
            z = z.reshape(chunk, b_n // 8, 8, z.shape[-1]).sum(axis=1)
            o_ref[target, pl.ds(start, chunk)] += z.sum(axis=1)
            return carry

        lax.fori_loop(0, a_n // chunk, body, 0)


def mttkrp_rows(blocks, coords, filled, whole):
    slot_count, a_n, b_n, c_n = blocks.shape
    _, side_blocks, _, rank_width = whole.shape
    grid_spec = pltpu.PrefetchScalarGridSpec(
        num_scalar_prefetch=2,
        grid=(slot_count,),
        in_specs=[
            pl.BlockSpec((1, a_n, b_n, c_n), lambda s, cr, fl: (s, 0, 0, 0)),
            pl.BlockSpec((None, 1, b_n, rank_width), lambda s, cr, fl: (0, cr[s, 1], 0, 0)),
            pl.BlockSpec((None, 1, c_n, rank_width), lambda s, cr, fl: (1, cr[s, 2], 0, 0)),
        ],
        out_specs=pl.BlockSpec((side_blocks, a_n, rank_width), lambda s, cr, fl: (0, 0, 0)),
    )
    return pl.pallas_call(
        mttkrp_kernel,
        grid_spec=grid_spec,
        out_shape=jax.ShapeDtypeStruct((side_blocks, a_n, rank_width), jnp.float32),
        cost_estimate=pl.CostEstimate(
            flops=2 * slot_count * a_n * b_n * c_n * rank_width,
            bytes_accessed=blocks.size * 2 + slot_count * (b_n + c_n) * rank_width * 2,
            transcendentals=0,
        ),
    )(coords, filled, blocks, whole, whole)


def on_device(layer_count, inl_count, blocks, coords, filled, factor_b, factor_c):
    slot_count = blocks.shape[0]
    own_cells = blocks.shape[1]
    side_blocks = factor_b.shape[0]
    rank_width = factor_b.shape[2]
    ways = inl_count
    gathered = inl_gather(factor_b, factor_c, ways)
    whole = gathered.reshape(2, side_blocks, ways * factor_b.shape[1], rank_width)
    flat = whole.reshape(2, -1, rank_width)
    gram_parts = lax.dot_general(
        flat, flat, (((1,), (1,)), ((0,), (0,))), preferred_element_type=jnp.float32
    )
    buffer = mttkrp_rows(blocks, coords, filled, whole)
    row_totals = buffer.reshape(side_blocks * own_cells, rank_width)
    solved = layer_allreduce_solve(row_totals, gram_parts, layer_count)
    return solved.reshape(side_blocks, own_cells, rank_width)


def solution(mesh):
    in_specs = (
        P("layer", "inl", None, None),
        P("layer", None),
        P("layer"),
        P(None, "inl", None),
        P(None, "inl", None),
    )
    out_specs = P(None, "inl", None)
    return jax.shard_map(
        functools.partial(on_device, mesh.shape["layer"], mesh.shape["inl"]),
        mesh=mesh,
        in_specs=in_specs,
        out_specs=out_specs,
        check_vma=False,
    )
```

```python
import functools

import jax
import jax.numpy as jnp
from jax import lax
from jax.experimental import pallas as pl
from jax.experimental.pallas import tpu as pltpu
from jax.sharding import PartitionSpec as P

INV_STEPS = 24
MESH = pl.DeviceIdType.MESH


def layer_allreduce_kernel(stages, far, ns_plan, x_ref, grams_ref, o_ref, inv_ref, acc, gath, g_ref, *rest):
    count = len(stages[0])
    bufs = rest[:count]
    far_buf = rest[count]
    send_rs, recv_rs, send_ag, recv_ag, far_send, far_recv = rest[count + 1:]
    me = lax.axis_index("layer")
    col = lax.axis_index("inl")
    far_ways = far_buf.shape[0]

    core = me % 2

    def group_index(step, ways):
        return (me // step) % ways

    def member(step, ways, other):
        return me + (other - group_index(step, ways)) * step

    groups = [
        (core * (1 << low1) + (1 - core) * (1 << low0), 2 if kind == "bin" else 4)
        for (kind, low0), (_, low1) in zip(stages[0], stages[1])
    ]
    far_step = 1 << far[0] if far else 1
    if far:
        groups.append((far_step, far_ways))
    barrier = pltpu.get_barrier_semaphore()
    signals = 0
    for low, ways in groups:
        mine = group_index(low, ways)
        for m in range(1, ways):
            pl.semaphore_signal(
                barrier, inc=1, device_id=(member(low, ways, (mine + m) % ways), col),
                device_id_type=MESH,
            )
            signals += 1
    pl.semaphore_wait(barrier, signals)

    width = g_ref.shape[0]
    rows = lax.broadcasted_iota(jnp.int32, (width, width), 0)
    cols = lax.broadcasted_iota(jnp.int32, (width, width), 1)
    two_ident = jnp.where(rows == cols, 2.0, 0.0).astype(jnp.float32)
    plan = iter(ns_plan)

    def ns_start():
        gram = grams_ref[0] * grams_ref[1]
        g_ref[...] = gram
        norm_sq = jnp.sum(jnp.sum(gram * gram, axis=1, keepdims=True), axis=0, keepdims=True)
        inv_ref[...] = (0.5 * two_ident) / jnp.sqrt(norm_sq)

    done = [0]

    def ns_steps():
        for _ in range(next(plan)):
            precision = (
                lax.Precision.HIGH if done[0] < INV_STEPS - 4
                else lax.Precision.HIGHEST
            )
            done[0] += 1
            current = inv_ref[...]
            product = jnp.dot(
                g_ref[...], current, precision=precision,
                preferred_element_type=jnp.float32,
            )
            inv_ref[...] = jnp.dot(
                current, two_ident - product, precision=precision,
                preferred_element_type=jnp.float32,
            )

    acc[...] = x_ref[...]
    lo = 0
    size = acc.shape[0]
    spans = []
    for j, (low, ways) in enumerate(groups[:count]):
        piece = size // ways
        mine = group_index(low, ways)
        copies = []
        for m in range(1, ways):
            other = (mine + m) % ways
            copy = pltpu.make_async_remote_copy(
                src_ref=acc.at[pl.ds(pl.multiple_of(lo + other * piece, 8), piece)],
                dst_ref=bufs[j].at[mine],
                send_sem=send_rs.at[4 * j + m],
                recv_sem=recv_rs.at[4 * j + mine],
                device_id=(member(low, ways, other), col),
                device_id_type=MESH,
            )
            copy.start()
            copies.append(copy)
        keep_lo = pl.multiple_of(lo + mine * piece, 8)
        bufs[j][mine] = acc[pl.ds(keep_lo, piece)]
        if j == 0:
            ns_start()
        ns_steps()
        for copy in copies:
            copy.wait_send()
        for m in range(1, ways):
            source = (mine + m) % ways
            pltpu.make_async_remote_copy(
                src_ref=bufs[j].at[source],
                dst_ref=bufs[j].at[source],
                send_sem=send_rs.at[4 * j],
                recv_sem=recv_rs.at[4 * j + source],
                device_id=(member(low, ways, source), col),
                device_id_type=MESH,
            ).wait_recv()
        total = bufs[j][0]
        for index in range(1, ways):
            total = total + bufs[j][index]
        acc[pl.ds(keep_lo, piece)] = total
        spans.append((lo, piece))
        lo = keep_lo
        size = piece

    if far:
        far_me = group_index(far_step, far_ways)
        far_buf[far_me] = acc[pl.ds(lo, size)]
        copies = []
        for m in range(1, far_ways):
            copy = pltpu.make_async_remote_copy(
                src_ref=acc.at[pl.ds(lo, size)],
                dst_ref=far_buf.at[far_me],
                send_sem=far_send.at[m],
                recv_sem=far_recv.at[far_me],
                device_id=(member(far_step, far_ways, (far_me + m) % far_ways), col),
                device_id_type=MESH,
            )
            copy.start()
            copies.append(copy)
        ns_steps()
        for copy in copies:
            copy.wait_send()
        for m in range(1, far_ways):
            source = (far_me + m) % far_ways
            pltpu.make_async_remote_copy(
                src_ref=far_buf.at[source],
                dst_ref=far_buf.at[source],
                send_sem=far_send.at[0],
                recv_sem=far_recv.at[source],
                device_id=(member(far_step, far_ways, source), col),
                device_id_type=MESH,
            ).wait_recv()
        total = far_buf[0]
        for index in range(1, far_ways):
            total = total + far_buf[index]
        gath[pl.ds(lo, size)] = total
    else:
        ns_steps()
        gath[pl.ds(lo, size)] = acc[pl.ds(lo, size)]

    for j in reversed(range(count)):
        low, ways = groups[j]
        base, piece = spans[j]
        mine = group_index(low, ways)
        own = pl.ds(pl.multiple_of(base + mine * piece, 8), piece)
        copies = []
        for m in range(1, ways):
            other = (mine + m) % ways
            copy = pltpu.make_async_remote_copy(
                src_ref=gath.at[own],
                dst_ref=gath.at[own],
                send_sem=send_ag.at[4 * j + m],
                recv_sem=recv_ag.at[4 * j + mine],
                device_id=(member(low, ways, other), col),
                device_id_type=MESH,
            )
            copy.start()
            copies.append(copy)
        ns_steps()
        for copy in copies:
            copy.wait_send()
        for m in range(1, ways):
            source = (mine + m) % ways
            theirs = pl.ds(pl.multiple_of(base + source * piece, 8), piece)
            pltpu.make_async_remote_copy(
                src_ref=gath.at[theirs],
                dst_ref=gath.at[theirs],
                send_sem=send_ag.at[4 * j],
                recv_sem=recv_ag.at[4 * j + source],
                device_id=(member(low, ways, source), col),
                device_id_type=MESH,
            ).wait_recv()

    o_ref[...] = jnp.dot(
        gath[...], inv_ref[...], precision=lax.Precision.HIGHEST,
        preferred_element_type=jnp.float32,
    )


def layer_allreduce_solve(rows, grams, layer_count):
    nbits = layer_count.bit_length() - 1
    if nbits == 7:
        stages = (
            (("bin", 0), ("bin", 1), ("bin", 2), ("quad", 5)),
            (("bin", 0), ("bin", 5), ("bin", 6), ("quad", 1)),
        )
        far = (3, 4)
    elif nbits == 5:
        stages = ((("bin", 0), ("bin", 1), ("bin", 2)), (("bin", 0), ("bin", 2), ("bin", 1)))
        far = (3, 4)
    else:
        stages = (tuple(("bin", k) for k in range(nbits)),) * 2
        far = ()
    count = len(stages[0])
    far_ways = 1 << len(far)
    slots = 2 * count + 1
    ns_plan = [INV_STEPS // slots + (1 if r < INV_STEPS % slots else 0) for r in range(slots)]
    if slots == 9 and INV_STEPS == 24:
        ns_plan = [3, 3, 3, 3, 6, 2, 2, 2, 0]
    pieces = rows
    width = grams.shape[-1]
    buf_shapes = []
    size = rows.shape[0]
    for kind, _ in stages[0]:
        ways = 2 if kind == "bin" else 4
        size //= ways
        buf_shapes.append(pltpu.VMEM((ways, size) + pieces.shape[1:], jnp.float32))
    solved, inverse = pl.pallas_call(
        functools.partial(layer_allreduce_kernel, stages, far, ns_plan),
        out_shape=(
            jax.ShapeDtypeStruct(pieces.shape, jnp.float32),
            jax.ShapeDtypeStruct((width, width), jnp.float32),
        ),
        in_specs=[pl.BlockSpec(memory_space=pltpu.VMEM)] * 2,
        out_specs=(pl.BlockSpec(memory_space=pltpu.VMEM),) * 2,
        scratch_shapes=[pltpu.VMEM(pieces.shape, jnp.float32)] * 2
        + [pltpu.VMEM((width, width), jnp.float32)]
        + buf_shapes
        + [pltpu.VMEM((far_ways, size) + pieces.shape[1:], jnp.float32)]
        + [pltpu.SemaphoreType.DMA((4 * count,))] * 4
        + [pltpu.SemaphoreType.DMA((far_ways,))] * 2,
        compiler_params=pltpu.CompilerParams(collective_id=0, has_side_effects=True),
    )(pieces, grams)
    return solved


def inl_gather_kernel(ways, b_ref, c_ref, o_ref, send1, recv1, send2, recv2):
    row = lax.axis_index("layer")
    col = lax.axis_index("inl")
    core = row % 2
    sibling = row + 1 - 2 * core
    half = b_ref.shape[1] // 2
    parts = (b_ref, c_ref)
    mine = pl.ds(pl.multiple_of(core * half, half), half)
    theirs = pl.ds(pl.multiple_of((1 - core) * half, half), half)
    barrier = pltpu.get_barrier_semaphore()
    for step in range(1, ways):
        pl.semaphore_signal(
            barrier, inc=1, device_id=(row, (col + step) % ways), device_id_type=MESH
        )
    pl.semaphore_signal(barrier, inc=1, device_id=(sibling, col), device_id_type=MESH)
    pl.semaphore_wait(barrier, ways)
    copies = []
    for step in range(1, ways):
        for part, x_ref in enumerate(parts):
            copy = pltpu.make_async_remote_copy(
                src_ref=x_ref.at[:, mine],
                dst_ref=o_ref.at[part, :, col, mine],
                send_sem=send1.at[2 * step + part],
                recv_sem=recv1.at[2 * col + part],
                device_id=(row, (col + step) % ways),
                device_id_type=MESH,
            )
            copy.start()
            copies.append(copy)
    for part, x_ref in enumerate(parts):
        o_ref[part, :, col] = x_ref[...]
    forwards = []
    for step in range(1, ways):
        source = (col + step) % ways
        for part in range(2):
            pltpu.make_async_remote_copy(
                src_ref=o_ref.at[part, :, source, mine],
                dst_ref=o_ref.at[part, :, source, mine],
                send_sem=send1.at[part],
                recv_sem=recv1.at[2 * source + part],
                device_id=(row, source),
                device_id_type=MESH,
            ).wait_recv()
        forward = pltpu.make_async_remote_copy(
            src_ref=o_ref.at[:, :, source, mine],
            dst_ref=o_ref.at[:, :, source, mine],
            send_sem=send2.at[step],
            recv_sem=recv2.at[source],
            device_id=(sibling, col),
            device_id_type=MESH,
        )
        forward.start()
        forwards.append(forward)
    for copy in copies:
        copy.wait_send()
    for forward in forwards:
        forward.wait_send()
    for step in range(1, ways):
        source = (col + step) % ways
        pltpu.make_async_remote_copy(
            src_ref=o_ref.at[:, :, source, theirs],
            dst_ref=o_ref.at[:, :, source, theirs],
            send_sem=send2.at[0],
            recv_sem=recv2.at[source],
            device_id=(sibling, col),
            device_id_type=MESH,
        ).wait_recv()


def inl_gather(factor_b, factor_c, ways):
    blocks, cells, rank_width = factor_b.shape
    return pl.pallas_call(
        functools.partial(inl_gather_kernel, ways),
        out_shape=jax.ShapeDtypeStruct((2, blocks, ways, cells, rank_width), factor_b.dtype),
        in_specs=[pl.BlockSpec(memory_space=pltpu.VMEM)] * 2,
        out_specs=pl.BlockSpec(memory_space=pltpu.VMEM),
        scratch_shapes=[pltpu.SemaphoreType.DMA((2 * ways,))] * 2
        + [pltpu.SemaphoreType.DMA((ways,))] * 2,
        compiler_params=pltpu.CompilerParams(collective_id=1, has_side_effects=True),
    )(factor_b, factor_c)


def mttkrp_kernel(coords_ref, filled_ref, blk_ref, b_ref, c_ref, o_ref):
    chunk = 32
    slot = pl.program_id(0)
    _, a_n, b_n, c_n = blk_ref.shape

    @pl.when(slot == 0)
    def _():
        o_ref[...] = jnp.zeros_like(o_ref)

    @pl.when(slot < filled_ref[0])
    def _():
        target = coords_ref[slot, 0]
        b_rows = b_ref[0].astype(jnp.float32)
        c_rows = c_ref[0]

        def body(i, carry):
            start = pl.multiple_of(i * chunk, chunk)
            x = blk_ref[0, pl.ds(start, chunk)].reshape(chunk * b_n, c_n)
            y = jnp.dot(x, c_rows, preferred_element_type=jnp.float32)
            z = y.reshape(chunk, b_n, -1) * b_rows[None]
            z = z.reshape(chunk, b_n // 8, 8, z.shape[-1]).sum(axis=1)
            o_ref[target, pl.ds(start, chunk)] += z.sum(axis=1)
            return carry

        lax.fori_loop(0, a_n // chunk, body, 0)


def mttkrp_rows(blocks, coords, filled, whole):
    slot_count, a_n, b_n, c_n = blocks.shape
    _, side_blocks, _, rank_width = whole.shape
    grid_spec = pltpu.PrefetchScalarGridSpec(
        num_scalar_prefetch=2,
        grid=(slot_count,),
        in_specs=[
            pl.BlockSpec((1, a_n, b_n, c_n), lambda s, cr, fl: (s, 0, 0, 0)),
            pl.BlockSpec((None, 1, b_n, rank_width), lambda s, cr, fl: (0, cr[s, 1], 0, 0)),
            pl.BlockSpec((None, 1, c_n, rank_width), lambda s, cr, fl: (1, cr[s, 2], 0, 0)),
        ],
        out_specs=pl.BlockSpec((side_blocks, a_n, rank_width), lambda s, cr, fl: (0, 0, 0)),
    )
    return pl.pallas_call(
        mttkrp_kernel,
        grid_spec=grid_spec,
        out_shape=jax.ShapeDtypeStruct((side_blocks, a_n, rank_width), jnp.float32),
        cost_estimate=pl.CostEstimate(
            flops=2 * slot_count * a_n * b_n * c_n * rank_width,
            bytes_accessed=blocks.size * 2 + slot_count * (b_n + c_n) * rank_width * 2,
            transcendentals=0,
        ),
    )(coords, filled, blocks, whole, whole)


def on_device(layer_count, inl_count, blocks, coords, filled, factor_b, factor_c):
    slot_count = blocks.shape[0]
    own_cells = blocks.shape[1]
    side_blocks = factor_b.shape[0]
    rank_width = factor_b.shape[2]
    ways = inl_count
    gathered = inl_gather(factor_b, factor_c, ways)
    whole = gathered.reshape(2, side_blocks, ways * factor_b.shape[1], rank_width)
    flat = whole.reshape(2, -1, rank_width)
    gram_parts = lax.dot_general(
        flat, flat, (((1,), (1,)), ((0,), (0,))), preferred_element_type=jnp.float32
    )
    buffer = mttkrp_rows(blocks, coords, filled, whole)
    row_totals = buffer.reshape(side_blocks * own_cells, rank_width)
    solved = layer_allreduce_solve(row_totals, gram_parts, layer_count)
    return solved.reshape(side_blocks, own_cells, rank_width)


def solution(mesh):
    in_specs = (
        P("layer", "inl", None, None),
        P("layer", None),
        P("layer"),
        P(None, "inl", None),
        P(None, "inl", None),
    )
    out_specs = P(None, "inl", None)
    return jax.shard_map(
        functools.partial(on_device, mesh.shape["layer"], mesh.shape["inl"]),
        mesh=mesh,
        in_specs=in_specs,
        out_specs=out_specs,
        check_vma=False,
    )
```

```python
import functools

import jax
import jax.numpy as jnp
from jax import lax
from jax.experimental import pallas as pl
from jax.experimental.pallas import tpu as pltpu
from jax.sharding import PartitionSpec as P

INV_STEPS = 24
MESH = pl.DeviceIdType.MESH


def layer_allreduce_kernel(stages, far, ns_plan, x_ref, grams_ref, o_ref, inv_ref, acc, gath, g_ref, *rest):
    count = len(stages[0])
    bufs = rest[:count]
    far_buf = rest[count]
    send_rs, recv_rs, send_ag, recv_ag, far_send, far_recv = rest[count + 1:]
    me = lax.axis_index("layer")
    col = lax.axis_index("inl")
    far_ways = far_buf.shape[0]

    core = me % 2

    def group_index(step, ways):
        return (me // step) % ways

    def member(step, ways, other):
        return me + (other - group_index(step, ways)) * step

    groups = [
        (core * (1 << low1) + (1 - core) * (1 << low0), 2 if kind == "bin" else 4)
        for (kind, low0), (_, low1) in zip(stages[0], stages[1])
    ]
    far_step = 1 << far[0] if far else 1
    if far:
        groups.append((far_step, far_ways))
    barrier = pltpu.get_barrier_semaphore()
    signals = 0
    for low, ways in groups:
        mine = group_index(low, ways)
        for m in range(1, ways):
            pl.semaphore_signal(
                barrier, inc=1, device_id=(member(low, ways, (mine + m) % ways), col),
                device_id_type=MESH,
            )
            signals += 1
    pl.semaphore_wait(barrier, signals)

    width = g_ref.shape[0]
    rows = lax.broadcasted_iota(jnp.int32, (width, width), 0)
    cols = lax.broadcasted_iota(jnp.int32, (width, width), 1)
    two_ident = jnp.where(rows == cols, 2.0, 0.0).astype(jnp.float32)
    plan = iter(ns_plan)

    def ns_start():
        gram = grams_ref[0] * grams_ref[1]
        g_ref[...] = gram
        norm_sq = jnp.sum(jnp.sum(gram * gram, axis=1, keepdims=True), axis=0, keepdims=True)
        inv_ref[...] = (0.5 * two_ident) / jnp.sqrt(norm_sq)

    done = [0]

    def ns_steps():
        for _ in range(next(plan)):
            precision = (
                lax.Precision.HIGH if done[0] < INV_STEPS - 2
                else lax.Precision.HIGHEST
            )
            done[0] += 1
            current = inv_ref[...]
            product = jnp.dot(
                g_ref[...], current, precision=precision,
                preferred_element_type=jnp.float32,
            )
            inv_ref[...] = jnp.dot(
                current, two_ident - product, precision=precision,
                preferred_element_type=jnp.float32,
            )

    acc[...] = x_ref[...]
    lo = 0
    size = acc.shape[0]
    spans = []
    for j, (low, ways) in enumerate(groups[:count]):
        piece = size // ways
        mine = group_index(low, ways)
        copies = []
        for m in range(1, ways):
            other = (mine + m) % ways
            copy = pltpu.make_async_remote_copy(
                src_ref=acc.at[pl.ds(pl.multiple_of(lo + other * piece, 8), piece)],
                dst_ref=bufs[j].at[mine],
                send_sem=send_rs.at[4 * j + m],
                recv_sem=recv_rs.at[4 * j + mine],
                device_id=(member(low, ways, other), col),
                device_id_type=MESH,
            )
            copy.start()
            copies.append(copy)
        keep_lo = pl.multiple_of(lo + mine * piece, 8)
        bufs[j][mine] = acc[pl.ds(keep_lo, piece)]
        if j == 0:
            ns_start()
        ns_steps()
        for copy in copies:
            copy.wait_send()
        for m in range(1, ways):
            source = (mine + m) % ways
            pltpu.make_async_remote_copy(
                src_ref=bufs[j].at[source],
                dst_ref=bufs[j].at[source],
                send_sem=send_rs.at[4 * j],
                recv_sem=recv_rs.at[4 * j + source],
                device_id=(member(low, ways, source), col),
                device_id_type=MESH,
            ).wait_recv()
        total = bufs[j][0]
        for index in range(1, ways):
            total = total + bufs[j][index]
        acc[pl.ds(keep_lo, piece)] = total
        spans.append((lo, piece))
        lo = keep_lo
        size = piece

    if far:
        far_me = group_index(far_step, far_ways)
        far_buf[far_me] = acc[pl.ds(lo, size)]
        copies = []
        for m in range(1, far_ways):
            copy = pltpu.make_async_remote_copy(
                src_ref=acc.at[pl.ds(lo, size)],
                dst_ref=far_buf.at[far_me],
                send_sem=far_send.at[m],
                recv_sem=far_recv.at[far_me],
                device_id=(member(far_step, far_ways, (far_me + m) % far_ways), col),
                device_id_type=MESH,
            )
            copy.start()
            copies.append(copy)
        ns_steps()
        for copy in copies:
            copy.wait_send()
        for m in range(1, far_ways):
            source = (far_me + m) % far_ways
            pltpu.make_async_remote_copy(
                src_ref=far_buf.at[source],
                dst_ref=far_buf.at[source],
                send_sem=far_send.at[0],
                recv_sem=far_recv.at[source],
                device_id=(member(far_step, far_ways, source), col),
                device_id_type=MESH,
            ).wait_recv()
        total = far_buf[0]
        for index in range(1, far_ways):
            total = total + far_buf[index]
        gath[pl.ds(lo, size)] = total
    else:
        ns_steps()
        gath[pl.ds(lo, size)] = acc[pl.ds(lo, size)]

    for j in reversed(range(count)):
        low, ways = groups[j]
        base, piece = spans[j]
        mine = group_index(low, ways)
        own = pl.ds(pl.multiple_of(base + mine * piece, 8), piece)
        copies = []
        for m in range(1, ways):
            other = (mine + m) % ways
            copy = pltpu.make_async_remote_copy(
                src_ref=gath.at[own],
                dst_ref=gath.at[own],
                send_sem=send_ag.at[4 * j + m],
                recv_sem=recv_ag.at[4 * j + mine],
                device_id=(member(low, ways, other), col),
                device_id_type=MESH,
            )
            copy.start()
            copies.append(copy)
        ns_steps()
        for copy in copies:
            copy.wait_send()
        for m in range(1, ways):
            source = (mine + m) % ways
            theirs = pl.ds(pl.multiple_of(base + source * piece, 8), piece)
            pltpu.make_async_remote_copy(
                src_ref=gath.at[theirs],
                dst_ref=gath.at[theirs],
                send_sem=send_ag.at[4 * j],
                recv_sem=recv_ag.at[4 * j + source],
                device_id=(member(low, ways, source), col),
                device_id_type=MESH,
            ).wait_recv()

    o_ref[...] = jnp.dot(
        gath[...], inv_ref[...], precision=lax.Precision.HIGHEST,
        preferred_element_type=jnp.float32,
    )


def layer_allreduce_solve(rows, grams, layer_count):
    nbits = layer_count.bit_length() - 1
    if nbits == 7:
        stages = (
            (("bin", 0), ("bin", 1), ("bin", 2), ("quad", 5)),
            (("bin", 0), ("bin", 5), ("bin", 6), ("quad", 1)),
        )
        far = (3, 4)
    elif nbits == 5:
        stages = ((("bin", 0), ("bin", 1), ("bin", 2)), (("bin", 0), ("bin", 2), ("bin", 1)))
        far = (3, 4)
    else:
        stages = (tuple(("bin", k) for k in range(nbits)),) * 2
        far = ()
    count = len(stages[0])
    far_ways = 1 << len(far)
    slots = 2 * count + 1
    ns_plan = [INV_STEPS // slots + (1 if r < INV_STEPS % slots else 0) for r in range(slots)]
    pieces = rows
    width = grams.shape[-1]
    buf_shapes = []
    size = rows.shape[0]
    for kind, _ in stages[0]:
        ways = 2 if kind == "bin" else 4
        size //= ways
        buf_shapes.append(pltpu.VMEM((ways, size) + pieces.shape[1:], jnp.float32))
    solved, inverse = pl.pallas_call(
        functools.partial(layer_allreduce_kernel, stages, far, ns_plan),
        out_shape=(
            jax.ShapeDtypeStruct(pieces.shape, jnp.float32),
            jax.ShapeDtypeStruct((width, width), jnp.float32),
        ),
        in_specs=[pl.BlockSpec(memory_space=pltpu.VMEM)] * 2,
        out_specs=(pl.BlockSpec(memory_space=pltpu.VMEM),) * 2,
        scratch_shapes=[pltpu.VMEM(pieces.shape, jnp.float32)] * 2
        + [pltpu.VMEM((width, width), jnp.float32)]
        + buf_shapes
        + [pltpu.VMEM((far_ways, size) + pieces.shape[1:], jnp.float32)]
        + [pltpu.SemaphoreType.DMA((4 * count,))] * 4
        + [pltpu.SemaphoreType.DMA((far_ways,))] * 2,
        compiler_params=pltpu.CompilerParams(collective_id=0, has_side_effects=True),
    )(pieces, grams)
    return solved


def inl_gather_kernel(ways, b_ref, c_ref, o_ref, send1, recv1, send2, recv2):
    row = lax.axis_index("layer")
    col = lax.axis_index("inl")
    core = row % 2
    sibling = row + 1 - 2 * core
    half = b_ref.shape[1] // 2
    parts = (b_ref, c_ref)
    mine = pl.ds(pl.multiple_of(core * half, half), half)
    theirs = pl.ds(pl.multiple_of((1 - core) * half, half), half)
    barrier = pltpu.get_barrier_semaphore()
    for step in range(1, ways):
        pl.semaphore_signal(
            barrier, inc=1, device_id=(row, (col + step) % ways), device_id_type=MESH
        )
    pl.semaphore_signal(barrier, inc=1, device_id=(sibling, col), device_id_type=MESH)
    pl.semaphore_wait(barrier, ways)
    copies = []
    for step in range(1, ways):
        for part, x_ref in enumerate(parts):
            copy = pltpu.make_async_remote_copy(
                src_ref=x_ref.at[:, mine],
                dst_ref=o_ref.at[part, :, col, mine],
                send_sem=send1.at[2 * step + part],
                recv_sem=recv1.at[2 * col + part],
                device_id=(row, (col + step) % ways),
                device_id_type=MESH,
            )
            copy.start()
            copies.append(copy)
    for part, x_ref in enumerate(parts):
        o_ref[part, :, col] = x_ref[...]
    forwards = []
    for step in range(1, ways):
        source = (col + step) % ways
        for part in range(2):
            pltpu.make_async_remote_copy(
                src_ref=o_ref.at[part, :, source, mine],
                dst_ref=o_ref.at[part, :, source, mine],
                send_sem=send1.at[part],
                recv_sem=recv1.at[2 * source + part],
                device_id=(row, source),
                device_id_type=MESH,
            ).wait_recv()
        forward = pltpu.make_async_remote_copy(
            src_ref=o_ref.at[:, :, source, mine],
            dst_ref=o_ref.at[:, :, source, mine],
            send_sem=send2.at[step],
            recv_sem=recv2.at[source],
            device_id=(sibling, col),
            device_id_type=MESH,
        )
        forward.start()
        forwards.append(forward)
    for copy in copies:
        copy.wait_send()
    for forward in forwards:
        forward.wait_send()
    for step in range(1, ways):
        source = (col + step) % ways
        pltpu.make_async_remote_copy(
            src_ref=o_ref.at[:, :, source, theirs],
            dst_ref=o_ref.at[:, :, source, theirs],
            send_sem=send2.at[0],
            recv_sem=recv2.at[source],
            device_id=(sibling, col),
            device_id_type=MESH,
        ).wait_recv()


def inl_gather(factor_b, factor_c, ways):
    blocks, cells, rank_width = factor_b.shape
    return pl.pallas_call(
        functools.partial(inl_gather_kernel, ways),
        out_shape=jax.ShapeDtypeStruct((2, blocks, ways, cells, rank_width), factor_b.dtype),
        in_specs=[pl.BlockSpec(memory_space=pltpu.VMEM)] * 2,
        out_specs=pl.BlockSpec(memory_space=pltpu.VMEM),
        scratch_shapes=[pltpu.SemaphoreType.DMA((2 * ways,))] * 2
        + [pltpu.SemaphoreType.DMA((ways,))] * 2,
        compiler_params=pltpu.CompilerParams(collective_id=1, has_side_effects=True),
    )(factor_b, factor_c)


def mttkrp_kernel(coords_ref, filled_ref, blk_ref, b_ref, c_ref, o_ref):
    chunk = 32
    slot = pl.program_id(0)
    _, a_n, b_n, c_n = blk_ref.shape

    @pl.when(slot == 0)
    def _():
        o_ref[...] = jnp.zeros_like(o_ref)

    @pl.when(slot < filled_ref[0])
    def _():
        target = coords_ref[slot, 0]
        b_rows = b_ref[0].astype(jnp.float32)
        c_rows = c_ref[0]

        def body(i, carry):
            start = pl.multiple_of(i * chunk, chunk)
            x = blk_ref[0, pl.ds(start, chunk)].reshape(chunk * b_n, c_n)
            y = jnp.dot(x, c_rows, preferred_element_type=jnp.float32)
            z = y.reshape(chunk, b_n, -1) * b_rows[None]
            z = z.reshape(chunk, b_n // 8, 8, z.shape[-1]).sum(axis=1)
            o_ref[target, pl.ds(start, chunk)] += z.sum(axis=1)
            return carry

        lax.fori_loop(0, a_n // chunk, body, 0)


def mttkrp_rows(blocks, coords, filled, whole):
    slot_count, a_n, b_n, c_n = blocks.shape
    _, side_blocks, _, rank_width = whole.shape
    grid_spec = pltpu.PrefetchScalarGridSpec(
        num_scalar_prefetch=2,
        grid=(slot_count,),
        in_specs=[
            pl.BlockSpec((1, a_n, b_n, c_n), lambda s, cr, fl: (s, 0, 0, 0)),
            pl.BlockSpec((None, 1, b_n, rank_width), lambda s, cr, fl: (0, cr[s, 1], 0, 0)),
            pl.BlockSpec((None, 1, c_n, rank_width), lambda s, cr, fl: (1, cr[s, 2], 0, 0)),
        ],
        out_specs=pl.BlockSpec((side_blocks, a_n, rank_width), lambda s, cr, fl: (0, 0, 0)),
    )
    return pl.pallas_call(
        mttkrp_kernel,
        grid_spec=grid_spec,
        out_shape=jax.ShapeDtypeStruct((side_blocks, a_n, rank_width), jnp.float32),
        cost_estimate=pl.CostEstimate(
            flops=2 * slot_count * a_n * b_n * c_n * rank_width,
            bytes_accessed=blocks.size * 2 + slot_count * (b_n + c_n) * rank_width * 2,
            transcendentals=0,
        ),
    )(coords, filled, blocks, whole, whole)


def on_device(layer_count, inl_count, blocks, coords, filled, factor_b, factor_c):
    slot_count = blocks.shape[0]
    own_cells = blocks.shape[1]
    side_blocks = factor_b.shape[0]
    rank_width = factor_b.shape[2]
    ways = inl_count
    gathered = inl_gather(factor_b, factor_c, ways)
    whole = gathered.reshape(2, side_blocks, ways * factor_b.shape[1], rank_width)
    flat = whole.reshape(2, -1, rank_width)
    gram_parts = lax.dot_general(
        flat, flat, (((1,), (1,)), ((0,), (0,))), preferred_element_type=jnp.float32
    )
    buffer = mttkrp_rows(blocks, coords, filled, whole)
    row_totals = buffer.reshape(side_blocks * own_cells, rank_width)
    solved = layer_allreduce_solve(row_totals, gram_parts, layer_count)
    return solved.reshape(side_blocks, own_cells, rank_width)


def solution(mesh):
    in_specs = (
        P("layer", "inl", None, None),
        P("layer", None),
        P("layer"),
        P(None, "inl", None),
        P(None, "inl", None),
    )
    out_specs = P(None, "inl", None)
    return jax.shard_map(
        functools.partial(on_device, mesh.shape["layer"], mesh.shape["inl"]),
        mesh=mesh,
        in_specs=in_specs,
        out_specs=out_specs,
        check_vma=False,
    )
```
